32 devices in a mesh: batch: 4 (over y, core), seq: 8 (over z, x).
Axes of the slice: x: 2, y: 2, z: 4, core: 2. Of those that a mesh axis runs over, the one named last changes fastest.
Arguments:
- tokens: bfloat16 [8, 32, 64, 768], P('batch', 'seq'), may hold values from -6 to 6
- cotangent: bfloat16 [8, 32, 64, 768], P('batch', 'seq'), may hold values from -6 to 6
- timestep: int32 [8], P('batch'), may hold values from 0 to 999
- class_ids: int32 [8], P('batch'), may hold values from 0 to 999
- heights: int32 [8], P('batch'), may hold values from 8 to 32, as said below
- widths: int32 [8], P('batch'), may hold values from 16 to 64, as said below
- time_weight: bfloat16 [256, 768], replicated, may hold values from -0.375 to 0.375
- class_table: bfloat16 [1000, 768], replicated, may hold values from -6 to 6
- ada_weight: bfloat16 [768, 4608], replicated, may hold values from -0.21875 to 0.21875
- ada_bias: float32 [4608], replicated, may hold values from -4 to 4
- conv_attn: bfloat16 [9, 768], replicated, may hold values from -2 to 2
- qkv_weight: bfloat16 [768, 2304], replicated, may hold values from -0.09375 to 0.09375
- proj_weight: bfloat16 [768, 768], replicated, may hold values from -1.75 to 1.75
- up_weight: bfloat16 [768, 3072], replicated, may hold values from -0.21875 to 0.21875
- conv_ffn: bfloat16 [9, 3072], replicated, may hold values from -2 to 2
- down_weight: bfloat16 [3072, 768], replicated, may hold values from -0.109375 to 0.109375
Outputs:
- layer_out: bfloat16 [8, 32, 64, 768], P('batch', 'seq')
- token_grad: float32 [8, 32, 64, 768], P('batch', 'seq')
- cond_grad: float32 [8, 768], P('batch')
- time_weight_grad: float32 [256, 768], P(None, ('batch', 'seq'))
- class_table_grad: float32 [1000, 768], P(None, ('batch', 'seq'))
- ada_weight_grad: float32 [768, 4608], P(('batch', 'seq'))
- ada_bias_grad: float32 [4608], P(('batch', 'seq'))
- conv_attn_grad: float32 [9, 768], P(None, ('batch', 'seq'))
- qkv_weight_grad: float32 [768, 2304], P(('batch', 'seq'))
- proj_weight_grad: float32 [768, 768], P(('batch', 'seq'))
- up_weight_grad: float32 [768, 3072], P(('batch', 'seq'))
- conv_ffn_grad: float32 [9, 3072], P(None, ('batch', 'seq'))
- down_weight_grad: float32 [3072, 768], P(None, ('batch', 'seq'))
The draws below stay inside these ranges and needn't reach their ends.
Inputs may be any that keep to these rules, and one draw needn't show every extreme that they name: `heights`: some latent has all 32 rows valid. `widths`: some latent has all 64 columns valid.
All inputs are finite; a program needn't handle non-finite values.
Results may differ from the reference program's by a relative error of at most 0.025.
Values may be sent and summed in bfloat16 or wider, within the bound.
No kernel may reach another device: no remote copies, remote signals or barrier semaphores. Data moves between devices by JAX's collectives and lax.ppermute only.
A program may use at most 448 MiB of HBM per device.

```python
import math
import jax
import jax.numpy as jnp
from jax import lax

D = 768
HEADS = 12
HEAD_DIM = 64
FF = 3072
CLASSES = 1000
FREQ = 256
GRID_W = 64
HEIGHT = 32
LATENTS = 8


def draw_heights(key, part):
    draw_key, pick_key = jax.random.split(jax.random.fold_in(key, 11))
    drawn = jax.random.randint(draw_key, (LATENTS,), HEIGHT // 4, HEIGHT + 1)
    chosen = jax.random.randint(pick_key, (), 0, LATENTS)
    return jnp.where(jnp.arange(LATENTS) == chosen, HEIGHT, drawn).astype(jnp.int32)


def draw_widths(key, part):
    draw_key, pick_key = jax.random.split(jax.random.fold_in(key, 23))
    drawn = jax.random.randint(draw_key, (LATENTS,), GRID_W // 4, GRID_W + 1)
    chosen = jax.random.randint(pick_key, (), 0, LATENTS)
    return jnp.where(jnp.arange(LATENTS) == chosen, GRID_W, drawn).astype(jnp.int32)


def plant(values, own_key, low, high):
    extent = values.shape
    spot = [jax.random.randint(jax.random.fold_in(own_key, axis), (), 0, extent[axis]) for axis in range(len(extent))]
    values = values.at[tuple(spot)].set(low)
    longest = extent.index(max(extent))
    spot[longest] = (spot[longest] + 1) % extent[longest]
    return values.at[tuple(spot)].set(high)


def block_levels(own_key, extent, cuts, smallest, high):
    loudness, own = 1.0, jax.random.fold_in(own_key, 6)
    for dim, shards_of in cuts:
        draws = jnp.exp(jax.random.uniform(jax.random.fold_in(own, dim), (shards_of,), jnp.float32, smallest / len(cuts), high / len(cuts)))
        loudness = loudness * jnp.repeat(draws, extent[dim] // shards_of).reshape([-1 if axis == dim else 1 for axis in range(len(extent))])
    return loudness


def scatter_about(stream_key, extent, deviation, bound, cuts=(), kind=jnp.bfloat16):
    array = jax.random.normal(stream_key, extent, jnp.float32) * deviation
    if len(cuts) > 0:
        array = block_levels(stream_key, extent, cuts, -0.22, 0.18) * array
    return jnp.clip(array, min=-bound, max=bound).astype(kind)


def setup_inputs(seed: int = 0) -> dict:
    splits = jax.random.split(jax.random.key(seed), 17)
    return {
        "tokens": scatter_about(splits[0], (LATENTS, HEIGHT, GRID_W, D), 1.0, 6.0, ((0, 4), (1, 8))),
        "cotangent": scatter_about(splits[1], (LATENTS, HEIGHT, GRID_W, D), 1.0, 6.0, ((0, 4), (1, 8))),
        "timestep": plant(jax.random.randint(splits[2], (LATENTS,), 0, 1000), jax.random.fold_in(splits[2], 1), 0, 999).astype(jnp.int32),
        "class_ids": plant(jax.random.randint(splits[3], (LATENTS,), 0, CLASSES), jax.random.fold_in(splits[3], 1), 0, CLASSES - 1).astype(jnp.int32),
        "heights": draw_heights(jax.random.fold_in(splits[16], 71), 0),
        "widths": draw_widths(jax.random.fold_in(splits[16], 71), 0),
        "time_weight": scatter_about(splits[6], (FREQ, D), FREQ ** -0.5, 0.375),
        "class_table": scatter_about(splits[7], (CLASSES, D), 1.0, 6.0),
        "ada_weight": scatter_about(splits[8], (D, 6 * D), D ** -0.5, 0.21875),
        "ada_bias": scatter_about(splits[9], (6 * D,), 1.0, 4.0, (), jnp.float32),
        "conv_attn": scatter_about(splits[10], (9, D), 9 ** -0.5, 2.0),
        "qkv_weight": scatter_about(splits[11], (D, 3 * D), (6 * D) ** -0.5, 0.09375),
        "proj_weight": scatter_about(splits[12], (D, D), (D // 64) ** -0.5, 1.75),
        "up_weight": scatter_about(splits[13], (D, FF), D ** -0.5, 0.21875),
        "conv_ffn": scatter_about(splits[14], (9, FF), 9 ** -0.5, 2.0),
        "down_weight": scatter_about(splits[15], (FF, D), FF ** -0.5, 0.109375),
    }


@jax.custom_vjp
def low(v):
    return lax.optimization_barrier(v.astype(jnp.bfloat16)).astype(jnp.float32)

@jax.custom_vjp
def low_back(v):
    return v

def low_keep(v):
    return (low(v), None)

def low_pass(kept, grad):
    return (grad,)

def back_keep(v):
    return (v, None)

def back_low(kept, grad):
    return (low(grad),)
low.defvjp(low_keep, low_pass)
low_back.defvjp(back_keep, back_low)
HIGHEST = lax.Precision.HIGHEST

def matmul(left, right):
    return jnp.dot(left, right, precision=HIGHEST, preferred_element_type=jnp.float32)

def normalize(values):
    centre = values - lax.optimization_barrier(jnp.mean(values, axis=-1, keepdims=True))
    spread = lax.optimization_barrier(jnp.mean(centre * centre, axis=-1, keepdims=True))
    return centre * lax.rsqrt(spread + 1e-06)

def gelu_exact(values):
    return 0.5 * values * (1.0 + lax.erf(values * 0.7071067811865476))

def depthwise(values, kernel):
    extent_rows = values.shape[0]
    extent_cols = values.shape[1]
    padded = jnp.pad(values, ((1, 1), (1, 1), (0, 0)))
    summed = jnp.zeros(values.shape, values.dtype)
    for offset in range(9):
        down_by = offset // 3
        right_by = offset % 3
        summed = summed + padded[down_by:down_by + extent_rows, right_by:right_by + extent_cols] * kernel[offset]
    return summed

def regroup(values):
    channels = values.shape[-1]
    parted = values.reshape(HEIGHT // 2, 2, GRID_W // 2, 2, channels)
    return parted.transpose(1, 3, 0, 2, 4).reshape(4, HEIGHT // 2 * (GRID_W // 2), channels)

def ungroup(values):
    channels = values.shape[-1]
    parted = values.reshape(2, 2, HEIGHT // 2, GRID_W // 2, channels)
    return parted.transpose(2, 0, 3, 1, 4).reshape(HEIGHT, GRID_W, channels)

def attend_group(operands):
    queries, keys_in, values_in, flags = operands
    head_q = queries.reshape(-1, HEADS, HEAD_DIM)
    head_k = keys_in.reshape(-1, HEADS, HEAD_DIM)
    head_v = values_in.reshape(-1, HEADS, HEAD_DIM)
    scores = jnp.einsum('qhe,khe->hqk', head_q, head_k, precision=HIGHEST) * HEAD_DIM ** (-0.5)
    scores = low_back(scores)
    scores = jnp.where(flags[None, None, :], scores, -1e+30)
    row_peak = lax.optimization_barrier(jnp.max(scores, axis=-1, keepdims=True))
    numerator = jnp.exp(scores - row_peak)
    probability = numerator / lax.optimization_barrier(jnp.sum(numerator, axis=-1, keepdims=True))
    mixed_out = jnp.einsum('hqk,khe->qhe', low(probability), head_v, precision=HIGHEST)
    return mixed_out.reshape(-1, D)

def forward_one(source, shift_cond, time_weight, class_table, ada_weight, ada_bias, conv_attn, qkv_weight, proj_weight, up_weight, conv_ffn, down_weight, embedding, class_index, usable):
    condition = matmul(low(embedding), time_weight) + class_table[class_index] + shift_cond
    pieces = (matmul(low(jax.nn.silu(condition)), ada_weight) + ada_bias).reshape(6, D)
    hidden = normalize(source) * (1.0 + pieces[1]) + pieces[0]
    entered = low(hidden * usable[..., None])
    mixed_in = low(low_back(entered + depthwise(entered, conv_attn)))
    triple = low(low_back(matmul(mixed_in.reshape(-1, D), qkv_weight))).reshape(HEIGHT, GRID_W, 3 * D)
    grouped = regroup(triple)
    flags = regroup(usable[..., None])[..., 0] > 0.5
    attended = lax.map(jax.checkpoint(attend_group), (grouped[..., :D], grouped[..., D:2 * D], grouped[..., 2 * D:], flags))
    attended = ungroup(attended)
    branch = low_back(matmul(low(low_back(attended)).reshape(-1, D), proj_weight)).reshape(HEIGHT, GRID_W, D)
    after_attn = source + pieces[2] * branch
    hidden_two = normalize(after_attn) * (1.0 + pieces[4]) + pieces[3]
    raised = low(low_back(matmul(low(hidden_two * usable[..., None]).reshape(-1, D), up_weight))).reshape(HEIGHT, GRID_W, FF)
    convolved = low_back(depthwise(raised, conv_ffn))
    activated = low(gelu_exact(convolved))
    expanded = low_back(matmul(activated.reshape(-1, FF), down_weight)).reshape(HEIGHT, GRID_W, D)
    return after_attn + pieces[5] * expanded

def reference(tokens, cotangent, timestep, class_ids, heights, widths, time_weight, class_table, ada_weight, ada_bias, conv_attn, qkv_weight, proj_weight, up_weight, conv_ffn, down_weight):
    weights = tuple((entry.astype(jnp.float32) for entry in (time_weight, class_table, ada_weight, ada_bias, conv_attn, qkv_weight, proj_weight, up_weight, conv_ffn, down_weight)))
    half_freq = FREQ // 2
    frequency = jnp.exp(-math.log(10000.0) * jnp.arange(half_freq, dtype=jnp.float32) / half_freq)
    row_ids = jnp.arange(HEIGHT, dtype=jnp.int32)
    col_ids = jnp.arange(GRID_W, dtype=jnp.int32)

    def per_latent(running, inputs):
        latent_tokens, latent_cot, time_step, class_index, height_limit, width_limit = inputs
        angles = time_step.astype(jnp.float32) * frequency
        embedding = jnp.concatenate([jnp.cos(angles), jnp.sin(angles)])
        usable = ((row_ids[:, None] < height_limit) & (col_ids[None, :] < width_limit)).astype(jnp.float32)

        def closed(source, shift_cond, *params):
            return forward_one(source, shift_cond, *params, embedding, class_index, usable)
        result, pullback = jax.vjp(closed, latent_tokens.astype(jnp.float32), jnp.zeros((D,), jnp.float32), *weights)
        gradients = pullback(latent_cot.astype(jnp.float32))
        running = tuple((old + new for old, new in zip(running, gradients[2:])))
        return (running, (result.astype(jnp.bfloat16), gradients[0], gradients[1]))
    zero_sums = tuple((jnp.zeros_like(entry) for entry in weights))
    weight_sums, (outputs, token_grads, cond_grads) = lax.scan(per_latent, zero_sums, (tokens, cotangent, timestep, class_ids, heights, widths))
    return (outputs, token_grads, cond_grads, weight_sums[0], weight_sums[1], weight_sums[2], weight_sums[3], weight_sums[4], weight_sums[5], weight_sums[6], weight_sums[7], weight_sums[8], weight_sums[9])
```

```python
import functools
import math

import jax
import jax.numpy as jnp
from jax import lax
from jax.experimental import pallas as pl
from jax.experimental.pallas import tpu as pltpu
from jax.sharding import PartitionSpec as P

D = 768
HEADS = 12
HEAD_DIM = 64
PAIR = 2 * HEAD_DIM
PAIRS = HEADS // 2
FF_BLOCK = 256
LANE_PARTS = D // 128
FACTOR = HEAD_DIM ** (-0.5)

F32 = jnp.float32
BF16 = jnp.bfloat16
HIGHEST = lax.Precision.HIGHEST
NN = (((1,), (0,)), ((), ()))
NT = (((1,), (1,)), ((), ()))
VMEM_LIMIT = 60 * 1024 * 1024


def mm(left, right, dims=NN):
    return lax.dot_general(left, right, dims, preferred_element_type=F32)


def shift_down(values):
    rows = lax.broadcasted_iota(jnp.int32, values.shape, 0)
    return jnp.where(rows == 0, 0.0, pltpu.roll(values, 1, 0))


def shift_up(values):
    count = values.shape[0]
    rows = lax.broadcasted_iota(jnp.int32, values.shape, 0)
    return jnp.where(rows == count - 1, 0.0, pltpu.roll(values, count - 1, 0))


def put_shifts(ref, row, parity, values):
    ref[row, 1 + parity] = values
    if parity == 0:
        ref[row, 3] = shift_up(values)
    else:
        ref[row, 0] = shift_down(values)


def normalize(values):
    centre = values - jnp.mean(values, axis=-1, keepdims=True)
    spread = jnp.mean(centre * centre, axis=-1, keepdims=True)
    scaled = lax.rsqrt(spread + 1e-06)
    return centre * scaled, scaled


def norm_back(grad_norm, normed, scaled):
    return scaled * (
        grad_norm
        - jnp.mean(grad_norm, axis=-1, keepdims=True)
        - normed * jnp.mean(grad_norm * normed, axis=-1, keepdims=True)
    )


def put_row(buf, row, values):
    for k in range(LANE_PARTS):
        buf[row, k] = values[:, 128 * k : 128 * (k + 1)]


def get_row(buf, row):
    return jnp.concatenate([buf[row, k] for k in range(LANE_PARTS)], axis=1)


def put_columns(buf, row, parity, values):
    for k in range(LANE_PARTS):
        buf[row, k, pl.ds(parity, values.shape[0], stride=2), :] = values[:, 128 * k : 128 * (k + 1)]


def get_columns(buf, row, parity):
    half = buf.shape[2] // 2
    return jnp.concatenate(
        [buf[row, k, pl.ds(parity, half, stride=2), :] for k in range(LANE_PARTS)], axis=1
    )


def usable_of(meta, latents, latent, row, parity, half):
    cols = 2 * lax.broadcasted_iota(jnp.int32, (half, 1), 0) + parity
    row_ok = jnp.logical_and(row >= 0, row < meta[latent])
    limit = jnp.where(row_ok, meta[latents + latent], 0)
    return (cols < limit).astype(F32)


def sum8(values):
    total = values[0:8]
    for start in range(8, values.shape[0], 8):
        total = total + values[start : start + 8]
    return total


def enter_kernel(meta, tok, top, bot, pieces, kern, out, buf, ent):
    latents = pl.num_programs(0)
    latent = pl.program_id(0)
    rows_here, cols = tok.shape[1], tok.shape[2]
    half = cols // 2
    row0 = meta[2 * latents]
    shift = pieces[0, 0:1, :]
    scale = 1.0 + pieces[0, 1:2, :]
    for rr in range(rows_here + 2):
        source = top[0, 0] if rr == 0 else bot[0, 0] if rr == rows_here + 1 else tok[0, rr - 1]
        put_row(buf, rr, source.astype(F32))
        for parity in range(2):
            normed, _ = normalize(get_columns(buf, rr, parity))
            ok = usable_of(meta, latents, latent, row0 + rr - 1, parity, half)
            put_shifts(ent, rr, parity, ((normed * scale + shift) * ok).astype(BF16).astype(F32))
    for row in range(rows_here):
        for parity in range(2):
            total = jnp.zeros((half, D), F32)
            for i in range(3):
                for j in range(3):
                    tap = 3 * i + j
                    total = total + ent[row + i, parity + j] * kern[tap : tap + 1, :]
            mixed = (ent[row + 1, 1 + parity] + total).astype(BF16)
            group = 2 * (row % 2) + parity
            out[0, group, (row // 2) * half : (row // 2 + 1) * half, :] = mixed


def enter(meta, tokens, top, bot, pieces, kern):
    latents, rows_here, cols, _ = tokens.shape
    half = cols // 2
    per_group = rows_here // 2 * half
    whole = lambda *shape: pl.BlockSpec(shape, lambda l, m: (l,) + (0,) * (len(shape) - 1))
    return pl.pallas_call(
        enter_kernel,
        out_shape=jax.ShapeDtypeStruct((latents, 4, per_group, D), BF16),
        grid_spec=pltpu.PrefetchScalarGridSpec(
            num_scalar_prefetch=1,
            grid=(latents,),
            in_specs=[
                whole(1, rows_here, cols, D),
                whole(1, 1, cols, D),
                whole(1, 1, cols, D),
                whole(1, 6, D),
                pl.BlockSpec((9, D), lambda l, m: (0, 0)),
            ],
            out_specs=whole(1, 4, per_group, D),
            scratch_shapes=[
                pltpu.VMEM((rows_here + 2, LANE_PARTS, cols, 128), F32),
                pltpu.VMEM((rows_here + 2, 4, half, D), F32),
            ],
        ),
        compiler_params=pltpu.CompilerParams(vmem_limit_bytes=VMEM_LIMIT),
        name="enter",
    )(meta, tokens, top, bot, pieces, kern)


def cot_kernel(meta, cot, top, bot, pieces, ge_out, get_out, cot_out, buf):
    rows_here, cols = cot.shape[1], cot.shape[2]
    half = cols // 2
    gate = pieces[0, 5:6, :]
    for rr in range(rows_here + 2):
        source = top[0, 0] if rr == 0 else bot[0, 0] if rr == rows_here + 1 else cot[0, rr - 1]
        put_row(buf, rr, source.astype(F32))
        for parity in range(2):
            values = get_columns(buf, rr, parity)
            scaled = (gate * values).astype(BF16)
            at = (2 * rr + parity) * half
            ge_out[0, at : at + half, :] = scaled
            if 1 <= rr <= rows_here:
                cot_out[0, at - cols : at - cols + half, :] = values.astype(BF16)
    inner = ge_out[0, cols : cols + rows_here * cols, :].astype(F32)
    get_out[0] = inner.T.astype(BF16)


def prepare_cot(meta, cotangent, top, bot, pieces):
    latents, rows_here, cols, _ = cotangent.shape
    whole = lambda *shape: pl.BlockSpec(shape, lambda l, m: (l,) + (0,) * (len(shape) - 1))
    own = rows_here * cols
    return pl.pallas_call(
        cot_kernel,
        out_shape=(
            jax.ShapeDtypeStruct((latents, own + 2 * cols, D), BF16),
            jax.ShapeDtypeStruct((latents, D, own), BF16),
            jax.ShapeDtypeStruct((latents, own, D), BF16),
        ),
        grid_spec=pltpu.PrefetchScalarGridSpec(
            num_scalar_prefetch=1,
            grid=(latents,),
            in_specs=[
                whole(1, rows_here, cols, D),
                whole(1, 1, cols, D),
                whole(1, 1, cols, D),
                whole(1, 6, D),
            ],
            out_specs=(whole(1, own + 2 * cols, D), whole(1, D, own), whole(1, own, D)),
            scratch_shapes=[pltpu.VMEM((rows_here + 2, LANE_PARTS, cols, 128), F32)],
        ),
        compiler_params=pltpu.CompilerParams(vmem_limit_bytes=VMEM_LIMIT),
        name="prepare_cot",
    )(meta, cotangent, top, bot, pieces)


def second_kernel(meta, att, tok, top2, top1, bot1, bot2, pieces, proj, e2_out, e2t_out, after_out, branch_out, buf, bran):
    latents = pl.num_programs(0)
    latent = pl.program_id(0)
    rows_here, cols = tok.shape[1], tok.shape[2]
    half = cols // 2
    row0 = meta[2 * latents]
    gate = pieces[0, 2:3, :]
    shift = pieces[0, 3:4, :]
    scale = 1.0 + pieces[0, 4:5, :]
    for group in range(4):
        bran[group] = mm(att[group], proj[...])
    for rr in range(rows_here + 4):
        at_row = rr - 2
        source = (
            top2[0, 0]
            if at_row == -2
            else top1[0, 0]
            if at_row == -1
            else bot1[0, 0]
            if at_row == rows_here
            else bot2[0, 0]
            if at_row == rows_here + 1
            else tok[0, at_row]
        )
        put_row(buf, rr, source.astype(F32))
        for parity in range(2):
            group = 2 * (rr % 2) + parity
            branch = bran[group, (rr // 2) * half : (rr // 2 + 1) * half, :]
            after = get_columns(buf, rr, parity) + gate * branch
            normed, _ = normalize(after)
            ok = usable_of(meta, latents, latent, row0 + at_row, parity, half)
            at = (2 * rr + parity) * half
            e2_out[0, at : at + half, :] = ((normed * scale + shift) * ok).astype(BF16)
            if 0 <= at_row < rows_here:
                own = at - 2 * cols
                after_out[0, own : own + half, :] = after
                branch_out[0, own : own + half, :] = branch
    inner = e2_out[0, 2 * cols : 2 * cols + rows_here * cols, :].astype(F32)
    e2t_out[0] = inner.T.astype(BF16)


def second(meta, attended, tokens, tops, bots, pieces, proj):
    latents, rows_here, cols, _ = tokens.shape
    half = cols // 2
    own = rows_here * cols
    wide = attended.shape[1]
    whole = lambda *shape: pl.BlockSpec(shape, lambda l, m: (l,) + (0,) * (len(shape) - 1))
    return pl.pallas_call(
        second_kernel,
        out_shape=(
            jax.ShapeDtypeStruct((latents, own + 4 * cols, D), BF16),
            jax.ShapeDtypeStruct((latents, D, own), BF16),
            jax.ShapeDtypeStruct((latents, own, D), F32),
            jax.ShapeDtypeStruct((latents, own, D), F32),
        ),
        grid_spec=pltpu.PrefetchScalarGridSpec(
            num_scalar_prefetch=1,
            grid=(latents,),
            in_specs=[
                whole(4, wide, D),
                whole(1, rows_here, cols, D),
                whole(1, 1, cols, D),
                whole(1, 1, cols, D),
                whole(1, 1, cols, D),
                whole(1, 1, cols, D),
                whole(1, 6, D),
                pl.BlockSpec((D, D), lambda l, m: (0, 0)),
            ],
            out_specs=(
                whole(1, own + 4 * cols, D),
                whole(1, D, own),
                whole(1, own, D),
                whole(1, own, D),
            ),
            scratch_shapes=[
                pltpu.VMEM((rows_here + 4, LANE_PARTS, cols, 128), F32),
                pltpu.VMEM((4, wide, D), F32),
            ],
        ),
        compiler_params=pltpu.CompilerParams(vmem_limit_bytes=VMEM_LIMIT),
        name="second",
    )(meta, attended, tokens, tops[1], tops[0], bots[0], bots[1], pieces, proj)


def ffn_kernel(e2, e2t, ge, get, up, down, kern, exp_out, ge2_out, down_out, up_out, kern_out, lifted, gact, gconv, act, graised, exp_acc, ge2_acc, down_acc, up_acc, kern_acc):
    step, latent = pl.program_id(0), pl.program_id(1)
    steps, latents = pl.num_programs(0), pl.num_programs(1)
    half = lifted.shape[2]
    rows_here = lifted.shape[0] - 4
    block = lifted.shape[3]

    raised = mm(e2[0], up[...]).astype(BF16).astype(F32)
    for rr in range(rows_here + 4):
        for parity in range(2):
            at = (2 * rr + parity) * half
            put_shifts(lifted, rr, parity, raised[at : at + half])
    gact[...] = mm(ge[0], down[...], NT)

    taps = [kern[t : t + 1, :] for t in range(9)]

    for rr in range(rows_here + 2):
        for parity in range(2):
            total = jnp.zeros((half, block), F32)
            for i in range(3):
                for j in range(3):
                    total = total + lifted[rr + i, parity + j] * taps[3 * i + j]
            cdf = 0.5 * (1.0 + lax.erf(total * 0.7071067811865476))
            bell = jnp.exp(-0.5 * total * total) * 0.3989422804014327
            at = (2 * rr + parity) * half
            if 1 <= rr <= rows_here:
                own = at - 2 * half
                act[own : own + half, :] = (total * cdf).astype(BF16)
            grad = gact[at : at + half, :] * (cdf + total * bell)
            put_shifts(gconv, rr, parity, grad.astype(BF16).astype(F32))

    sums = [jnp.zeros((8, block), F32) for _ in range(9)]
    for row in range(rows_here):
        for parity in range(2):
            total = jnp.zeros((half, block), F32)
            here = gconv[row + 1, 1 + parity]
            for i in range(3):
                for j in range(3):
                    total = total + gconv[row + 2 - i, parity + 2 - j] * taps[3 * i + j]
                    sums[3 * i + j] = sums[3 * i + j] + sum8(lifted[row + 1 + i, parity + j] * here)
            at = (2 * row + parity) * half
            graised[at : at + half, :] = total.astype(BF16)

    expanded = mm(act[...], down[...])
    grad_e2 = mm(graised[...], up[...], NT)
    down_part = mm(get[0], act[...])
    up_part = mm(e2t[0], graised[...])

    @pl.when(step == 0)
    def _():
        exp_acc[latent] = expanded
        ge2_acc[latent] = grad_e2

    @pl.when(step > 0)
    def _():
        exp_acc[latent] += expanded
        ge2_acc[latent] += grad_e2

    @pl.when(latent == 0)
    def _():
        down_acc[...] = down_part
        up_acc[...] = up_part
        for t in range(9):
            kern_acc[t] = sums[t]

    @pl.when(latent > 0)
    def _():
        down_acc[...] += down_part
        up_acc[...] += up_part
        for t in range(9):
            kern_acc[t] += sums[t]

    @pl.when(latent == latents - 1)
    def _():
        down_out[...] = down_acc[...].astype(BF16)
        up_out[...] = up_acc[...].astype(BF16)
        for t in range(9):
            kern_out[t : t + 1, :] = jnp.sum(kern_acc[t], axis=0, keepdims=True)

    @pl.when(step == steps - 1)
    def _():
        exp_out[latent] = exp_acc[latent]
        ge2_out[latent] = ge2_acc[latent]


def ffn(e2, e2t, ge, get, up, down, kern, cols):
    latents = e2.shape[0]
    half = cols // 2
    own = e2t.shape[2]
    rows_here = own // cols
    hidden = up.shape[1]
    steps = hidden // FF_BLOCK
    per_latent = lambda *shape: pl.BlockSpec((1,) + shape, lambda f, l: (l, 0, 0))
    return pl.pallas_call(
        ffn_kernel,
        out_shape=(
            jax.ShapeDtypeStruct((latents, own, D), F32),
            jax.ShapeDtypeStruct((latents, own, D), F32),
            jax.ShapeDtypeStruct((D, hidden), BF16),
            jax.ShapeDtypeStruct((D, hidden), BF16),
            jax.ShapeDtypeStruct((9, hidden), F32),
        ),
        grid=(steps, latents),
        in_specs=[
            per_latent(own + 4 * cols, D),
            per_latent(D, own),
            per_latent(own + 2 * cols, D),
            per_latent(D, own),
            pl.BlockSpec((D, FF_BLOCK), lambda f, l: (0, f)),
            pl.BlockSpec((FF_BLOCK, D), lambda f, l: (f, 0)),
            pl.BlockSpec((9, FF_BLOCK), lambda f, l: (0, f)),
        ],
        out_specs=(
            pl.BlockSpec((latents, own, D), lambda f, l: (0, 0, 0)),
            pl.BlockSpec((latents, own, D), lambda f, l: (0, 0, 0)),
            pl.BlockSpec((D, FF_BLOCK), lambda f, l: (0, f)),
            pl.BlockSpec((D, FF_BLOCK), lambda f, l: (0, f)),
            pl.BlockSpec((9, FF_BLOCK), lambda f, l: (0, f)),
        ),
        scratch_shapes=[
            pltpu.VMEM((rows_here + 4, 4, half, FF_BLOCK), F32),
            pltpu.VMEM((own + 2 * cols, FF_BLOCK), F32),
            pltpu.VMEM((rows_here + 2, 4, half, FF_BLOCK), F32),
            pltpu.VMEM((own, FF_BLOCK), BF16),
            pltpu.VMEM((own, FF_BLOCK), BF16),
            pltpu.VMEM((latents, own, D), F32),
            pltpu.VMEM((latents, own, D), F32),
            pltpu.VMEM((D, FF_BLOCK), F32),
            pltpu.VMEM((D, FF_BLOCK), F32),
            pltpu.VMEM((9, 8, FF_BLOCK), F32),
        ],
        compiler_params=pltpu.CompilerParams(vmem_limit_bytes=VMEM_LIMIT),
        name="ffn",
    )(e2, e2t, ge, get, up, down, kern)


def middle_kernel(meta, exp, ge2, after_in, branch_in, cot_in, pieces, proj, out, after_grad, gb_out, gatt_out, sums_out, buf):
    latents = pl.num_programs(0)
    latent = pl.program_id(0)
    rows_here, cols = out.shape[1], out.shape[2]
    half = cols // 2
    row0 = meta[2 * latents]
    gate_one = pieces[0, 2:3, :]
    scale = 1.0 + pieces[0, 4:5, :]
    gate_two = pieces[0, 5:6, :]
    sums = [jnp.zeros((8, D), F32) for _ in range(4)]
    for row in range(rows_here):
        for parity in range(2):
            at = (2 * row + parity) * half
            part = pl.ds(at, half)
            after = after_in[0, part, :]
            cot = cot_in[0, part, :].astype(F32)
            expanded = exp[0, part, :]
            put_columns(buf, row, parity, after + gate_two * expanded)
            normed, scaled = normalize(after)
            ok = usable_of(meta, latents, latent, row0 + row, parity, half)
            grad = ge2[0, part, :] * ok
            grad_after = cot + norm_back(grad * scale, normed, scaled)
            after_grad[0, part, :] = grad_after
            sums[0] = sums[0] + sum8(grad_after * branch_in[0, part, :])
            sums[1] = sums[1] + sum8(grad)
            sums[2] = sums[2] + sum8(grad * normed)
            sums[3] = sums[3] + sum8(cot * expanded)
            group = 2 * (row % 2) + parity
            to = pl.ds((row // 2) * half, half)
            gb_out[0, group, to, :] = (gate_one * grad_after).astype(BF16)
        out[0, row] = get_row(buf, row).astype(BF16)
    for k in range(4):
        sums_out[0, k : k + 1, :] = jnp.sum(sums[k], axis=0, keepdims=True)
    for group in range(4):
        gatt_out[0, group] = mm(gb_out[0, group], proj[...], NT).astype(BF16)


def middle(meta, exp, ge2, after, branch, cot, pieces, proj, rows_here, cols):
    latents, own, _ = exp.shape
    per_group = own // 4
    whole = lambda *shape: pl.BlockSpec(shape, lambda l, m: (l,) + (0,) * (len(shape) - 1))
    return pl.pallas_call(
        middle_kernel,
        out_shape=(
            jax.ShapeDtypeStruct((latents, rows_here, cols, D), BF16),
            jax.ShapeDtypeStruct((latents, own, D), F32),
            jax.ShapeDtypeStruct((latents, 4, per_group, D), BF16),
            jax.ShapeDtypeStruct((latents, 4, per_group, D), BF16),
            jax.ShapeDtypeStruct((latents, 4, D), F32),
        ),
        grid_spec=pltpu.PrefetchScalarGridSpec(
            num_scalar_prefetch=1,
            grid=(latents,),
            in_specs=[
                whole(1, own, D),
                whole(1, own, D),
                whole(1, own, D),
                whole(1, own, D),
                whole(1, own, D),
                whole(1, 6, D),
                pl.BlockSpec((D, D), lambda l, m: (0, 0)),
            ],
            out_specs=(
                whole(1, rows_here, cols, D),
                whole(1, own, D),
                whole(1, 4, per_group, D),
                whole(1, 4, per_group, D),
                whole(1, 4, D),
            ),
            scratch_shapes=[
                pltpu.VMEM((rows_here, LANE_PARTS, cols, 128), F32),
            ],
        ),
        compiler_params=pltpu.CompilerParams(vmem_limit_bytes=VMEM_LIMIT),
        name="middle",
    )(meta, exp, ge2, after, branch, cot, pieces, proj)


def leave_kernel(meta, gm, tok, top, bot, after_grad, pieces, kern, out, kern_out, sums_out, buf, ent, gmx, obuf):
    latents = pl.num_programs(0)
    latent = pl.program_id(0)
    rows_here, cols = tok.shape[1], tok.shape[2]
    half = cols // 2
    row0 = meta[2 * latents]
    shift = pieces[0, 0:1, :]
    scale = 1.0 + pieces[0, 1:2, :]
    taps = [kern[t : t + 1, :] for t in range(9)]
    for rr in range(rows_here + 2):
        source = top[0, 0] if rr == 0 else bot[0, 0] if rr == rows_here + 1 else tok[0, rr - 1]
        put_row(buf, rr, source.astype(F32))
        for parity in range(2):
            normed, _ = normalize(get_columns(buf, rr, parity))
            ok = usable_of(meta, latents, latent, row0 + rr - 1, parity, half)
            put_shifts(ent, rr, parity, ((normed * scale + shift) * ok).astype(BF16).astype(F32))
            group = 2 * ((rr + 1) % 2) + parity
            at = (rr // 2) * half
            put_shifts(gmx, rr, parity, gm[group, at : at + half, :].astype(F32))
    sums = [jnp.zeros((8, D), F32) for _ in range(2)]
    tap_sums = [jnp.zeros((8, D), F32) for _ in range(9)]
    for row in range(rows_here):
        for parity in range(2):
            here = gmx[row + 1, 1 + parity]
            total = here
            for i in range(3):
                for j in range(3):
                    t = 3 * i + j
                    total = total + gmx[row + 2 - i, parity + 2 - j] * taps[t]
                    tap_sums[t] = tap_sums[t] + sum8(ent[row + i, parity + j] * here)
            ok = usable_of(meta, latents, latent, row0 + row, parity, half)
            grad = total * ok
            normed, scaled = normalize(get_columns(buf, row + 1, parity))
            sums[0] = sums[0] + sum8(grad)
            sums[1] = sums[1] + sum8(grad * normed)
            at = (2 * row + parity) * half
            back = after_grad[0, at : at + half, :] + norm_back(grad * scale, normed, scaled)
            put_columns(obuf, row, parity, back)
        out[0, row] = get_row(obuf, row)
    for k in range(2):
        sums_out[0, k : k + 1, :] = jnp.sum(sums[k], axis=0, keepdims=True)
    for t in range(9):
        kern_out[0, t : t + 1, :] = jnp.sum(tap_sums[t], axis=0, keepdims=True)


def leave(meta, gm, tokens, top, bot, after_grad, pieces, kern):
    latents, rows_here, cols, _ = tokens.shape
    half = cols // 2
    own = rows_here * cols
    wide = gm.shape[1]
    whole = lambda *shape: pl.BlockSpec(shape, lambda l, m: (l,) + (0,) * (len(shape) - 1))
    return pl.pallas_call(
        leave_kernel,
        out_shape=(
            jax.ShapeDtypeStruct((latents, rows_here, cols, D), F32),
            jax.ShapeDtypeStruct((latents, 9, D), F32),
            jax.ShapeDtypeStruct((latents, 2, D), F32),
        ),
        grid_spec=pltpu.PrefetchScalarGridSpec(
            num_scalar_prefetch=1,
            grid=(latents,),
            in_specs=[
                whole(4, wide, D),
                whole(1, rows_here, cols, D),
                whole(1, 1, cols, D),
                whole(1, 1, cols, D),
                whole(1, own, D),
                whole(1, 6, D),
                pl.BlockSpec((9, D), lambda l, m: (0, 0)),
            ],
            out_specs=(whole(1, rows_here, cols, D), whole(1, 9, D), whole(1, 2, D)),
            scratch_shapes=[
                pltpu.VMEM((rows_here + 2, LANE_PARTS, cols, 128), F32),
                pltpu.VMEM((rows_here + 2, 4, half, D), F32),
                pltpu.VMEM((rows_here + 2, 4, half, D), F32),
                pltpu.VMEM((rows_here, LANE_PARTS, cols, 128), F32),
            ],
        ),
        compiler_params=pltpu.CompilerParams(vmem_limit_bytes=VMEM_LIMIT),
        name="leave",
    )(meta, gm, tokens, top, bot, after_grad, pieces, kern)


def pair_parts(values):
    lanes = lax.broadcasted_iota(jnp.int32, values.shape, 1)
    first = lanes < HEAD_DIM
    zero = jnp.zeros_like(values)
    return jnp.where(first, values, zero), jnp.where(first, zero, values)


def attend_kernel(mixed, wq, wk, wvt, bias, out, lse_out):
    tokens = mixed.shape[0]
    strips, window, _ = out.shape
    step = tokens // strips
    margin = (window - step) // 2
    m = mixed[...]
    query = (mm(m, wq[...]).astype(BF16) * FACTOR).astype(BF16)
    key = mm(m, wk[...]).astype(BF16)
    value_t = mm(wvt[...], m, NT).astype(BF16)
    keep = jnp.tile(bias[...], (1, tokens // 128))
    parts = []
    for e, key_e in enumerate(pair_parts(key)):
        scores = mm(key_e, query, NT) + keep
        peak = jnp.max(scores, axis=0, keepdims=True)
        raw = jnp.exp(scores - peak)
        total = jnp.sum(raw, axis=0, keepdims=True)
        prob = (raw * (1.0 / total)).astype(BF16)
        parts.append(mm(value_t[e * HEAD_DIM : (e + 1) * HEAD_DIM], prob))
        lse_out[0, e : e + 1, :] = peak + jnp.log(total)
    att = jnp.concatenate(parts, axis=0).T.astype(BF16)
    blank = jnp.zeros((margin, PAIR), BF16)
    for s in range(strips):
        low, high = s * step - margin, (s + 1) * step + margin
        if low < 0:
            out[s] = jnp.concatenate([blank, att[:high]], axis=0)
        elif high > tokens:
            out[s] = jnp.concatenate([att[low:], blank], axis=0)
        else:
            out[s] = att[low:high]


def attend(mixed, weight, weight_t, bias, strips, window):
    tokens = mixed.shape[0]
    return pl.pallas_call(
        attend_kernel,
        out_shape=(
            jax.ShapeDtypeStruct((strips, window, D), BF16),
            jax.ShapeDtypeStruct((PAIRS, 2, tokens), F32),
        ),
        grid=(PAIRS,),
        in_specs=[
            pl.BlockSpec((tokens, D), lambda p: (0, 0)),
            pl.BlockSpec((D, PAIR), lambda p: (0, p)),
            pl.BlockSpec((D, PAIR), lambda p: (0, PAIRS + p)),
            pl.BlockSpec((PAIR, D), lambda p: (2 * PAIRS + p, 0)),
            pl.BlockSpec((tokens, 128), lambda p: (0, 0)),
        ],
        out_specs=(
            pl.BlockSpec((strips, window, PAIR), lambda p: (0, 0, p)),
            pl.BlockSpec((1, 2, tokens), lambda p: (p, 0, 0)),
        ),
        compiler_params=pltpu.CompilerParams(vmem_limit_bytes=VMEM_LIMIT),
        name="attend",
    )(mixed, weight, weight, weight_t, bias)


def attend_back_kernel(offset, query, key, value, key_t, bias, lse, gatt, wq, wk, wv, dq_out, dk_out, dv_out, gm_out, acc):
    tokens = query.shape[0]
    strips, window, _ = gm_out.shape
    step = tokens // strips
    margin = window - step
    p = pl.program_id(0)
    q = query[...]
    keep = jnp.tile(bias[...], (1, tokens // 128))
    queries = pair_parts(q)
    keys = pair_parts(key[...])
    values = pair_parts(value[...])
    grads = pair_parts(gatt[...])
    dk = jnp.zeros((tokens, PAIR), F32)
    dv = jnp.zeros((tokens, PAIR), F32)
    parts = []
    for e in range(2):
        scores = mm(keys[e], q, NT) * FACTOR + keep
        prob = jnp.exp(scores - lse[0, e : e + 1, :])
        grad_prob = mm(values[e], gatt[...], NT)
        delta = jnp.sum(prob * grad_prob, axis=0, keepdims=True)
        grad_scores = (prob * (grad_prob - delta)).astype(BF16)
        dv = dv + mm(prob.astype(BF16), grads[e])
        dk = dk + mm(grad_scores, queries[e])
        parts.append(mm(key_t[e * HEAD_DIM : (e + 1) * HEAD_DIM], grad_scores))
    dq = (jnp.concatenate(parts, axis=0).T * FACTOR).astype(BF16)
    dk = (dk * FACTOR).astype(BF16)
    dv = dv.astype(BF16)
    dq_out[...] = dq
    dk_out[...] = dk
    dv_out[...] = dv
    total = mm(dq, wq[...], NT) + mm(dk, wk[...], NT) + mm(dv, wv[...], NT)

    @pl.when(p == 0)
    def _():
        acc[0:margin] = jnp.zeros((margin, D), F32)
        acc[margin + tokens :] = jnp.zeros((margin, D), F32)
        acc[margin : margin + tokens] = total

    @pl.when(p > 0)
    def _():
        acc[margin : margin + tokens] += total

    @pl.when(p == pl.num_programs(0) - 1)
    def _():
        for s in range(strips):
            start = pl.multiple_of(offset[0] + s * step, 8)
            gm_out[s] = acc[pl.ds(start, window), :].astype(BF16)


def attend_back(offset, triple, key_t, bias, lse, gatt, weight, strips, window):
    tokens = triple.shape[0]
    margin = window - tokens // strips
    part = lambda k: pl.BlockSpec((tokens, PAIR), lambda p, o: (0, k * PAIRS + p))
    slab = lambda k: pl.BlockSpec((D, PAIR), lambda p, o: (0, k * PAIRS + p))
    return pl.pallas_call(
        attend_back_kernel,
        out_shape=(
            jax.ShapeDtypeStruct((tokens, D), BF16),
            jax.ShapeDtypeStruct((tokens, D), BF16),
            jax.ShapeDtypeStruct((tokens, D), BF16),
            jax.ShapeDtypeStruct((strips, window, D), BF16),
        ),
        grid_spec=pltpu.PrefetchScalarGridSpec(
            num_scalar_prefetch=1,
            grid=(PAIRS,),
            in_specs=[
                part(0),
                part(1),
                part(2),
                pl.BlockSpec((PAIR, tokens), lambda p, o: (p, 0)),
                pl.BlockSpec((tokens, 128), lambda p, o: (0, 0)),
                pl.BlockSpec((1, 2, tokens), lambda p, o: (p, 0, 0)),
                part(0),
                slab(0),
                slab(1),
                slab(2),
            ],
            out_specs=(
                part(0),
                part(0),
                part(0),
                pl.BlockSpec((strips, window, D), lambda p, o: (0, 0, 0)),
            ),
            scratch_shapes=[pltpu.VMEM((tokens + 2 * margin, D), F32)],
        ),
        compiler_params=pltpu.CompilerParams(vmem_limit_bytes=VMEM_LIMIT),
        name="attend_back",
    )(offset, triple, triple, triple, key_t, bias, lse, gatt, weight, weight, weight)


def from_before(values, axis):
    count = lax.axis_size(axis)
    return lax.ppermute(values, axis, [(i, i + 1) for i in range(count - 1)])


def from_after(values, axis):
    count = lax.axis_size(axis)
    return lax.ppermute(values, axis, [(i + 1, i) for i in range(count - 1)])


def exchange(values, axis, bit):
    count = lax.axis_size(axis)
    return lax.ppermute(values, axis, [(i, i ^ bit) for i in range(count)])


def swap(values):
    return lax.all_to_all(values, "seq", 0, 0, tiled=False)


BITS = {"y": ("batch", 2), "c": ("batch", 1), "h": ("seq", 4), "l": ("seq", 2), "x": ("seq", 1)}
ORDER = "ychlx"


def halve(values, dims, bit):
    axis, mask = BITS[bit]
    mine = (lax.axis_index(axis) // mask) % 2
    at = dims.index(bit)
    send = lax.dynamic_index_in_dim(values, 1 - mine, at, keepdims=False)
    keep = lax.dynamic_index_in_dim(values, mine, at, keepdims=False)
    got = exchange(send, axis, mask)
    return keep.astype(F32) + got.astype(F32), dims.replace(bit, "")


def reduce_rows(values, order):
    shape = values.shape
    devices = lax.axis_size("batch") * lax.axis_size("seq")
    if lax.axis_size("batch") != 4 or lax.axis_size("seq") != 8:
        return lax.psum_scatter(values, ("batch", "seq"), scatter_dimension=0, tiled=True).astype(F32)
    values = values.reshape((2, 2, 2, 2, 2, shape[0] // devices, shape[1]))
    dims = ORDER
    for bit in order:
        values, dims = halve(values.astype(BF16), dims, bit)
    return values


def gather_seq(values):
    count = lax.axis_size("seq")
    me = lax.axis_index("seq")
    if count > 8:
        return lax.all_gather(values, "seq", axis=0)
    got = [values]
    for k in range(1, count):
        got.append(lax.ppermute(values, "seq", [(i, (i + k) % count) for i in range(count)]))
    back = jnp.stack(got[::-1])
    return lax.dynamic_slice_in_dim(jnp.concatenate([back, back]), (count - 1 - me) % count, count)


def attend_plain(mixed, weight, ok, heads):
    wide = heads * HEAD_DIM
    triple = mm(mixed, weight).astype(BF16)
    split = lambda k: triple[:, k * wide : (k + 1) * wide].reshape(-1, heads, HEAD_DIM)
    queries, keys, values = split(0), split(1), split(2)
    scores = jnp.einsum("qhe,khe->hqk", queries, keys, preferred_element_type=F32) * FACTOR
    scores = jnp.where(ok[None, None, :], scores, -1e30)
    prob = jax.nn.softmax(scores, axis=-1)
    out = jnp.einsum("hqk,khe->qhe", prob.astype(BF16), values, preferred_element_type=F32)
    return out.reshape(-1, wide).astype(BF16), (queries, keys, values, prob)


def attend_plain_back(saved, grad, weight):
    queries, keys, values, prob = saved
    heads = queries.shape[1]
    grad = grad.reshape(-1, heads, HEAD_DIM)
    grad_prob = jnp.einsum("qhe,khe->hqk", grad, values, preferred_element_type=F32)
    delta = jnp.sum(prob * grad_prob, axis=-1, keepdims=True)
    grad_scores = (prob * (grad_prob - delta)).astype(BF16)
    dq = jnp.einsum("hqk,khe->qhe", grad_scores, keys, preferred_element_type=F32) * FACTOR
    dk = jnp.einsum("hqk,qhe->khe", grad_scores, queries, preferred_element_type=F32) * FACTOR
    dv = jnp.einsum("hqk,qhe->khe", prob.astype(BF16), grad, preferred_element_type=F32)
    flat = lambda v: v.reshape(v.shape[0], -1).astype(BF16)
    grads = jnp.concatenate([flat(dq), flat(dk), flat(dv)], axis=1)
    return grads, mm(grads, weight, NT)


def shards(
    tokens,
    cotangent,
    timestep,
    class_ids,
    heights,
    widths,
    time_weight,
    class_table,
    ada_weight,
    ada_bias,
    conv_attn,
    qkv_weight,
    proj_weight,
    up_weight,
    conv_ffn,
    down_weight,
):
    latents, rows_here, cols, _ = tokens.shape
    half = cols // 2
    seq_count = lax.axis_size("seq")
    seq_place = lax.axis_index("seq")
    batch_count = lax.axis_size("batch")
    batch_place = lax.axis_index("batch")
    devices = batch_count * seq_count
    blocks = latents * 4
    share = seq_count // blocks
    per_group = rows_here // 2 * half
    group_tokens = seq_count * per_group

    first, last = tokens[:, :1], tokens[:, rows_here - 1 :]
    top = from_before(last, "seq")
    bot = from_after(first, "seq")
    top_two = from_before(tokens[:, rows_here - 2 : rows_here - 1], "seq")
    bot_two = from_after(tokens[:, 1:2], "seq")
    cot_top = from_before(cotangent[:, rows_here - 1 :], "seq")
    cot_bot = from_after(cotangent[:, :1], "seq")

    half_freq = time_weight.shape[0] // 2
    frequency = jnp.exp(-math.log(10000.0) * jnp.arange(half_freq, dtype=F32) / half_freq)
    angles = timestep.astype(F32)[:, None] * frequency[None, :]
    embedding = jnp.concatenate([jnp.cos(angles), jnp.sin(angles)], axis=1).astype(BF16)
    one_hot = (
        class_ids[:, None] == jnp.arange(class_table.shape[0], dtype=jnp.int32)[None, :]
    ).astype(BF16)
    condition = mm(embedding, time_weight) + mm(one_hot, class_table)
    logistic = jax.nn.sigmoid(condition)
    activated_cond = (condition * logistic).astype(BF16)
    pieces = (mm(activated_cond, ada_weight) + ada_bias).reshape(latents, 6, D)
    meta = jnp.concatenate(
        [heights, widths, jnp.reshape(seq_place * rows_here, (1,))]
    ).astype(jnp.int32)
    kern_attn = conv_attn.astype(F32)
    kern_ffn = conv_ffn.astype(F32)

    mixed = enter(meta, tokens, top, bot, pieces, kern_attn)
    sent = mixed.reshape(blocks, 1, per_group, D)
    sent = jnp.broadcast_to(sent, (blocks, share, per_group, D)).reshape(seq_count, per_group, D)
    grouped = swap(sent).reshape(group_tokens, D)

    my_block = seq_place // share
    my_latent = my_block // 4
    my_a = (my_block // 2) % 2
    my_b = my_block % 2
    places = jnp.arange(group_tokens, dtype=jnp.int32)
    key_row = places // half * 2 + my_a
    key_col = places % half * 2 + my_b
    height = lax.dynamic_index_in_dim(heights, my_latent, 0, keepdims=False)
    width = lax.dynamic_index_in_dim(widths, my_latent, 0, keepdims=False)
    key_ok = (key_row < height) & (key_col < width)

    margin = half
    window = per_group + 2 * margin
    if share == 1:
        bias = jnp.broadcast_to(jnp.where(key_ok, 0.0, -1e30)[:, None], (group_tokens, 128))
        weight_t = qkv_weight.T
        windows, lse = attend(grouped, qkv_weight, weight_t, bias, seq_count, window)
        attended = swap(windows)
    else:
        heads = HEADS // share
        wide = heads * HEAD_DIM
        chunk = seq_place % share
        thirds = qkv_weight.reshape(D, 3, share, wide)
        my_weight = lax.dynamic_index_in_dim(thirds, chunk, 2, keepdims=False).reshape(D, 3 * wide)
        att, saved = attend_plain(grouped, my_weight, key_ok, heads)
        att = jnp.pad(att, ((margin, margin), (0, 0)))
        windows = jnp.stack(
            [att[s * per_group : s * per_group + window] for s in range(seq_count)]
        )
        attended = swap(windows).reshape(blocks, share, window, wide)
        attended = attended.transpose(0, 2, 1, 3).reshape(blocks, window, D)

    ge, get, cot_split = prepare_cot(meta, cotangent, cot_top, cot_bot, pieces)
    e2, e2t, after_attn, branch = second(
        meta, attended, tokens, (top, top_two), (bot, bot_two), pieces, proj_weight
    )
    expanded, grad_e2, down_grad, up_grad, conv_ffn_part = ffn(
        e2, e2t, ge, get, up_weight, down_weight, kern_ffn, cols
    )
    output, grad_after, grad_branch, grad_attended, mid_sums = middle(
        meta, expanded, grad_e2, after_attn, branch, cot_split, pieces, proj_weight, rows_here, cols
    )

    att_own = attended[:, margin : margin + per_group].reshape(blocks * per_group, D)
    flat_branch = grad_branch.reshape(blocks * per_group, D)
    proj_grad = mm(att_own, flat_branch, (((0,), (0,)), ((), ()))).astype(BF16)
    tall = per_group + margin
    if share == 1:
        gatt = swap(grad_attended.reshape(seq_count, per_group, D)).reshape(group_tokens, D)
        triple = mm(grouped, qkv_weight).astype(BF16)
        key_t = mm(weight_t[D : 2 * D], grouped, NT).astype(BF16)
        offset = jnp.reshape(margin * (1 - my_a), (1,)).astype(jnp.int32)
        dq, dk, dv, gm_windows = attend_back(
            offset, triple, key_t, bias, lse, gatt, qkv_weight, seq_count, tall
        )
        gm = swap(gm_windows)
        grad_triple = jnp.concatenate([dq, dk, dv], axis=1)
        qkv_grad = mm(grouped, grad_triple, (((0,), (0,)), ((), ()))).astype(BF16)
    else:
        sent = grad_attended.reshape(blocks, per_group, share, wide).transpose(0, 2, 1, 3)
        gatt = swap(sent.reshape(seq_count, per_group, wide)).reshape(group_tokens, wide)
        grad_triple, gm_part = attend_plain_back(saved, gatt, my_weight)
        base = jnp.pad(gm_part.astype(BF16), ((margin, margin), (0, 0)))
        base = lax.dynamic_slice_in_dim(base, margin * (1 - my_a), group_tokens + margin)
        gm_windows = jnp.stack(
            [base[s * per_group : s * per_group + tall] for s in range(seq_count)]
        )
        gm = swap(gm_windows).reshape(blocks, share, tall, D)
        gm = jnp.sum(gm.astype(F32), axis=1).astype(BF16)
        own_grad = mm(grouped, grad_triple, (((0,), (0,)), ((), ()))).astype(BF16)
        spread = jnp.zeros((D, 3, share, wide), BF16)
        qkv_grad = lax.dynamic_update_index_in_dim(
            spread, own_grad.reshape(D, 3, wide), chunk, 2
        ).reshape(D, 3 * D)

    token_grad, conv_attn_part, end_sums = leave(
        meta, gm, tokens, top, bot, grad_after, pieces, kern_attn
    )

    down_rows = reduce_rows(down_grad, "cyxlh")
    up_rows = reduce_rows(up_grad, "cxlyh")
    proj_rows = reduce_rows(proj_grad, "clhyx")
    qkv_rows = reduce_rows(qkv_grad, "clyhx")

    ffn_rows = conv_ffn_part.reshape(9 * conv_ffn_part.shape[1] // D, D)
    early = jnp.sum(
        gather_seq(jnp.concatenate([mid_sums.reshape(latents * 4, D), ffn_rows])), axis=0
    )
    late = jnp.sum(
        gather_seq(
            jnp.concatenate([end_sums.reshape(latents * 2, D), jnp.sum(conv_attn_part, axis=0)])
        ),
        axis=0,
    )
    early_all = lax.all_gather(early, "batch", axis=0)
    late_all = lax.all_gather(late, "batch", axis=0)
    total = batch_count * latents
    mid_all = early_all[:, : latents * 4].reshape(total, 4, D)
    end_all = late_all[:, : latents * 2].reshape(total, 2, D)
    grad_pieces = jnp.concatenate([end_all, mid_all], axis=1).reshape(total, 6 * D)
    conv_ffn_grad = jnp.sum(early_all[:, latents * 4 :], axis=0).reshape(9, -1)
    conv_attn_grad = jnp.sum(late_all[:, latents * 2 :], axis=0)

    here = batch_place * seq_count + seq_place
    own_cols = D // devices
    conditions = lax.all_gather(
        jnp.concatenate([condition, embedding.astype(F32)], axis=1), "batch", axis=0
    ).reshape(total, -1)
    ids_all = lax.all_gather(class_ids, "batch", axis=0).reshape(total)
    embedding_all = conditions[:, D:]
    condition_all = conditions[:, :D]
    logistic_all = jax.nn.sigmoid(condition_all)
    activated_all = (condition_all * logistic_all).astype(BF16).astype(F32)
    grad_silu = lax.dot_general(
        grad_pieces, ada_weight.astype(F32), NT, precision=HIGHEST, preferred_element_type=F32
    )
    cond_all = grad_silu * logistic_all * (1.0 + condition_all * (1.0 - logistic_all))
    cond_grad = lax.dynamic_slice_in_dim(cond_all, batch_place * latents, latents)
    cond_cols = lax.dynamic_slice_in_dim(cond_all, here * own_cols, own_cols, axis=1)
    act_cols = lax.dynamic_slice_in_dim(activated_all, here * own_cols, own_cols, axis=1)
    outer = lambda left, right: lax.dot_general(
        left, right, (((0,), (0,)), ((), ())), precision=HIGHEST, preferred_element_type=F32
    )
    hot_all = (ids_all[:, None] == jnp.arange(class_table.shape[0], dtype=jnp.int32)[None, :]).astype(F32)
    bias_grad = jnp.sum(grad_pieces, axis=0)
    bias_cols = 6 * D // devices
    hidden_cols = conv_ffn.shape[1] // devices
    return (
        output,
        token_grad,
        cond_grad,
        outer(embedding_all, cond_cols),
        outer(hot_all, cond_cols),
        outer(act_cols, grad_pieces),
        lax.dynamic_slice_in_dim(bias_grad, here * bias_cols, bias_cols),
        lax.dynamic_slice_in_dim(conv_attn_grad, here * own_cols, own_cols, axis=1),
        qkv_rows,
        proj_rows,
        up_rows,
        lax.dynamic_slice_in_dim(conv_ffn_grad, here * hidden_cols, hidden_cols, axis=1),
        down_rows.T,
    )


def solution(mesh):
    strips = P("batch", "seq", None, None)
    in_specs = (strips, strips) + (P("batch"),) * 4 + (P(),) * 10
    both = ("batch", "seq")
    out_specs = (
        strips,
        strips,
        P("batch", None),
        P(None, both),
        P(None, both),
        P(both, None),
        P(both),
        P(None, both),
        P(both, None),
        P(both, None),
        P(both, None),
        P(None, both),
        P(None, both),
    )
    return jax.shard_map(shards, mesh=mesh, in_specs=in_specs, out_specs=out_specs, check_vma=False)
```

```python
import functools
import math

import jax
import jax.numpy as jnp
from jax import lax
from jax.experimental import pallas as pl
from jax.experimental.pallas import tpu as pltpu
from jax.sharding import PartitionSpec as P

D = 768
HEADS = 12
HEAD_DIM = 64
PAIR = 2 * HEAD_DIM
PAIRS = HEADS // 2
FF_BLOCK = 256
LANE_PARTS = D // 128
FACTOR = HEAD_DIM ** (-0.5)

F32 = jnp.float32
BF16 = jnp.bfloat16
HIGHEST = lax.Precision.HIGHEST
NN = (((1,), (0,)), ((), ()))
NT = (((1,), (1,)), ((), ()))
VMEM_LIMIT = 60 * 1024 * 1024


def mm(left, right, dims=NN):
    return lax.dot_general(left, right, dims, preferred_element_type=F32)


def shift_down(values):
    rows = lax.broadcasted_iota(jnp.int32, values.shape, 0)
    return jnp.where(rows == 0, 0.0, pltpu.roll(values, 1, 0))


def shift_up(values):
    count = values.shape[0]
    rows = lax.broadcasted_iota(jnp.int32, values.shape, 0)
    return jnp.where(rows == count - 1, 0.0, pltpu.roll(values, count - 1, 0))


def put_shifts(ref, row, parity, values):
    ref[row, 1 + parity] = values
    if parity == 0:
        ref[row, 3] = shift_up(values)
    else:
        ref[row, 0] = shift_down(values)


def normalize(values):
    centre = values - jnp.mean(values, axis=-1, keepdims=True)
    spread = jnp.mean(centre * centre, axis=-1, keepdims=True)
    scaled = lax.rsqrt(spread + 1e-06)
    return centre * scaled, scaled


def norm_back(grad_norm, normed, scaled):
    return scaled * (
        grad_norm
        - jnp.mean(grad_norm, axis=-1, keepdims=True)
        - normed * jnp.mean(grad_norm * normed, axis=-1, keepdims=True)
    )


def put_row(buf, row, values):
    for k in range(LANE_PARTS):
        buf[row, k] = values[:, 128 * k : 128 * (k + 1)]


def get_row(buf, row):
    return jnp.concatenate([buf[row, k] for k in range(LANE_PARTS)], axis=1)


def put_columns(buf, row, parity, values):
    for k in range(LANE_PARTS):
        buf[row, k, pl.ds(parity, values.shape[0], stride=2), :] = values[:, 128 * k : 128 * (k + 1)]


def get_columns(buf, row, parity):
    half = buf.shape[2] // 2
    return jnp.concatenate(
        [buf[row, k, pl.ds(parity, half, stride=2), :] for k in range(LANE_PARTS)], axis=1
    )


def usable_of(meta, latents, latent, row, parity, half):
    cols = 2 * lax.broadcasted_iota(jnp.int32, (half, 1), 0) + parity
    row_ok = jnp.logical_and(row >= 0, row < meta[latent])
    limit = jnp.where(row_ok, meta[latents + latent], 0)
    return (cols < limit).astype(F32)


def sum8(values):
    total = values[0:8]
    for start in range(8, values.shape[0], 8):
        total = total + values[start : start + 8]
    return total


def enter_kernel(meta, tok, top, bot, pieces, kern, out, buf, ent):
    latents = pl.num_programs(0)
    latent = pl.program_id(0)
    rows_here, cols = tok.shape[1], tok.shape[2]
    half = cols // 2
    row0 = meta[2 * latents]
    shift = pieces[0, 0:1, :]
    scale = 1.0 + pieces[0, 1:2, :]
    for rr in range(rows_here + 2):
        source = top[0, 0] if rr == 0 else bot[0, 0] if rr == rows_here + 1 else tok[0, rr - 1]
        put_row(buf, rr, source.astype(F32))
        for parity in range(2):
            normed, _ = normalize(get_columns(buf, rr, parity))
            ok = usable_of(meta, latents, latent, row0 + rr - 1, parity, half)
            put_shifts(ent, rr, parity, ((normed * scale + shift) * ok).astype(BF16).astype(F32))
    for row in range(rows_here):
        for parity in range(2):
            total = jnp.zeros((half, D), F32)
            for i in range(3):
                for j in range(3):
                    tap = 3 * i + j
                    total = total + ent[row + i, parity + j] * kern[tap : tap + 1, :]
            mixed = (ent[row + 1, 1 + parity] + total).astype(BF16)
            group = 2 * (row % 2) + parity
            out[0, group, (row // 2) * half : (row // 2 + 1) * half, :] = mixed


def enter(meta, tokens, top, bot, pieces, kern):
    latents, rows_here, cols, _ = tokens.shape
    half = cols // 2
    per_group = rows_here // 2 * half
    whole = lambda *shape: pl.BlockSpec(shape, lambda l, m: (l,) + (0,) * (len(shape) - 1))
    return pl.pallas_call(
        enter_kernel,
        out_shape=jax.ShapeDtypeStruct((latents, 4, per_group, D), BF16),
        grid_spec=pltpu.PrefetchScalarGridSpec(
            num_scalar_prefetch=1,
            grid=(latents,),
            in_specs=[
                whole(1, rows_here, cols, D),
                whole(1, 1, cols, D),
                whole(1, 1, cols, D),
                whole(1, 6, D),
                pl.BlockSpec((9, D), lambda l, m: (0, 0)),
            ],
            out_specs=whole(1, 4, per_group, D),
            scratch_shapes=[
                pltpu.VMEM((rows_here + 2, LANE_PARTS, cols, 128), F32),
                pltpu.VMEM((rows_here + 2, 4, half, D), F32),
            ],
        ),
        compiler_params=pltpu.CompilerParams(vmem_limit_bytes=VMEM_LIMIT),
        name="enter",
    )(meta, tokens, top, bot, pieces, kern)


def cot_kernel(meta, cot, top, bot, pieces, ge_out, get_out, cot_out, buf):
    rows_here, cols = cot.shape[1], cot.shape[2]
    half = cols // 2
    gate = pieces[0, 5:6, :]
    for rr in range(rows_here + 2):
        source = top[0, 0] if rr == 0 else bot[0, 0] if rr == rows_here + 1 else cot[0, rr - 1]
        put_row(buf, rr, source.astype(F32))
        for parity in range(2):
            values = get_columns(buf, rr, parity)
            scaled = (gate * values).astype(BF16)
            at = (2 * rr + parity) * half
            ge_out[0, at : at + half, :] = scaled
            if 1 <= rr <= rows_here:
                cot_out[0, at - cols : at - cols + half, :] = values.astype(BF16)
    inner = ge_out[0, cols : cols + rows_here * cols, :].astype(F32)
    get_out[0] = inner.T.astype(BF16)


def prepare_cot(meta, cotangent, top, bot, pieces):
    latents, rows_here, cols, _ = cotangent.shape
    whole = lambda *shape: pl.BlockSpec(shape, lambda l, m: (l,) + (0,) * (len(shape) - 1))
    own = rows_here * cols
    return pl.pallas_call(
        cot_kernel,
        out_shape=(
            jax.ShapeDtypeStruct((latents, own + 2 * cols, D), BF16),
            jax.ShapeDtypeStruct((latents, D, own), BF16),
            jax.ShapeDtypeStruct((latents, own, D), BF16),
        ),
        grid_spec=pltpu.PrefetchScalarGridSpec(
            num_scalar_prefetch=1,
            grid=(latents,),
            in_specs=[
                whole(1, rows_here, cols, D),
                whole(1, 1, cols, D),
                whole(1, 1, cols, D),
                whole(1, 6, D),
            ],
            out_specs=(whole(1, own + 2 * cols, D), whole(1, D, own), whole(1, own, D)),
            scratch_shapes=[pltpu.VMEM((rows_here + 2, LANE_PARTS, cols, 128), F32)],
        ),
        compiler_params=pltpu.CompilerParams(vmem_limit_bytes=VMEM_LIMIT),
        name="prepare_cot",
    )(meta, cotangent, top, bot, pieces)


def second_kernel(meta, att, tok, top2, top1, bot1, bot2, pieces, proj, e2_out, e2t_out, after_out, branch_out, buf, bran):
    latents = pl.num_programs(0)
    latent = pl.program_id(0)
    rows_here, cols = tok.shape[1], tok.shape[2]
    half = cols // 2
    row0 = meta[2 * latents]
    gate = pieces[0, 2:3, :]
    shift = pieces[0, 3:4, :]
    scale = 1.0 + pieces[0, 4:5, :]
    for group in range(4):
        bran[group] = mm(att[group], proj[...])
    for rr in range(rows_here + 4):
        at_row = rr - 2
        source = (
            top2[0, 0]
            if at_row == -2
            else top1[0, 0]
            if at_row == -1
            else bot1[0, 0]
            if at_row == rows_here
            else bot2[0, 0]
            if at_row == rows_here + 1
            else tok[0, at_row]
        )
        put_row(buf, rr, source.astype(F32))
        for parity in range(2):
            group = 2 * (rr % 2) + parity
            branch = bran[group, (rr // 2) * half : (rr // 2 + 1) * half, :]
            after = get_columns(buf, rr, parity) + gate * branch
            normed, _ = normalize(after)
            ok = usable_of(meta, latents, latent, row0 + at_row, parity, half)
            at = (2 * rr + parity) * half
            e2_out[0, at : at + half, :] = ((normed * scale + shift) * ok).astype(BF16)
            if 0 <= at_row < rows_here:
                own = at - 2 * cols
                after_out[0, own : own + half, :] = after
                branch_out[0, own : own + half, :] = branch
    inner = e2_out[0, 2 * cols : 2 * cols + rows_here * cols, :].astype(F32)
    e2t_out[0] = inner.T.astype(BF16)


def second(meta, attended, tokens, tops, bots, pieces, proj):
    latents, rows_here, cols, _ = tokens.shape
    half = cols // 2
    own = rows_here * cols
    wide = attended.shape[1]
    whole = lambda *shape: pl.BlockSpec(shape, lambda l, m: (l,) + (0,) * (len(shape) - 1))
    return pl.pallas_call(
        second_kernel,
        out_shape=(
            jax.ShapeDtypeStruct((latents, own + 4 * cols, D), BF16),
            jax.ShapeDtypeStruct((latents, D, own), BF16),
            jax.ShapeDtypeStruct((latents, own, D), F32),
            jax.ShapeDtypeStruct((latents, own, D), F32),
        ),
        grid_spec=pltpu.PrefetchScalarGridSpec(
            num_scalar_prefetch=1,
            grid=(latents,),
            in_specs=[
                whole(4, wide, D),
                whole(1, rows_here, cols, D),
                whole(1, 1, cols, D),
                whole(1, 1, cols, D),
                whole(1, 1, cols, D),
                whole(1, 1, cols, D),
                whole(1, 6, D),
                pl.BlockSpec((D, D), lambda l, m: (0, 0)),
            ],
            out_specs=(
                whole(1, own + 4 * cols, D),
                whole(1, D, own),
                whole(1, own, D),
                whole(1, own, D),
            ),
            scratch_shapes=[
                pltpu.VMEM((rows_here + 4, LANE_PARTS, cols, 128), F32),
                pltpu.VMEM((4, wide, D), F32),
            ],
        ),
        compiler_params=pltpu.CompilerParams(vmem_limit_bytes=VMEM_LIMIT),
        name="second",
    )(meta, attended, tokens, tops[1], tops[0], bots[0], bots[1], pieces, proj)


def normal_parts(values):
    density = jnp.exp(-0.5 * values * values) * 0.3989422804014327
    t = 1.0 / (1.0 + 0.2316419 * jnp.abs(values))
    series = t * (
        0.319381530
        + t * (-0.356563782 + t * (1.781477937 + t * (-1.821255978 + t * 1.330274429)))
    )
    tail = density * series
    return jnp.where(values > 0.0, 1.0 - tail, tail), density


def ffn_kernel(core, e2, e2t, ge, get, up, down, kern_in, exp_out, ge2_out, send_out, keep_out, kern_out, *scratch):
    latents = e2.shape[0]
    lifted, gact, gconv, act, graised = [scratch[k * latents : (k + 1) * latents] for k in range(5)]
    down_acc, up_acc = scratch[5 * latents :]
    step = pl.program_id(0)
    half = lifted[0].shape[2]
    rows_here = lifted[0].shape[0] - 4
    block = lifted[0].shape[3]
    taps = [kern_in[t : t + 1, :].astype(F32) for t in range(9)]
    sums = [jnp.zeros((8, block), F32) for _ in range(9)]
    rows_per = 4

    def lift(latent, part):
        size = rows_per * 2 * half
        raised = mm(e2[latent, part * size : (part + 1) * size], up[...])
        raised = raised.astype(BF16).astype(F32)
        for k in range(rows_per):
            for parity in range(2):
                at = (2 * k + parity) * half
                put_shifts(lifted[latent], part * rows_per + k, parity, raised[at : at + half])

    def pull(latent, part):
        size = gact[latent].shape[0] // 2
        at = part * size
        gact[latent][at : at + size] = mm(ge[latent, at : at + size], down[...], NT)

    def bend(latent, rr):
        for parity in range(2):
            total = None
            for i in range(3):
                for j in range(3):
                    term = lifted[latent][rr + i, parity + j] * taps[3 * i + j]
                    total = term if total is None else total + term
            cdf, density = normal_parts(total)
            at = (2 * rr + parity) * half
            if 1 <= rr <= rows_here:
                own = at - 2 * half
                act[latent][own : own + half, :] = (total * cdf).astype(BF16)
            grad = gact[latent][at : at + half, :] * (cdf + total * density)
            put_shifts(gconv[latent], rr, parity, grad.astype(BF16).astype(F32))

    def unbend(latent, row):
        for parity in range(2):
            total = None
            here = gconv[latent][row + 1, 1 + parity]
            for i in range(3):
                for j in range(3):
                    t = 3 * i + j
                    term = gconv[latent][row + 2 - i, parity + 2 - j] * taps[t]
                    total = term if total is None else total + term
                    sums[t] = sums[t] + sum8(lifted[latent][row + 1 + i, parity + j] * here)
            at = (2 * row + parity) * half
            graised[latent][at : at + half, :] = total.astype(BF16)

    def gather(latent, part):
        cut = slice(part * 256, (part + 1) * 256)
        if part == 0:
            exp_out[latent] += mm(act[latent][...], down[...])
        elif part == 1:
            ge2_out[latent] += mm(graised[latent][...], up[...], NT)
        elif part == 2:
            value = mm(get[latent], act[latent][...])
            down_acc[...] = value if latent == 0 else down_acc[...] + value
        else:
            value = mm(e2t[latent], graised[latent][...])
            up_acc[...] = value if latent == 0 else up_acc[...] + value

    @pl.when(step == 0)
    def _():
        exp_out[...] = jnp.zeros_like(exp_out)
        ge2_out[...] = jnp.zeros_like(ge2_out)

    lifts = (rows_here + 4) // rows_per
    for part in range(lifts):
        lift(0, part)
    for part in range(2):
        pull(0, part)
    for latent in range(latents):
        more = []
        if latent + 1 < latents:
            more += [functools.partial(lift, latent + 1, part) for part in range(lifts)]
            more += [functools.partial(pull, latent + 1, part) for part in range(2)]
        if latent > 0:
            more += [functools.partial(gather, latent - 1, part) for part in range(4)]
        work = [functools.partial(bend, latent, rr) for rr in range(rows_here + 2)]
        work += [functools.partial(unbend, latent, row) for row in range(rows_here)]
        for k, unit in enumerate(work):
            if k < len(more):
                more[k]()
            unit()
        for unit in more[len(work) :]:
            unit()
    for part in range(4):
        gather(latents - 1, part)

    size = down_acc.shape[0] // 4
    for which, acc in enumerate((down_acc, up_acc)):
        for y in range(2):
            mine = pl.multiple_of((2 * y + core[0]) * size, 8)
            other = pl.multiple_of((2 * y + 1 - core[0]) * size, 8)
            keep_out[which, y] = acc[pl.ds(mine, size), :].astype(BF16)
            send_out[which, y] = acc[pl.ds(other, size), :].astype(BF16)
    for t in range(9):
        kern_out[t : t + 1, :] = jnp.sum(sums[t], axis=0, keepdims=True)


def ffn(core, e2, e2t, ge, get, up, down, kern, cols):
    latents = e2.shape[0]
    half = cols // 2
    own = e2t.shape[2]
    rows_here = own // cols
    hidden = up.shape[1]
    fixed = lambda *shape: pl.BlockSpec(shape, lambda f, c: (0,) * len(shape))
    parts = jax.ShapeDtypeStruct((2, 2, D // 4, hidden), BF16)
    parts_spec = pl.BlockSpec((2, 2, D // 4, FF_BLOCK), lambda f, c: (0, 0, 0, f))
    each = lambda *args: [pltpu.VMEM(*args)] * latents
    return pl.pallas_call(
        ffn_kernel,
        out_shape=(
            jax.ShapeDtypeStruct((latents, own, D), F32),
            jax.ShapeDtypeStruct((latents, own, D), F32),
            parts,
            parts,
            jax.ShapeDtypeStruct((9, hidden), F32),
        ),
        grid_spec=pltpu.PrefetchScalarGridSpec(
            num_scalar_prefetch=1,
            grid=(hidden // FF_BLOCK,),
            in_specs=[
                fixed(latents, own + 4 * cols, D),
                fixed(latents, D, own),
                fixed(latents, own + 2 * cols, D),
                fixed(latents, D, own),
                pl.BlockSpec((D, FF_BLOCK), lambda f, c: (0, f)),
                pl.BlockSpec((FF_BLOCK, D), lambda f, c: (f, 0)),
                pl.BlockSpec((9, FF_BLOCK), lambda f, c: (0, f)),
            ],
            out_specs=(
                fixed(latents, own, D),
                fixed(latents, own, D),
                parts_spec,
                parts_spec,
                pl.BlockSpec((9, FF_BLOCK), lambda f, c: (0, f)),
            ),
            scratch_shapes=each((rows_here + 4, 4, half, FF_BLOCK), F32)
            + each((own + 2 * cols, FF_BLOCK), F32)
            + each((rows_here + 2, 4, half, FF_BLOCK), F32)
            + each((own, FF_BLOCK), BF16)
            + each((own, FF_BLOCK), BF16)
            + [pltpu.VMEM((D, FF_BLOCK), F32), pltpu.VMEM((D, FF_BLOCK), F32)],
        ),
        compiler_params=pltpu.CompilerParams(vmem_limit_bytes=VMEM_LIMIT),
        name="ffn",
    )(core, e2, e2t, ge, get, up, down, kern)


def middle_kernel(meta, exp, ge2, after_in, branch_in, cot_in, pieces, proj, out, after_grad, gb_out, gatt_out, sums_out, buf):
    latents = pl.num_programs(0)
    latent = pl.program_id(0)
    rows_here, cols = out.shape[1], out.shape[2]
    half = cols // 2
    row0 = meta[2 * latents]
    gate_one = pieces[0, 2:3, :]
    scale = 1.0 + pieces[0, 4:5, :]
    gate_two = pieces[0, 5:6, :]
    sums = [jnp.zeros((8, D), F32) for _ in range(4)]
    for row in range(rows_here):
        for parity in range(2):
            at = (2 * row + parity) * half
            part = pl.ds(at, half)
            after = after_in[0, part, :]
            cot = cot_in[0, part, :].astype(F32)
            expanded = exp[0, part, :]
            put_columns(buf, row, parity, after + gate_two * expanded)
            normed, scaled = normalize(after)
            ok = usable_of(meta, latents, latent, row0 + row, parity, half)
            grad = ge2[0, part, :] * ok
            grad_after = cot + norm_back(grad * scale, normed, scaled)
            after_grad[0, part, :] = grad_after
            sums[0] = sums[0] + sum8(grad_after * branch_in[0, part, :])
            sums[1] = sums[1] + sum8(grad)
            sums[2] = sums[2] + sum8(grad * normed)
            sums[3] = sums[3] + sum8(cot * expanded)
            group = 2 * (row % 2) + parity
            to = pl.ds((row // 2) * half, half)
            gb_out[0, group, to, :] = (gate_one * grad_after).astype(BF16)
        out[0, row] = get_row(buf, row).astype(BF16)
    for k in range(4):
        sums_out[0, k : k + 1, :] = jnp.sum(sums[k], axis=0, keepdims=True)
    for group in range(4):
        gatt_out[0, group] = mm(gb_out[0, group], proj[...], NT).astype(BF16)


def middle(meta, exp, ge2, after, branch, cot, pieces, proj, rows_here, cols):
    latents, own, _ = exp.shape
    per_group = own // 4
    whole = lambda *shape: pl.BlockSpec(shape, lambda l, m: (l,) + (0,) * (len(shape) - 1))
    return pl.pallas_call(
        middle_kernel,
        out_shape=(
            jax.ShapeDtypeStruct((latents, rows_here, cols, D), BF16),
            jax.ShapeDtypeStruct((latents, own, D), F32),
            jax.ShapeDtypeStruct((latents, 4, per_group, D), BF16),
            jax.ShapeDtypeStruct((latents, 4, per_group, D), BF16),
            jax.ShapeDtypeStruct((latents, 4, D), F32),
        ),
        grid_spec=pltpu.PrefetchScalarGridSpec(
            num_scalar_prefetch=1,
            grid=(latents,),
            in_specs=[
                whole(1, own, D),
                whole(1, own, D),
                whole(1, own, D),
                whole(1, own, D),
                whole(1, own, D),
                whole(1, 6, D),
                pl.BlockSpec((D, D), lambda l, m: (0, 0)),
            ],
            out_specs=(
                whole(1, rows_here, cols, D),
                whole(1, own, D),
                whole(1, 4, per_group, D),
                whole(1, 4, per_group, D),
                whole(1, 4, D),
            ),
            scratch_shapes=[
                pltpu.VMEM((rows_here, LANE_PARTS, cols, 128), F32),
            ],
        ),
        compiler_params=pltpu.CompilerParams(vmem_limit_bytes=VMEM_LIMIT),
        name="middle",
    )(meta, exp, ge2, after, branch, cot, pieces, proj)


def leave_kernel(meta, gm, tok, top, bot, after_grad, pieces, kern, out, kern_out, sums_out, buf, ent, gmx, obuf):
    latents = pl.num_programs(0)
    latent = pl.program_id(0)
    rows_here, cols = tok.shape[1], tok.shape[2]
    half = cols // 2
    row0 = meta[2 * latents]
    shift = pieces[0, 0:1, :]
    scale = 1.0 + pieces[0, 1:2, :]
    taps = [kern[t : t + 1, :] for t in range(9)]
    for rr in range(rows_here + 2):
        source = top[0, 0] if rr == 0 else bot[0, 0] if rr == rows_here + 1 else tok[0, rr - 1]
        put_row(buf, rr, source.astype(F32))
        for parity in range(2):
            normed, _ = normalize(get_columns(buf, rr, parity))
            ok = usable_of(meta, latents, latent, row0 + rr - 1, parity, half)
            put_shifts(ent, rr, parity, ((normed * scale + shift) * ok).astype(BF16).astype(F32))
            group = 2 * ((rr + 1) % 2) + parity
            at = (rr // 2) * half
            put_shifts(gmx, rr, parity, gm[group, at : at + half, :].astype(F32))
    sums = [jnp.zeros((8, D), F32) for _ in range(2)]
    tap_sums = [jnp.zeros((8, D), F32) for _ in range(9)]
    for row in range(rows_here):
        for parity in range(2):
            here = gmx[row + 1, 1 + parity]
            total = here
            for i in range(3):
                for j in range(3):
                    t = 3 * i + j
                    total = total + gmx[row + 2 - i, parity + 2 - j] * taps[t]
                    tap_sums[t] = tap_sums[t] + sum8(ent[row + i, parity + j] * here)
            ok = usable_of(meta, latents, latent, row0 + row, parity, half)
            grad = total * ok
            normed, scaled = normalize(get_columns(buf, row + 1, parity))
            sums[0] = sums[0] + sum8(grad)
            sums[1] = sums[1] + sum8(grad * normed)
            at = (2 * row + parity) * half
            back = after_grad[0, at : at + half, :] + norm_back(grad * scale, normed, scaled)
            put_columns(obuf, row, parity, back)
        out[0, row] = get_row(obuf, row)
    for k in range(2):
        sums_out[0, k : k + 1, :] = jnp.sum(sums[k], axis=0, keepdims=True)
    for t in range(9):
        kern_out[0, t : t + 1, :] = jnp.sum(tap_sums[t], axis=0, keepdims=True)


def leave(meta, gm, tokens, top, bot, after_grad, pieces, kern):
    latents, rows_here, cols, _ = tokens.shape
    half = cols // 2
    own = rows_here * cols
    wide = gm.shape[1]
    whole = lambda *shape: pl.BlockSpec(shape, lambda l, m: (l,) + (0,) * (len(shape) - 1))
    return pl.pallas_call(
        leave_kernel,
        out_shape=(
            jax.ShapeDtypeStruct((latents, rows_here, cols, D), F32),
            jax.ShapeDtypeStruct((latents, 9, D), F32),
            jax.ShapeDtypeStruct((latents, 2, D), F32),
        ),
        grid_spec=pltpu.PrefetchScalarGridSpec(
            num_scalar_prefetch=1,
            grid=(latents,),
            in_specs=[
                whole(4, wide, D),
                whole(1, rows_here, cols, D),
                whole(1, 1, cols, D),
                whole(1, 1, cols, D),
                whole(1, own, D),
                whole(1, 6, D),
                pl.BlockSpec((9, D), lambda l, m: (0, 0)),
            ],
            out_specs=(whole(1, rows_here, cols, D), whole(1, 9, D), whole(1, 2, D)),
            scratch_shapes=[
                pltpu.VMEM((rows_here + 2, LANE_PARTS, cols, 128), F32),
                pltpu.VMEM((rows_here + 2, 4, half, D), F32),
                pltpu.VMEM((rows_here + 2, 4, half, D), F32),
                pltpu.VMEM((rows_here, LANE_PARTS, cols, 128), F32),
            ],
        ),
        compiler_params=pltpu.CompilerParams(vmem_limit_bytes=VMEM_LIMIT),
        name="leave",
    )(meta, gm, tokens, top, bot, after_grad, pieces, kern)


def pair_parts(values):
    lanes = lax.broadcasted_iota(jnp.int32, values.shape, 1)
    first = lanes < HEAD_DIM
    zero = jnp.zeros_like(values)
    return jnp.where(first, values, zero), jnp.where(first, zero, values)


def attend_kernel(mixed, wq, wk, wvt, bias, out, lse_out):
    tokens = mixed.shape[0]
    strips, window, _ = out.shape
    step = tokens // strips
    margin = (window - step) // 2
    m = mixed[...]
    query = (mm(m, wq[...]).astype(BF16) * FACTOR).astype(BF16)
    key = mm(m, wk[...]).astype(BF16)
    value_t = mm(wvt[...], m, NT).astype(BF16)
    keep = jnp.tile(bias[...], (1, tokens // 128))
    parts = []
    for e, key_e in enumerate(pair_parts(key)):
        scores = mm(key_e, query, NT) + keep
        peak = jnp.max(scores, axis=0, keepdims=True)
        raw = jnp.exp(scores - peak)
        total = jnp.sum(raw, axis=0, keepdims=True)
        prob = (raw * (1.0 / total)).astype(BF16)
        parts.append(mm(value_t[e * HEAD_DIM : (e + 1) * HEAD_DIM], prob))
        lse_out[0, e : e + 1, :] = peak + jnp.log(total)
    att = jnp.concatenate(parts, axis=0).T.astype(BF16)
    blank = jnp.zeros((margin, PAIR), BF16)
    for s in range(strips):
        low, high = s * step - margin, (s + 1) * step + margin
        if low < 0:
            out[s] = jnp.concatenate([blank, att[:high]], axis=0)
        elif high > tokens:
            out[s] = jnp.concatenate([att[low:], blank], axis=0)
        else:
            out[s] = att[low:high]


def attend(mixed, weight, weight_t, bias, strips, window):
    tokens = mixed.shape[0]
    return pl.pallas_call(
        attend_kernel,
        out_shape=(
            jax.ShapeDtypeStruct((strips, window, D), BF16),
            jax.ShapeDtypeStruct((PAIRS, 2, tokens), F32),
        ),
        grid=(PAIRS,),
        in_specs=[
            pl.BlockSpec((tokens, D), lambda p: (0, 0)),
            pl.BlockSpec((D, PAIR), lambda p: (0, p)),
            pl.BlockSpec((D, PAIR), lambda p: (0, PAIRS + p)),
            pl.BlockSpec((PAIR, D), lambda p: (2 * PAIRS + p, 0)),
            pl.BlockSpec((tokens, 128), lambda p: (0, 0)),
        ],
        out_specs=(
            pl.BlockSpec((strips, window, PAIR), lambda p: (0, 0, p)),
            pl.BlockSpec((1, 2, tokens), lambda p: (p, 0, 0)),
        ),
        compiler_params=pltpu.CompilerParams(vmem_limit_bytes=VMEM_LIMIT),
        name="attend",
    )(mixed, weight, weight, weight_t, bias)


def attend_back_kernel(offset, query, key, value, key_t, bias, lse, gatt, wq, wk, wv, dq_out, dk_out, dv_out, gm_out, acc):
    tokens = query.shape[0]
    strips, window, _ = gm_out.shape
    step = tokens // strips
    margin = window - step
    p = pl.program_id(0)
    q = query[...]
    keep = jnp.tile(bias[...], (1, tokens // 128))
    queries = pair_parts(q)
    keys = pair_parts(key[...])
    values = pair_parts(value[...])
    grads = pair_parts(gatt[...])
    dk = jnp.zeros((tokens, PAIR), F32)
    dv = jnp.zeros((tokens, PAIR), F32)
    parts = []
    for e in range(2):
        scores = mm(keys[e], q, NT) * FACTOR + keep
        prob = jnp.exp(scores - lse[0, e : e + 1, :])
        grad_prob = mm(values[e], gatt[...], NT)
        delta = jnp.sum(prob * grad_prob, axis=0, keepdims=True)
        grad_scores = (prob * (grad_prob - delta)).astype(BF16)
        dv = dv + mm(prob.astype(BF16), grads[e])
        dk = dk + mm(grad_scores, queries[e])
        parts.append(mm(key_t[e * HEAD_DIM : (e + 1) * HEAD_DIM], grad_scores))
    dq = (jnp.concatenate(parts, axis=0).T * FACTOR).astype(BF16)
    dk = (dk * FACTOR).astype(BF16)
    dv = dv.astype(BF16)
    dq_out[...] = dq
    dk_out[...] = dk
    dv_out[...] = dv
    total = mm(dq, wq[...], NT) + mm(dk, wk[...], NT) + mm(dv, wv[...], NT)

    @pl.when(p == 0)
    def _():
        acc[0:margin] = jnp.zeros((margin, D), F32)
        acc[margin + tokens :] = jnp.zeros((margin, D), F32)
        acc[margin : margin + tokens] = total

    @pl.when(p > 0)
    def _():
        acc[margin : margin + tokens] += total

    @pl.when(p == pl.num_programs(0) - 1)
    def _():
        for s in range(strips):
            start = pl.multiple_of(offset[0] + s * step, 8)
            gm_out[s] = acc[pl.ds(start, window), :].astype(BF16)


def attend_back(offset, triple, key_t, bias, lse, gatt, weight, strips, window):
    tokens = triple.shape[0]
    margin = window - tokens // strips
    part = lambda k: pl.BlockSpec((tokens, PAIR), lambda p, o: (0, k * PAIRS + p))
    slab = lambda k: pl.BlockSpec((D, PAIR), lambda p, o: (0, k * PAIRS + p))
    return pl.pallas_call(
        attend_back_kernel,
        out_shape=(
            jax.ShapeDtypeStruct((tokens, D), BF16),
            jax.ShapeDtypeStruct((tokens, D), BF16),
            jax.ShapeDtypeStruct((tokens, D), BF16),
            jax.ShapeDtypeStruct((strips, window, D), BF16),
        ),
        grid_spec=pltpu.PrefetchScalarGridSpec(
            num_scalar_prefetch=1,
            grid=(PAIRS,),
            in_specs=[
                part(0),
                part(1),
                part(2),
                pl.BlockSpec((PAIR, tokens), lambda p, o: (p, 0)),
                pl.BlockSpec((tokens, 128), lambda p, o: (0, 0)),
                pl.BlockSpec((1, 2, tokens), lambda p, o: (p, 0, 0)),
                part(0),
                slab(0),
                slab(1),
                slab(2),
            ],
            out_specs=(
                part(0),
                part(0),
                part(0),
                pl.BlockSpec((strips, window, D), lambda p, o: (0, 0, 0)),
            ),
            scratch_shapes=[pltpu.VMEM((tokens + 2 * margin, D), F32)],
        ),
        compiler_params=pltpu.CompilerParams(vmem_limit_bytes=VMEM_LIMIT),
        name="attend_back",
    )(offset, triple, triple, triple, key_t, bias, lse, gatt, weight, weight, weight)


def from_before(values, axis):
    count = lax.axis_size(axis)
    return lax.ppermute(values, axis, [(i, i + 1) for i in range(count - 1)])


def from_after(values, axis):
    count = lax.axis_size(axis)
    return lax.ppermute(values, axis, [(i + 1, i) for i in range(count - 1)])


def swap(values):
    return lax.all_to_all(values, "seq", 0, 0, tiled=False)


BITS = {"y": ("batch", 2), "c": ("batch", 1), "h": ("seq", 4), "l": ("seq", 2), "x": ("seq", 1)}
ORDER = "ychlx"


def blocks_of(values):
    return values.reshape(values.shape[:-2] + (2, 2, 2, 2, 2, values.shape[-2] // 32, values.shape[-1]))


def split(values, dims, bit):
    axis, mask = BITS[bit]
    mine = (lax.axis_index(axis) // mask) % 2
    at = values.ndim - 2 - len(dims) + dims.index(bit)
    send = lax.dynamic_index_in_dim(values, 1 - mine, at, keepdims=False)
    keep = lax.dynamic_index_in_dim(values, mine, at, keepdims=False)
    return send, keep, dims.replace(bit, "")


def hop(values, bit):
    axis, mask = BITS[bit]
    count = lax.axis_size(axis)
    return lax.ppermute(values, axis, [(i, i ^ mask) for i in range(count)])


def add(keep, got):
    return keep.astype(F32) + got.astype(F32)


def after(values, *others):
    return lax.optimization_barrier((values,) + others)[0]


def reduce_rest(values, dims, order):
    for bit in order:
        send, keep, dims = split(values.astype(BF16), dims, bit)
        values = add(keep, hop(send, bit))
    return values


def scatter_rows(values):
    return lax.psum_scatter(values, ("batch", "seq"), scatter_dimension=0, tiled=True).astype(F32)


def sum_and_gather(common, sliced):
    seq_count, batch_count = lax.axis_size("seq"), lax.axis_size("batch")
    rows, cols = sliced.shape
    mine = cols // (seq_count * batch_count)
    parts = sliced.reshape(rows, batch_count, seq_count, mine).transpose(2, 1, 0, 3).reshape(seq_count, -1)
    flat = common.reshape(1, -1)
    whole = jnp.concatenate([jnp.broadcast_to(flat, (seq_count, flat.shape[1])), parts], axis=1)
    pad = -whole.shape[1] % 1024
    whole = jnp.pad(whole, ((0, 0), (0, pad))).reshape(seq_count, -1, 128)
    summed = jnp.sum(swap(whole), axis=0)
    gathered = lax.all_gather(summed, "batch", axis=0).reshape(batch_count, -1)
    common_all = gathered[:, : flat.shape[1]].reshape((batch_count,) + common.shape)
    parts_all = jnp.sum(gathered[:, flat.shape[1] : flat.shape[1] + parts.shape[1]], axis=0)
    own = lax.dynamic_index_in_dim(
        parts_all.reshape(batch_count, rows, mine), lax.axis_index("batch"), 0, keepdims=False
    )
    return common_all, own


def attend_plain(mixed, weight, ok, heads):
    wide = heads * HEAD_DIM
    triple = mm(mixed, weight).astype(BF16)
    split = lambda k: triple[:, k * wide : (k + 1) * wide].reshape(-1, heads, HEAD_DIM)
    queries, keys, values = split(0), split(1), split(2)
    scores = jnp.einsum("qhe,khe->hqk", queries, keys, preferred_element_type=F32) * FACTOR
    scores = jnp.where(ok[None, None, :], scores, -1e30)
    prob = jax.nn.softmax(scores, axis=-1)
    out = jnp.einsum("hqk,khe->qhe", prob.astype(BF16), values, preferred_element_type=F32)
    return out.reshape(-1, wide).astype(BF16), (queries, keys, values, prob)


def attend_plain_back(saved, grad, weight):
    queries, keys, values, prob = saved
    heads = queries.shape[1]
    grad = grad.reshape(-1, heads, HEAD_DIM)
    grad_prob = jnp.einsum("qhe,khe->hqk", grad, values, preferred_element_type=F32)
    delta = jnp.sum(prob * grad_prob, axis=-1, keepdims=True)
    grad_scores = (prob * (grad_prob - delta)).astype(BF16)
    dq = jnp.einsum("hqk,khe->qhe", grad_scores, keys, preferred_element_type=F32) * FACTOR
    dk = jnp.einsum("hqk,qhe->khe", grad_scores, queries, preferred_element_type=F32) * FACTOR
    dv = jnp.einsum("hqk,qhe->khe", prob.astype(BF16), grad, preferred_element_type=F32)
    flat = lambda v: v.reshape(v.shape[0], -1).astype(BF16)
    grads = jnp.concatenate([flat(dq), flat(dk), flat(dv)], axis=1)
    return grads, mm(grads, weight, NT)


def shards(
    tokens,
    cotangent,
    timestep,
    class_ids,
    heights,
    widths,
    time_weight,
    class_table,
    ada_weight,
    ada_bias,
    conv_attn,
    qkv_weight,
    proj_weight,
    up_weight,
    conv_ffn,
    down_weight,
):
    latents, rows_here, cols, _ = tokens.shape
    half = cols // 2
    seq_count = lax.axis_size("seq")
    seq_place = lax.axis_index("seq")
    batch_count = lax.axis_size("batch")
    batch_place = lax.axis_index("batch")
    devices = batch_count * seq_count
    blocks = latents * 4
    share = seq_count // blocks
    per_group = rows_here // 2 * half
    group_tokens = seq_count * per_group

    first, last = tokens[:, :1], tokens[:, rows_here - 1 :]
    top = from_before(last, "seq")
    bot = from_after(first, "seq")
    top_two = from_before(tokens[:, rows_here - 2 : rows_here - 1], "seq")
    bot_two = from_after(tokens[:, 1:2], "seq")
    cot_top = from_before(cotangent[:, rows_here - 1 :], "seq")
    cot_bot = from_after(cotangent[:, :1], "seq")

    half_freq = time_weight.shape[0] // 2
    frequency = jnp.exp(-math.log(10000.0) * jnp.arange(half_freq, dtype=F32) / half_freq)
    angles = timestep.astype(F32)[:, None] * frequency[None, :]
    embedding = jnp.concatenate([jnp.cos(angles), jnp.sin(angles)], axis=1).astype(BF16)
    one_hot = (
        class_ids[:, None] == jnp.arange(class_table.shape[0], dtype=jnp.int32)[None, :]
    ).astype(BF16)
    condition = mm(embedding, time_weight) + mm(one_hot, class_table)
    logistic = jax.nn.sigmoid(condition)
    activated_cond = (condition * logistic).astype(BF16)
    pieces = (mm(activated_cond, ada_weight) + ada_bias).reshape(latents, 6, D)
    meta = jnp.concatenate(
        [heights, widths, jnp.reshape(seq_place * rows_here, (1,))]
    ).astype(jnp.int32)
    kern_attn = conv_attn.astype(F32)
    core = jnp.reshape(batch_place % 2, (1,)).astype(jnp.int32)

    mixed = enter(meta, tokens, top, bot, pieces, kern_attn)
    sent = mixed.reshape(blocks, 1, per_group, D)
    sent = jnp.broadcast_to(sent, (blocks, share, per_group, D)).reshape(seq_count, per_group, D)
    grouped = swap(sent).reshape(group_tokens, D)

    my_block = seq_place // share
    my_latent = my_block // 4
    my_a = (my_block // 2) % 2
    my_b = my_block % 2
    places = jnp.arange(group_tokens, dtype=jnp.int32)
    key_row = places // half * 2 + my_a
    key_col = places % half * 2 + my_b
    height = lax.dynamic_index_in_dim(heights, my_latent, 0, keepdims=False)
    width = lax.dynamic_index_in_dim(widths, my_latent, 0, keepdims=False)
    key_ok = (key_row < height) & (key_col < width)

    margin = half
    window = per_group + 2 * margin
    if share == 1:
        bias = jnp.broadcast_to(jnp.where(key_ok, 0.0, -1e30)[:, None], (group_tokens, 128))
        weight_t = qkv_weight.T
        windows, lse = attend(grouped, qkv_weight, weight_t, bias, seq_count, window)
        attended = swap(windows)
    else:
        heads = HEADS // share
        wide = heads * HEAD_DIM
        chunk = seq_place % share
        thirds = qkv_weight.reshape(D, 3, share, wide)
        my_weight = lax.dynamic_index_in_dim(thirds, chunk, 2, keepdims=False).reshape(D, 3 * wide)
        att, saved = attend_plain(grouped, my_weight, key_ok, heads)
        att = jnp.pad(att, ((margin, margin), (0, 0)))
        windows = jnp.stack(
            [att[s * per_group : s * per_group + window] for s in range(seq_count)]
        )
        attended = swap(windows).reshape(blocks, share, window, wide)
        attended = attended.transpose(0, 2, 1, 3).reshape(blocks, window, D)

    ge, get, cot_split = prepare_cot(meta, cotangent, cot_top, cot_bot, pieces)
    conditions = lax.all_gather(
        jnp.concatenate([condition, embedding.astype(F32), class_ids.astype(F32)[:, None]], axis=1),
        "batch",
        axis=0,
    )
    if share == 1:
        triple = mm(grouped, qkv_weight).astype(BF16)
        key_t = mm(weight_t[D : 2 * D], grouped, NT).astype(BF16)
        attended, ge, triple, key_t, conditions = lax.optimization_barrier(
            (attended, ge, triple, key_t, conditions)
        )
    e2, e2t, after_attn, branch = second(
        meta, attended, tokens, (top, top_two), (bot, bot_two), pieces, proj_weight
    )
    expanded, grad_e2, send_c, keep_c, conv_ffn_part = ffn(
        core, e2, e2t, ge, get, up_weight, down_weight, conv_ffn, cols
    )
    halving = batch_count == 4 and seq_count == 8
    if halving:
        got_c = hop(send_c, "c")
    output, grad_after, grad_branch, grad_attended, mid_sums = middle(
        meta, expanded, grad_e2, after_attn, branch, cot_split, pieces, proj_weight, rows_here, cols
    )

    att_own = attended[:, margin : margin + per_group].reshape(blocks * per_group, D)
    flat_branch = grad_branch.reshape(blocks * per_group, D)
    proj_grad = mm(att_own, flat_branch, (((0,), (0,)), ((), ()))).astype(BF16)
    hidden = conv_ffn.shape[1]
    own_hidden = hidden // devices
    side = conv_ffn_part.reshape(9, devices, own_hidden).transpose(1, 0, 2).reshape(devices, -1)
    side_rows = D // devices
    side_cols = -(-9 * own_hidden // (128 * side_rows)) * 128
    side = jnp.pad(side, ((0, 0), (0, side_rows * side_cols - 9 * own_hidden)))
    side = side.reshape(D, side_cols).astype(BF16)
    tall = per_group + margin
    if share == 1:
        gatt = swap(grad_attended.reshape(seq_count, per_group, D)).reshape(group_tokens, D)
        if halving:
            keep_c = after(keep_c, grad_attended)
            sums = add(keep_c, got_c).astype(BF16).reshape(2, 2, 2, 2, 2, D // devices, hidden)
            send_a, keep_a, dims_a = split(sums[0], "yhlx", "y")
            send_b, keep_b, dims_b = split(sums[1], "yhlx", "x")
            gatt, send_a, send_b = lax.optimization_barrier((gatt, send_a, send_b))
            got_a, got_b = hop(send_a, "y"), hop(send_b, "x")
        offset = jnp.reshape(margin * (1 - my_a), (1,)).astype(jnp.int32)
        dq, dk, dv, gm_windows = attend_back(
            offset, triple, key_t, bias, lse, gatt, qkv_weight, seq_count, tall
        )
        gm = swap(gm_windows)
        turned = (((0,), (0,)), ((), ()))
        rest_one = mm(grouped, jnp.concatenate([dq, dk], axis=1), turned).astype(BF16)
        rest_two = jnp.concatenate([mm(grouped, dv, turned).astype(BF16), proj_grad, side], axis=1)
    else:
        sent = grad_attended.reshape(blocks, per_group, share, wide).transpose(0, 2, 1, 3)
        gatt = swap(sent.reshape(seq_count, per_group, wide)).reshape(group_tokens, wide)
        grad_triple, gm_part = attend_plain_back(saved, gatt, my_weight)
        base = jnp.pad(gm_part.astype(BF16), ((margin, margin), (0, 0)))
        base = lax.dynamic_slice_in_dim(base, margin * (1 - my_a), group_tokens + margin)
        gm_windows = jnp.stack(
            [base[s * per_group : s * per_group + tall] for s in range(seq_count)]
        )
        gm = swap(gm_windows).reshape(blocks, share, tall, D)
        gm = jnp.sum(gm.astype(F32), axis=1).astype(BF16)
        own_grad = mm(grouped, grad_triple, (((0,), (0,)), ((), ()))).astype(BF16)
        spread = jnp.zeros((D, 3, share, wide), BF16)
        qkv_grad = lax.dynamic_update_index_in_dim(
            spread, own_grad.reshape(D, 3, wide), chunk, 2
        ).reshape(D, 3 * D)
        rest_one = qkv_grad[:, : 2 * D]
        rest_two = jnp.concatenate([qkv_grad[:, 2 * D :], proj_grad, side], axis=1)

    if halving:
        keep_a, keep_b = after(keep_a, gm_windows), after(keep_b, gm_windows)
        send_a, keep_a, dims_a = split(add(keep_a, got_a).astype(BF16), dims_a, "x")
        send_b, keep_b, dims_b = split(add(keep_b, got_b).astype(BF16), dims_b, "y")
        got_a, got_b = hop(send_a, "x"), hop(send_b, "y")
        send_one, keep_one, dims_one = split(blocks_of(rest_one), ORDER, "c")
        send_two, keep_two, dims_two = split(blocks_of(rest_two), ORDER, "c")
        got_one, got_two = hop(send_one, "c"), hop(send_two, "c")
        send_one, keep_one, dims_one = split(add(keep_one, got_one).astype(BF16), dims_one, "y")
        send_two, keep_two, dims_two = split(add(keep_two, got_two).astype(BF16), dims_two, "x")
        got_one, got_two = hop(send_one, "y"), hop(send_two, "x")
    total = batch_count * latents

    here = batch_place * seq_count + seq_place
    own_cols = D // devices
    conditions = conditions.reshape(total, -1)
    condition_all = conditions[:, :D]
    embedding_all = conditions[:, D : D + embedding.shape[1]]
    ids_all = conditions[:, -1].astype(jnp.int32)
    logistic_all = jax.nn.sigmoid(condition_all)
    activated_all = (condition_all * logistic_all).astype(BF16).astype(F32)
    slope_all = logistic_all * (1.0 + condition_all * (1.0 - logistic_all))

    def back_through(grads):
        high = lax.reduce_precision(grads, 8, 7)
        middle_term = lax.reduce_precision(grads - high, 8, 7)
        low = grads - high - middle_term
        product = mm(jnp.concatenate([high, middle_term, low]).astype(BF16), ada_weight, NT)
        return product[:total] + product[total : 2 * total] + product[2 * total :]

    token_grad, conv_attn_part, end_sums = leave(
        meta, gm, tokens, top, bot, grad_after, pieces, kern_attn
    )

    all_sums, conv_attn_grad = sum_and_gather(
        jnp.concatenate([end_sums, mid_sums], axis=1), jnp.sum(conv_attn_part, axis=0)
    )
    if halving:
        pair = jnp.stack([add(keep_a, got_a), add(keep_b, got_b)])
        pair = reduce_rest(pair, dims_a, "lh")
        down_rows, up_rows = pair[0], pair[1]
        send_one, keep_one, dims_one = split(add(keep_one, got_one).astype(BF16), dims_one, "x")
        send_two, keep_two, dims_two = split(add(keep_two, got_two).astype(BF16), dims_two, "y")
        got_one, got_two = hop(send_one, "x"), hop(send_two, "y")
        rest_rows = jnp.concatenate([add(keep_one, got_one), add(keep_two, got_two)], axis=-1)
        rest_rows = reduce_rest(rest_rows, dims_one, "lh")
    else:
        whole = jnp.stack([keep_c, send_c])
        whole = jnp.where(core[0] == 0, whole, whole[::-1]).transpose(1, 2, 0, 3, 4)
        whole = whole.reshape(2, D, hidden)
        down_rows, up_rows = scatter_rows(whole[0]), scatter_rows(whole[1])
        rest_rows = scatter_rows(jnp.concatenate([rest_one, rest_two], axis=1))
    qkv_rows = rest_rows[:, : 3 * D]
    proj_rows = rest_rows[:, 3 * D : 4 * D]
    conv_ffn_grad = rest_rows[:, 4 * D :].reshape(-1)[: 9 * own_hidden].reshape(9, own_hidden)

    grad_pieces = all_sums.reshape(total, 6 * D)
    grad_silu = back_through(grad_pieces)
    cond_all = grad_silu * slope_all
    cond_grad = lax.dynamic_slice_in_dim(cond_all, batch_place * latents, latents)
    cond_cols = lax.dynamic_slice_in_dim(cond_all, here * own_cols, own_cols, axis=1)
    act_cols = lax.dynamic_slice_in_dim(activated_all, here * own_cols, own_cols, axis=1)
    outer = lambda left, right: lax.dot_general(
        left, right, (((0,), (0,)), ((), ())), precision=HIGHEST, preferred_element_type=F32
    )
    hot_all = (ids_all[:, None] == jnp.arange(class_table.shape[0], dtype=jnp.int32)[None, :]).astype(F32)
    bias_cols = 6 * D // devices
    bias_grad = jnp.sum(
        lax.dynamic_slice_in_dim(grad_pieces, here * bias_cols, bias_cols, axis=1), axis=0
    )
    return (
        output,
        token_grad,
        cond_grad,
        outer(embedding_all, cond_cols),
        outer(hot_all, cond_cols),
        outer(act_cols, grad_pieces),
        bias_grad,
        conv_attn_grad,
        qkv_rows,
        proj_rows,
        up_rows,
        conv_ffn_grad,
        down_rows.T,
    )


def solution(mesh):
    strips = P("batch", "seq", None, None)
    in_specs = (strips, strips) + (P("batch"),) * 4 + (P(),) * 10
    both = ("batch", "seq")
    out_specs = (
        strips,
        strips,
        P("batch", None),
        P(None, both),
        P(None, both),
        P(both, None),
        P(both),
        P(None, both),
        P(both, None),
        P(both, None),
        P(both, None),
        P(None, both),
        P(None, both),
    )
    return jax.shard_map(shards, mesh=mesh, in_specs=in_specs, out_specs=out_specs, check_vma=False)
```

```python
import functools
import math

import jax
import jax.numpy as jnp
from jax import lax
from jax.experimental import pallas as pl
from jax.experimental.pallas import tpu as pltpu
from jax.sharding import PartitionSpec as P

D = 768
HEADS = 12
HEAD_DIM = 64
PAIR = 2 * HEAD_DIM
PAIRS = HEADS // 2
FF_BLOCK = 256
LANE_PARTS = D // 128
FACTOR = HEAD_DIM ** (-0.5)

F32 = jnp.float32
BF16 = jnp.bfloat16
HIGHEST = lax.Precision.HIGHEST
NN = (((1,), (0,)), ((), ()))
NT = (((1,), (1,)), ((), ()))
VMEM_LIMIT = 60 * 1024 * 1024


def mm(left, right, dims=NN):
    return lax.dot_general(left, right, dims, preferred_element_type=F32)


def shift_down(values):
    rows = lax.broadcasted_iota(jnp.int32, values.shape, 0)
    return jnp.where(rows == 0, 0.0, pltpu.roll(values, 1, 0))


def shift_up(values):
    count = values.shape[0]
    rows = lax.broadcasted_iota(jnp.int32, values.shape, 0)
    return jnp.where(rows == count - 1, 0.0, pltpu.roll(values, count - 1, 0))


def put_shifts(ref, row, parity, values):
    ref[row, 1 + parity] = values
    if parity == 0:
        ref[row, 3] = shift_up(values)
    else:
        ref[row, 0] = shift_down(values)


def normalize(values):
    centre = values - jnp.mean(values, axis=-1, keepdims=True)
    spread = jnp.mean(centre * centre, axis=-1, keepdims=True)
    scaled = lax.rsqrt(spread + 1e-06)
    return centre * scaled, scaled


def norm_back(grad_norm, normed, scaled):
    return scaled * (
        grad_norm
        - jnp.mean(grad_norm, axis=-1, keepdims=True)
        - normed * jnp.mean(grad_norm * normed, axis=-1, keepdims=True)
    )


def put_row(buf, row, values):
    for k in range(LANE_PARTS):
        buf[row, k] = values[:, 128 * k : 128 * (k + 1)]


def get_row(buf, row):
    return jnp.concatenate([buf[row, k] for k in range(LANE_PARTS)], axis=1)


def put_columns(buf, row, parity, values):
    for k in range(LANE_PARTS):
        buf[row, k, pl.ds(parity, values.shape[0], stride=2), :] = values[:, 128 * k : 128 * (k + 1)]


def get_columns(buf, row, parity):
    half = buf.shape[2] // 2
    return jnp.concatenate(
        [buf[row, k, pl.ds(parity, half, stride=2), :] for k in range(LANE_PARTS)], axis=1
    )


def usable_of(meta, latents, latent, row, parity, half):
    cols = 2 * lax.broadcasted_iota(jnp.int32, (half, 1), 0) + parity
    row_ok = jnp.logical_and(row >= 0, row < meta[latent])
    limit = jnp.where(row_ok, meta[latents + latent], 0)
    return (cols < limit).astype(F32)


def sum8(values):
    total = values[0:8]
    for start in range(8, values.shape[0], 8):
        total = total + values[start : start + 8]
    return total


def enter_kernel(meta, tok, top, bot, pieces, kern, out, buf, ent):
    latents = pl.num_programs(0)
    latent = pl.program_id(0)
    rows_here, cols = tok.shape[1], tok.shape[2]
    half = cols // 2
    row0 = meta[2 * latents]
    shift = pieces[0, 0:1, :]
    scale = 1.0 + pieces[0, 1:2, :]
    for rr in range(rows_here + 2):
        source = top[0, 0] if rr == 0 else bot[0, 0] if rr == rows_here + 1 else tok[0, rr - 1]
        put_row(buf, rr, source.astype(F32))
        for parity in range(2):
            normed, _ = normalize(get_columns(buf, rr, parity))
            ok = usable_of(meta, latents, latent, row0 + rr - 1, parity, half)
            put_shifts(ent, rr, parity, ((normed * scale + shift) * ok).astype(BF16).astype(F32))
    for row in range(rows_here):
        for parity in range(2):
            total = jnp.zeros((half, D), F32)
            for i in range(3):
                for j in range(3):
                    tap = 3 * i + j
                    total = total + ent[row + i, parity + j] * kern[tap : tap + 1, :]
            mixed = (ent[row + 1, 1 + parity] + total).astype(BF16)
            group = 2 * (row % 2) + parity
            out[0, group, (row // 2) * half : (row // 2 + 1) * half, :] = mixed


def enter(meta, tokens, top, bot, pieces, kern):
    latents, rows_here, cols, _ = tokens.shape
    half = cols // 2
    per_group = rows_here // 2 * half
    whole = lambda *shape: pl.BlockSpec(shape, lambda l, m: (l,) + (0,) * (len(shape) - 1))
    return pl.pallas_call(
        enter_kernel,
        out_shape=jax.ShapeDtypeStruct((latents, 4, per_group, D), BF16),
        grid_spec=pltpu.PrefetchScalarGridSpec(
            num_scalar_prefetch=1,
            grid=(latents,),
            in_specs=[
                whole(1, rows_here, cols, D),
                whole(1, 1, cols, D),
                whole(1, 1, cols, D),
                whole(1, 6, D),
                pl.BlockSpec((9, D), lambda l, m: (0, 0)),
            ],
            out_specs=whole(1, 4, per_group, D),
            scratch_shapes=[
                pltpu.VMEM((rows_here + 2, LANE_PARTS, cols, 128), F32),
                pltpu.VMEM((rows_here + 2, 4, half, D), F32),
            ],
        ),
        compiler_params=pltpu.CompilerParams(vmem_limit_bytes=VMEM_LIMIT),
        cost_estimate=pl.CostEstimate(flops=6_000_000_000, bytes_accessed=4_000_000, transcendentals=0),
        name="enter",
    )(meta, tokens, top, bot, pieces, kern)


def cot_kernel(meta, cot, top, bot, pieces, ge_out, get_out, cot_out, buf):
    rows_here, cols = cot.shape[1], cot.shape[2]
    half = cols // 2
    gate = pieces[0, 5:6, :]
    for rr in range(rows_here + 2):
        source = top[0, 0] if rr == 0 else bot[0, 0] if rr == rows_here + 1 else cot[0, rr - 1]
        put_row(buf, rr, source.astype(F32))
        for parity in range(2):
            values = get_columns(buf, rr, parity)
            scaled = (gate * values).astype(BF16)
            at = (2 * rr + parity) * half
            ge_out[0, at : at + half, :] = scaled
            if 1 <= rr <= rows_here:
                cot_out[0, at - cols : at - cols + half, :] = values.astype(BF16)
    inner = ge_out[0, cols : cols + rows_here * cols, :].astype(F32)
    get_out[0] = inner.T.astype(BF16)


def prepare_cot(meta, cotangent, top, bot, pieces):
    latents, rows_here, cols, _ = cotangent.shape
    whole = lambda *shape: pl.BlockSpec(shape, lambda l, m: (l,) + (0,) * (len(shape) - 1))
    own = rows_here * cols
    return pl.pallas_call(
        cot_kernel,
        out_shape=(
            jax.ShapeDtypeStruct((latents, own + 2 * cols, D), BF16),
            jax.ShapeDtypeStruct((latents, D, own), BF16),
            jax.ShapeDtypeStruct((latents, own, D), BF16),
        ),
        grid_spec=pltpu.PrefetchScalarGridSpec(
            num_scalar_prefetch=1,
            grid=(latents,),
            in_specs=[
                whole(1, rows_here, cols, D),
                whole(1, 1, cols, D),
                whole(1, 1, cols, D),
                whole(1, 6, D),
            ],
            out_specs=(whole(1, own + 2 * cols, D), whole(1, D, own), whole(1, own, D)),
            scratch_shapes=[pltpu.VMEM((rows_here + 2, LANE_PARTS, cols, 128), F32)],
        ),
        compiler_params=pltpu.CompilerParams(vmem_limit_bytes=VMEM_LIMIT),
        cost_estimate=pl.CostEstimate(flops=4_000_000_000, bytes_accessed=4_000_000, transcendentals=0),
        name="prepare_cot",
    )(meta, cotangent, top, bot, pieces)


def second_kernel(meta, att, tok, top2, top1, bot1, bot2, pieces, proj, e2_out, e2t_out, after_out, branch_out, buf, bran):
    latents = pl.num_programs(0)
    latent = pl.program_id(0)
    rows_here, cols = tok.shape[1], tok.shape[2]
    half = cols // 2
    row0 = meta[2 * latents]
    gate = pieces[0, 2:3, :]
    shift = pieces[0, 3:4, :]
    scale = 1.0 + pieces[0, 4:5, :]
    for group in range(4):
        bran[group] = mm(att[group], proj[...])
    for rr in range(rows_here + 4):
        at_row = rr - 2
        source = (
            top2[0, 0]
            if at_row == -2
            else top1[0, 0]
            if at_row == -1
            else bot1[0, 0]
            if at_row == rows_here
            else bot2[0, 0]
            if at_row == rows_here + 1
            else tok[0, at_row]
        )
        put_row(buf, rr, source.astype(F32))
        for parity in range(2):
            group = 2 * (rr % 2) + parity
            branch = bran[group, (rr // 2) * half : (rr // 2 + 1) * half, :]
            after = get_columns(buf, rr, parity) + gate * branch
            normed, _ = normalize(after)
            ok = usable_of(meta, latents, latent, row0 + at_row, parity, half)
            at = (2 * rr + parity) * half
            e2_out[0, at : at + half, :] = ((normed * scale + shift) * ok).astype(BF16)
            if 0 <= at_row < rows_here:
                own = at - 2 * cols
                after_out[0, own : own + half, :] = after
                branch_out[0, own : own + half, :] = branch
    inner = e2_out[0, 2 * cols : 2 * cols + rows_here * cols, :].astype(F32)
    e2t_out[0] = inner.T.astype(BF16)


def second(meta, attended, tokens, tops, bots, pieces, proj):
    latents, rows_here, cols, _ = tokens.shape
    half = cols // 2
    own = rows_here * cols
    wide = attended.shape[1]
    whole = lambda *shape: pl.BlockSpec(shape, lambda l, m: (l,) + (0,) * (len(shape) - 1))
    return pl.pallas_call(
        second_kernel,
        out_shape=(
            jax.ShapeDtypeStruct((latents, own + 4 * cols, D), BF16),
            jax.ShapeDtypeStruct((latents, D, own), BF16),
            jax.ShapeDtypeStruct((latents, own, D), F32),
            jax.ShapeDtypeStruct((latents, own, D), F32),
        ),
        grid_spec=pltpu.PrefetchScalarGridSpec(
            num_scalar_prefetch=1,
            grid=(latents,),
            in_specs=[
                whole(4, wide, D),
                whole(1, rows_here, cols, D),
                whole(1, 1, cols, D),
                whole(1, 1, cols, D),
                whole(1, 1, cols, D),
                whole(1, 1, cols, D),
                whole(1, 6, D),
                pl.BlockSpec((D, D), lambda l, m: (0, 0)),
            ],
            out_specs=(
                whole(1, own + 4 * cols, D),
                whole(1, D, own),
                whole(1, own, D),
                whole(1, own, D),
            ),
            scratch_shapes=[
                pltpu.VMEM((rows_here + 4, LANE_PARTS, cols, 128), F32),
                pltpu.VMEM((4, wide, D), F32),
            ],
        ),
        compiler_params=pltpu.CompilerParams(vmem_limit_bytes=VMEM_LIMIT),
        cost_estimate=pl.CostEstimate(flops=7_000_000_000, bytes_accessed=4_000_000, transcendentals=0),
        name="second",
    )(meta, attended, tokens, tops[1], tops[0], bots[0], bots[1], pieces, proj)


def normal_parts(values):
    density = jnp.exp(-0.5 * values * values) * 0.3989422804014327
    t = 1.0 / (1.0 + 0.2316419 * jnp.abs(values))
    series = t * (
        0.319381530
        + t * (-0.356563782 + t * (1.781477937 + t * (-1.821255978 + t * 1.330274429)))
    )
    tail = density * series
    return jnp.where(values > 0.0, 1.0 - tail, tail), density


def ffn_kernel(core, e2, e2t, ge, get, up, down, kern_in, exp_out, ge2_out, send_out, keep_out, kern_out, *scratch):
    latents = e2.shape[0]
    lifted, gact, gconv, act, graised = [scratch[k * latents : (k + 1) * latents] for k in range(5)]
    down_acc, up_acc = scratch[5 * latents :]
    step = pl.program_id(0)
    half = lifted[0].shape[2]
    rows_here = lifted[0].shape[0] - 4
    block = lifted[0].shape[3]
    taps = [kern_in[t : t + 1, :].astype(F32) for t in range(9)]
    sums = [jnp.zeros((8, block), F32) for _ in range(9)]
    rows_per = 4

    def lift(latent, part):
        size = rows_per * 2 * half
        raised = mm(e2[latent, part * size : (part + 1) * size], up[...])
        raised = raised.astype(BF16).astype(F32)
        for k in range(rows_per):
            for parity in range(2):
                at = (2 * k + parity) * half
                put_shifts(lifted[latent], part * rows_per + k, parity, raised[at : at + half])

    def pull(latent, part):
        size = gact[latent].shape[0] // 2
        at = part * size
        gact[latent][at : at + size] = mm(ge[latent, at : at + size], down[...], NT)

    def bend(latent, rr):
        for parity in range(2):
            total = None
            for i in range(3):
                for j in range(3):
                    term = lifted[latent][rr + i, parity + j] * taps[3 * i + j]
                    total = term if total is None else total + term
            cdf, density = normal_parts(total)
            at = (2 * rr + parity) * half
            if 1 <= rr <= rows_here:
                own = at - 2 * half
                act[latent][own : own + half, :] = (total * cdf).astype(BF16)
            grad = gact[latent][at : at + half, :] * (cdf + total * density)
            put_shifts(gconv[latent], rr, parity, grad.astype(BF16).astype(F32))

    def unbend(latent, row):
        for parity in range(2):
            total = None
            here = gconv[latent][row + 1, 1 + parity]
            for i in range(3):
                for j in range(3):
                    t = 3 * i + j
                    term = gconv[latent][row + 2 - i, parity + 2 - j] * taps[t]
                    total = term if total is None else total + term
                    sums[t] = sums[t] + sum8(lifted[latent][row + 1 + i, parity + j] * here)
            at = (2 * row + parity) * half
            graised[latent][at : at + half, :] = total.astype(BF16)

    def gather(latent, part):
        cut = slice(part * 256, (part + 1) * 256)
        if part == 0:
            exp_out[latent] += mm(act[latent][...], down[...])
        elif part == 1:
            ge2_out[latent] += mm(graised[latent][...], up[...], NT)
        elif part == 2:
            value = mm(get[latent], act[latent][...])
            down_acc[...] = value if latent == 0 else down_acc[...] + value
        else:
            value = mm(e2t[latent], graised[latent][...])
            up_acc[...] = value if latent == 0 else up_acc[...] + value

    @pl.when(step == 0)
    def _():
        exp_out[...] = jnp.zeros_like(exp_out)
        ge2_out[...] = jnp.zeros_like(ge2_out)

    lifts = (rows_here + 4) // rows_per
    for part in range(lifts):
        lift(0, part)
    for part in range(2):
        pull(0, part)
    for latent in range(latents):
        more = []
        if latent + 1 < latents:
            more += [functools.partial(lift, latent + 1, part) for part in range(lifts)]
            more += [functools.partial(pull, latent + 1, part) for part in range(2)]
        if latent > 0:
            more += [functools.partial(gather, latent - 1, part) for part in range(4)]
        work = [functools.partial(bend, latent, rr) for rr in range(rows_here + 2)]
        work += [functools.partial(unbend, latent, row) for row in range(rows_here)]
        for k, unit in enumerate(work):
            if k < len(more):
                more[k]()
            unit()
        for unit in more[len(work) :]:
            unit()
    for part in range(4):
        gather(latents - 1, part)

    size = down_acc.shape[0] // 4
    for which, acc in enumerate((down_acc, up_acc)):
        for y in range(2):
            mine = pl.multiple_of((2 * y + core[0]) * size, 8)
            other = pl.multiple_of((2 * y + 1 - core[0]) * size, 8)
            keep_out[which, y] = acc[pl.ds(mine, size), :].astype(BF16)
            send_out[which, y] = acc[pl.ds(other, size), :].astype(BF16)
    for t in range(9):
        kern_out[t : t + 1, :] = jnp.sum(sums[t], axis=0, keepdims=True)


def ffn(core, e2, e2t, ge, get, up, down, kern, cols):
    latents = e2.shape[0]
    half = cols // 2
    own = e2t.shape[2]
    rows_here = own // cols
    hidden = up.shape[1]
    fixed = lambda *shape: pl.BlockSpec(shape, lambda f, c: (0,) * len(shape))
    parts = jax.ShapeDtypeStruct((2, 2, D // 4, hidden), BF16)
    parts_spec = pl.BlockSpec((2, 2, D // 4, FF_BLOCK), lambda f, c: (0, 0, 0, f))
    each = lambda *args: [pltpu.VMEM(*args)] * latents
    return pl.pallas_call(
        ffn_kernel,
        out_shape=(
            jax.ShapeDtypeStruct((latents, own, D), F32),
            jax.ShapeDtypeStruct((latents, own, D), F32),
            parts,
            parts,
            jax.ShapeDtypeStruct((9, hidden), F32),
        ),
        grid_spec=pltpu.PrefetchScalarGridSpec(
            num_scalar_prefetch=1,
            grid=(hidden // FF_BLOCK,),
            in_specs=[
                fixed(latents, own + 4 * cols, D),
                fixed(latents, D, own),
                fixed(latents, own + 2 * cols, D),
                fixed(latents, D, own),
                pl.BlockSpec((D, FF_BLOCK), lambda f, c: (0, f)),
                pl.BlockSpec((FF_BLOCK, D), lambda f, c: (f, 0)),
                pl.BlockSpec((9, FF_BLOCK), lambda f, c: (0, f)),
            ],
            out_specs=(
                fixed(latents, own, D),
                fixed(latents, own, D),
                parts_spec,
                parts_spec,
                pl.BlockSpec((9, FF_BLOCK), lambda f, c: (0, f)),
            ),
            scratch_shapes=each((rows_here + 4, 4, half, FF_BLOCK), F32)
            + each((own + 2 * cols, FF_BLOCK), F32)
            + each((rows_here + 2, 4, half, FF_BLOCK), F32)
            + each((own, FF_BLOCK), BF16)
            + each((own, FF_BLOCK), BF16)
            + [pltpu.VMEM((D, FF_BLOCK), F32), pltpu.VMEM((D, FF_BLOCK), F32)],
        ),
        compiler_params=pltpu.CompilerParams(vmem_limit_bytes=VMEM_LIMIT),
        cost_estimate=pl.CostEstimate(flops=48_000_000_000, bytes_accessed=4_000_000, transcendentals=0),
        name="ffn",
    )(core, e2, e2t, ge, get, up, down, kern)


def middle_kernel(meta, exp, ge2, after_in, branch_in, cot_in, pieces, proj, out, after_grad, gb_out, gatt_out, sums_out, buf):
    latents = pl.num_programs(0)
    latent = pl.program_id(0)
    rows_here, cols = out.shape[1], out.shape[2]
    half = cols // 2
    row0 = meta[2 * latents]
    gate_one = pieces[0, 2:3, :]
    scale = 1.0 + pieces[0, 4:5, :]
    gate_two = pieces[0, 5:6, :]
    sums = [jnp.zeros((8, D), F32) for _ in range(4)]
    for row in range(rows_here):
        for parity in range(2):
            at = (2 * row + parity) * half
            part = pl.ds(at, half)
            after = after_in[0, part, :]
            cot = cot_in[0, part, :].astype(F32)
            expanded = exp[0, part, :]
            put_columns(buf, row, parity, after + gate_two * expanded)
            normed, scaled = normalize(after)
            ok = usable_of(meta, latents, latent, row0 + row, parity, half)
            grad = ge2[0, part, :] * ok
            grad_after = cot + norm_back(grad * scale, normed, scaled)
            after_grad[0, part, :] = grad_after
            sums[0] = sums[0] + sum8(grad_after * branch_in[0, part, :])
            sums[1] = sums[1] + sum8(grad)
            sums[2] = sums[2] + sum8(grad * normed)
            sums[3] = sums[3] + sum8(cot * expanded)
            group = 2 * (row % 2) + parity
            to = pl.ds((row // 2) * half, half)
            gb_out[0, group, to, :] = (gate_one * grad_after).astype(BF16)
        out[0, row] = get_row(buf, row).astype(BF16)
    for k in range(4):
        sums_out[0, k : k + 1, :] = jnp.sum(sums[k], axis=0, keepdims=True)
    for group in range(4):
        gatt_out[0, group] = mm(gb_out[0, group], proj[...], NT).astype(BF16)


def middle(meta, exp, ge2, after, branch, cot, pieces, proj, rows_here, cols):
    latents, own, _ = exp.shape
    per_group = own // 4
    whole = lambda *shape: pl.BlockSpec(shape, lambda l, m: (l,) + (0,) * (len(shape) - 1))
    return pl.pallas_call(
        middle_kernel,
        out_shape=(
            jax.ShapeDtypeStruct((latents, rows_here, cols, D), BF16),
            jax.ShapeDtypeStruct((latents, own, D), F32),
            jax.ShapeDtypeStruct((latents, 4, per_group, D), BF16),
            jax.ShapeDtypeStruct((latents, 4, per_group, D), BF16),
            jax.ShapeDtypeStruct((latents, 4, D), F32),
        ),
        grid_spec=pltpu.PrefetchScalarGridSpec(
            num_scalar_prefetch=1,
            grid=(latents,),
            in_specs=[
                whole(1, own, D),
                whole(1, own, D),
                whole(1, own, D),
                whole(1, own, D),
                whole(1, own, D),
                whole(1, 6, D),
                pl.BlockSpec((D, D), lambda l, m: (0, 0)),
            ],
            out_specs=(
                whole(1, rows_here, cols, D),
                whole(1, own, D),
                whole(1, 4, per_group, D),
                whole(1, 4, per_group, D),
                whole(1, 4, D),
            ),
            scratch_shapes=[
                pltpu.VMEM((rows_here, LANE_PARTS, cols, 128), F32),
            ],
        ),
        compiler_params=pltpu.CompilerParams(vmem_limit_bytes=VMEM_LIMIT),
        cost_estimate=pl.CostEstimate(flops=10_000_000_000, bytes_accessed=4_000_000, transcendentals=0),
        name="middle",
    )(meta, exp, ge2, after, branch, cot, pieces, proj)


def leave_kernel(meta, gm, tok, top, bot, after_grad, pieces, kern, out, kern_out, sums_out, buf, ent, gmx, obuf):
    latents = pl.num_programs(0)
    latent = pl.program_id(0)
    rows_here, cols = tok.shape[1], tok.shape[2]
    half = cols // 2
    row0 = meta[2 * latents]
    shift = pieces[0, 0:1, :]
    scale = 1.0 + pieces[0, 1:2, :]
    taps = [kern[t : t + 1, :] for t in range(9)]
    for rr in range(rows_here + 2):
        source = top[0, 0] if rr == 0 else bot[0, 0] if rr == rows_here + 1 else tok[0, rr - 1]
        put_row(buf, rr, source.astype(F32))
        for parity in range(2):
            normed, _ = normalize(get_columns(buf, rr, parity))
            ok = usable_of(meta, latents, latent, row0 + rr - 1, parity, half)
            put_shifts(ent, rr, parity, ((normed * scale + shift) * ok).astype(BF16).astype(F32))
            group = 2 * ((rr + 1) % 2) + parity
            at = (rr // 2) * half
            put_shifts(gmx, rr, parity, gm[group, at : at + half, :].astype(F32))
    sums = [jnp.zeros((8, D), F32) for _ in range(2)]
    tap_sums = [jnp.zeros((8, D), F32) for _ in range(9)]
    for row in range(rows_here):
        for parity in range(2):
            here = gmx[row + 1, 1 + parity]
            total = here
            for i in range(3):
                for j in range(3):
                    t = 3 * i + j
                    total = total + gmx[row + 2 - i, parity + 2 - j] * taps[t]
                    tap_sums[t] = tap_sums[t] + sum8(ent[row + i, parity + j] * here)
            ok = usable_of(meta, latents, latent, row0 + row, parity, half)
            grad = total * ok
            normed, scaled = normalize(get_columns(buf, row + 1, parity))
            sums[0] = sums[0] + sum8(grad)
            sums[1] = sums[1] + sum8(grad * normed)
            at = (2 * row + parity) * half
            back = after_grad[0, at : at + half, :] + norm_back(grad * scale, normed, scaled)
            put_columns(obuf, row, parity, back)
        out[0, row] = get_row(obuf, row)
    for k in range(2):
        sums_out[0, k : k + 1, :] = jnp.sum(sums[k], axis=0, keepdims=True)
    for t in range(9):
        kern_out[0, t : t + 1, :] = jnp.sum(tap_sums[t], axis=0, keepdims=True)


def leave(meta, gm, tokens, top, bot, after_grad, pieces, kern):
    latents, rows_here, cols, _ = tokens.shape
    half = cols // 2
    own = rows_here * cols
    wide = gm.shape[1]
    whole = lambda *shape: pl.BlockSpec(shape, lambda l, m: (l,) + (0,) * (len(shape) - 1))
    return pl.pallas_call(
        leave_kernel,
        out_shape=(
            jax.ShapeDtypeStruct((latents, rows_here, cols, D), F32),
            jax.ShapeDtypeStruct((latents, 9, D), F32),
            jax.ShapeDtypeStruct((latents, 2, D), F32),
        ),
        grid_spec=pltpu.PrefetchScalarGridSpec(
            num_scalar_prefetch=1,
            grid=(latents,),
            in_specs=[
                whole(4, wide, D),
                whole(1, rows_here, cols, D),
                whole(1, 1, cols, D),
                whole(1, 1, cols, D),
                whole(1, own, D),
                whole(1, 6, D),
                pl.BlockSpec((9, D), lambda l, m: (0, 0)),
            ],
            out_specs=(whole(1, rows_here, cols, D), whole(1, 9, D), whole(1, 2, D)),
            scratch_shapes=[
                pltpu.VMEM((rows_here + 2, LANE_PARTS, cols, 128), F32),
                pltpu.VMEM((rows_here + 2, 4, half, D), F32),
                pltpu.VMEM((rows_here + 2, 4, half, D), F32),
                pltpu.VMEM((rows_here, LANE_PARTS, cols, 128), F32),
            ],
        ),
        compiler_params=pltpu.CompilerParams(vmem_limit_bytes=VMEM_LIMIT),
        cost_estimate=pl.CostEstimate(flops=10_000_000_000, bytes_accessed=4_000_000, transcendentals=0),
        name="leave",
    )(meta, gm, tokens, top, bot, after_grad, pieces, kern)


def pair_parts(values):
    lanes = lax.broadcasted_iota(jnp.int32, values.shape, 1)
    first = lanes < HEAD_DIM
    zero = jnp.zeros_like(values)
    return jnp.where(first, values, zero), jnp.where(first, zero, values)


def attend_kernel(mixed, wq, wk, wvt, bias, out, lse_out):
    tokens = mixed.shape[0]
    strips, window, _ = out.shape
    step = tokens // strips
    margin = (window - step) // 2
    m = mixed[...]
    query = (mm(m, wq[...]).astype(BF16) * FACTOR).astype(BF16)
    key = mm(m, wk[...]).astype(BF16)
    value_t = mm(wvt[...], m, NT).astype(BF16)
    keep = jnp.tile(bias[...], (1, tokens // 128))
    parts = []
    for e, key_e in enumerate(pair_parts(key)):
        scores = mm(key_e, query, NT) + keep
        peak = jnp.max(scores, axis=0, keepdims=True)
        raw = jnp.exp(scores - peak)
        total = jnp.sum(raw, axis=0, keepdims=True)
        prob = (raw * (1.0 / total)).astype(BF16)
        parts.append(mm(value_t[e * HEAD_DIM : (e + 1) * HEAD_DIM], prob))
        lse_out[0, e : e + 1, :] = peak + jnp.log(total)
    att = jnp.concatenate(parts, axis=0).T.astype(BF16)
    blank = jnp.zeros((margin, PAIR), BF16)
    for s in range(strips):
        low, high = s * step - margin, (s + 1) * step + margin
        if low < 0:
            out[s] = jnp.concatenate([blank, att[:high]], axis=0)
        elif high > tokens:
            out[s] = jnp.concatenate([att[low:], blank], axis=0)
        else:
            out[s] = att[low:high]


def attend(mixed, weight, weight_t, bias, strips, window):
    tokens = mixed.shape[0]
    return pl.pallas_call(
        attend_kernel,
        out_shape=(
            jax.ShapeDtypeStruct((strips, window, D), BF16),
            jax.ShapeDtypeStruct((PAIRS, 2, tokens), F32),
        ),
        grid=(PAIRS,),
        in_specs=[
            pl.BlockSpec((tokens, D), lambda p: (0, 0)),
            pl.BlockSpec((D, PAIR), lambda p: (0, p)),
            pl.BlockSpec((D, PAIR), lambda p: (0, PAIRS + p)),
            pl.BlockSpec((PAIR, D), lambda p: (2 * PAIRS + p, 0)),
            pl.BlockSpec((tokens, 128), lambda p: (0, 0)),
        ],
        out_specs=(
            pl.BlockSpec((strips, window, PAIR), lambda p: (0, 0, p)),
            pl.BlockSpec((1, 2, tokens), lambda p: (p, 0, 0)),
        ),
        compiler_params=pltpu.CompilerParams(vmem_limit_bytes=VMEM_LIMIT),
        cost_estimate=pl.CostEstimate(flops=16_000_000_000, bytes_accessed=4_000_000, transcendentals=0),
        name="attend",
    )(mixed, weight, weight, weight_t, bias)


def attend_back_kernel(offset, query, key, value, key_t, bias, lse, gatt, wq, wk, wv, mixed_t, send_out, keep_out, gm_out, acc, part):
    tokens = query.shape[0]
    strips, window, _ = gm_out.shape
    step = tokens // strips
    margin = window - step
    p = pl.program_id(0)
    q = query[...]
    keep = jnp.tile(bias[...], (1, tokens // 128))
    queries = pair_parts(q)
    keys = pair_parts(key[...])
    values = pair_parts(value[...])
    grads = pair_parts(gatt[...])
    dk = jnp.zeros((tokens, PAIR), F32)
    dv = jnp.zeros((tokens, PAIR), F32)
    parts = []
    for e in range(2):
        scores = mm(keys[e], q, NT) * FACTOR + keep
        prob = jnp.exp(scores - lse[0, e : e + 1, :])
        grad_prob = mm(values[e], gatt[...], NT)
        delta = jnp.sum(prob * grad_prob, axis=0, keepdims=True)
        grad_scores = (prob * (grad_prob - delta)).astype(BF16)
        dv = dv + mm(prob.astype(BF16), grads[e])
        dk = dk + mm(grad_scores, queries[e])
        parts.append(mm(key_t[e * HEAD_DIM : (e + 1) * HEAD_DIM], grad_scores))
    dq = (jnp.concatenate(parts, axis=0).T * FACTOR).astype(BF16)
    dk = (dk * FACTOR).astype(BF16)
    dv = dv.astype(BF16)
    size = D // 4
    for k, grad in enumerate((dq, dk, dv)):
        part[k] = mm(mixed_t[...], grad)
        for y in range(2):
            mine = pl.multiple_of((2 * y + offset[1]) * size, 8)
            other = pl.multiple_of((2 * y + 1 - offset[1]) * size, 8)
            keep_out[k, y] = part[k, pl.ds(mine, size), :].astype(BF16)
            send_out[k, y] = part[k, pl.ds(other, size), :].astype(BF16)
    total = mm(dq, wq[...], NT) + mm(dk, wk[...], NT) + mm(dv, wv[...], NT)

    @pl.when(p == 0)
    def _():
        acc[0:margin] = jnp.zeros((margin, D), F32)
        acc[margin + tokens :] = jnp.zeros((margin, D), F32)
        acc[margin : margin + tokens] = total

    @pl.when(p > 0)
    def _():
        acc[margin : margin + tokens] += total

    @pl.when(p == pl.num_programs(0) - 1)
    def _():
        for s in range(strips):
            start = pl.multiple_of(offset[0] + s * step, 8)
            gm_out[s] = acc[pl.ds(start, window), :].astype(BF16)


def attend_back(offset, triple, key_t, bias, lse, gatt, weight, mixed_t, strips, window):
    tokens = triple.shape[0]
    margin = window - tokens // strips
    part = lambda k: pl.BlockSpec((tokens, PAIR), lambda p, o: (0, k * PAIRS + p))
    slab = lambda k: pl.BlockSpec((D, PAIR), lambda p, o: (0, k * PAIRS + p))
    parts = jax.ShapeDtypeStruct((3, 2, D // 4, D), BF16)
    parts_spec = pl.BlockSpec((3, 2, D // 4, PAIR), lambda p, o: (0, 0, 0, p))
    return pl.pallas_call(
        attend_back_kernel,
        out_shape=(
            parts,
            parts,
            jax.ShapeDtypeStruct((strips, window, D), BF16),
        ),
        grid_spec=pltpu.PrefetchScalarGridSpec(
            num_scalar_prefetch=1,
            grid=(PAIRS,),
            in_specs=[
                part(0),
                part(1),
                part(2),
                pl.BlockSpec((PAIR, tokens), lambda p, o: (p, 0)),
                pl.BlockSpec((tokens, 128), lambda p, o: (0, 0)),
                pl.BlockSpec((1, 2, tokens), lambda p, o: (p, 0, 0)),
                part(0),
                slab(0),
                slab(1),
                slab(2),
                pl.BlockSpec((D, tokens), lambda p, o: (0, 0)),
            ],
            out_specs=(
                parts_spec,
                parts_spec,
                pl.BlockSpec((strips, window, D), lambda p, o: (0, 0, 0)),
            ),
            scratch_shapes=[
                pltpu.VMEM((tokens + 2 * margin, D), F32),
                pltpu.VMEM((3, D, PAIR), F32),
            ],
        ),
        compiler_params=pltpu.CompilerParams(vmem_limit_bytes=VMEM_LIMIT),
        cost_estimate=pl.CostEstimate(flops=23_000_000_000, bytes_accessed=4_000_000, transcendentals=0),
        name="attend_back",
    )(offset, triple, triple, triple, key_t, bias, lse, gatt, weight, weight, weight, mixed_t)


def from_before(values, axis):
    count = lax.axis_size(axis)
    return lax.ppermute(values, axis, [(i, i + 1) for i in range(count - 1)])


def from_after(values, axis):
    count = lax.axis_size(axis)
    return lax.ppermute(values, axis, [(i + 1, i) for i in range(count - 1)])


def swap(values):
    return lax.all_to_all(values, "seq", 0, 0, tiled=False)


BITS = {"y": ("batch", 2), "c": ("batch", 1), "h": ("seq", 4), "l": ("seq", 2), "x": ("seq", 1)}
ORDER = "ychlx"


def blocks_of(values):
    return values.reshape(values.shape[:-2] + (2, 2, 2, 2, 2, values.shape[-2] // 32, values.shape[-1]))


def split(values, dims, bit):
    axis, mask = BITS[bit]
    mine = (lax.axis_index(axis) // mask) % 2
    at = values.ndim - 2 - len(dims) + dims.index(bit)
    send = lax.dynamic_index_in_dim(values, 1 - mine, at, keepdims=False)
    keep = lax.dynamic_index_in_dim(values, mine, at, keepdims=False)
    return send, keep, dims.replace(bit, "")


def hop(values, bit):
    axis, mask = BITS[bit]
    count = lax.axis_size(axis)
    return lax.ppermute(values, axis, [(i, i ^ mask) for i in range(count)])


def add(keep, got):
    return keep.astype(F32) + got.astype(F32)


def after(values, *others):
    return lax.optimization_barrier((values,) + others)[0]


def reduce_rest(values, dims, order):
    for bit in order:
        send, keep, dims = split(values.astype(BF16), dims, bit)
        values = add(keep, hop(send, bit))
    return values


def scatter_rows(values):
    return lax.psum_scatter(values, ("batch", "seq"), scatter_dimension=0, tiled=True).astype(F32)


def sum_and_gather(common, sliced):
    seq_count, batch_count = lax.axis_size("seq"), lax.axis_size("batch")
    batch_place = lax.axis_index("batch")
    flat = common.reshape(1, -1)
    pieces = [jnp.broadcast_to(flat, (seq_count, flat.shape[1]))]
    for values in sliced:
        cut = values.reshape(values.shape[0], batch_count, seq_count, -1).transpose(2, 1, 0, 3)
        pieces.append(cut.reshape(seq_count, -1))
    whole = jnp.concatenate(pieces, axis=1)
    whole = jnp.pad(whole, ((0, 0), (0, -whole.shape[1] % 1024))).reshape(seq_count, -1, 128)
    summed = jnp.sum(swap(whole), axis=0)
    gathered = lax.all_gather(summed, "batch", axis=0).reshape(batch_count, -1)
    common_all = gathered[:, : flat.shape[1]].reshape((batch_count,) + common.shape)
    at = flat.shape[1]
    own = []
    for values, piece in zip(sliced, pieces[1:]):
        part = jnp.sum(gathered[:, at : at + piece.shape[1]], axis=0)
        part = part.reshape(batch_count, values.shape[0], -1)
        own.append(lax.dynamic_index_in_dim(part, batch_place, 0, keepdims=False))
        at += piece.shape[1]
    return common_all, own


def attend_plain(mixed, weight, ok, heads):
    wide = heads * HEAD_DIM
    triple = mm(mixed, weight).astype(BF16)
    split = lambda k: triple[:, k * wide : (k + 1) * wide].reshape(-1, heads, HEAD_DIM)
    queries, keys, values = split(0), split(1), split(2)
    scores = jnp.einsum("qhe,khe->hqk", queries, keys, preferred_element_type=F32) * FACTOR
    scores = jnp.where(ok[None, None, :], scores, -1e30)
    prob = jax.nn.softmax(scores, axis=-1)
    out = jnp.einsum("hqk,khe->qhe", prob.astype(BF16), values, preferred_element_type=F32)
    return out.reshape(-1, wide).astype(BF16), (queries, keys, values, prob)


def attend_plain_back(saved, grad, weight):
    queries, keys, values, prob = saved
    heads = queries.shape[1]
    grad = grad.reshape(-1, heads, HEAD_DIM)
    grad_prob = jnp.einsum("qhe,khe->hqk", grad, values, preferred_element_type=F32)
    delta = jnp.sum(prob * grad_prob, axis=-1, keepdims=True)
    grad_scores = (prob * (grad_prob - delta)).astype(BF16)
    dq = jnp.einsum("hqk,khe->qhe", grad_scores, keys, preferred_element_type=F32) * FACTOR
    dk = jnp.einsum("hqk,qhe->khe", grad_scores, queries, preferred_element_type=F32) * FACTOR
    dv = jnp.einsum("hqk,qhe->khe", prob.astype(BF16), grad, preferred_element_type=F32)
    flat = lambda v: v.reshape(v.shape[0], -1).astype(BF16)
    grads = jnp.concatenate([flat(dq), flat(dk), flat(dv)], axis=1)
    return grads, mm(grads, weight, NT)


def shards(
    tokens,
    cotangent,
    timestep,
    class_ids,
    heights,
    widths,
    time_weight,
    class_table,
    ada_weight,
    ada_bias,
    conv_attn,
    qkv_weight,
    proj_weight,
    up_weight,
    conv_ffn,
    down_weight,
):
    latents, rows_here, cols, _ = tokens.shape
    half = cols // 2
    seq_count = lax.axis_size("seq")
    seq_place = lax.axis_index("seq")
    batch_count = lax.axis_size("batch")
    batch_place = lax.axis_index("batch")
    devices = batch_count * seq_count
    blocks = latents * 4
    share = seq_count // blocks
    per_group = rows_here // 2 * half
    group_tokens = seq_count * per_group

    first, last = tokens[:, :1], tokens[:, rows_here - 1 :]
    top = from_before(last, "seq")
    bot = from_after(first, "seq")

    half_freq = time_weight.shape[0] // 2
    frequency = jnp.exp(-math.log(10000.0) * jnp.arange(half_freq, dtype=F32) / half_freq)
    angles = timestep.astype(F32)[:, None] * frequency[None, :]
    embedding = jnp.concatenate([jnp.cos(angles), jnp.sin(angles)], axis=1).astype(BF16)
    one_hot = (
        class_ids[:, None] == jnp.arange(class_table.shape[0], dtype=jnp.int32)[None, :]
    ).astype(BF16)
    condition = mm(embedding, time_weight) + mm(one_hot, class_table)
    logistic = jax.nn.sigmoid(condition)
    activated_cond = (condition * logistic).astype(BF16)
    pieces = (mm(activated_cond, ada_weight) + ada_bias).reshape(latents, 6, D)
    meta = jnp.concatenate(
        [heights, widths, jnp.reshape(seq_place * rows_here, (1,))]
    ).astype(jnp.int32)
    kern_attn = conv_attn.astype(F32)
    core = jnp.reshape(batch_place % 2, (1,)).astype(jnp.int32)

    mixed = enter(meta, tokens, top, bot, pieces, kern_attn)
    sent = mixed.reshape(blocks, 1, per_group, D)
    sent = jnp.broadcast_to(sent, (blocks, share, per_group, D)).reshape(seq_count, per_group, D)
    grouped = swap(sent).reshape(group_tokens, D)

    weight_t = qkv_weight.T
    low_rows = jnp.stack([tokens[:, rows_here - 2 : rows_here - 1], cotangent[:, rows_here - 1 :]])
    high_rows = jnp.stack([tokens[:, 1:2], cotangent[:, :1]])
    low_rows, high_rows, grouped = lax.optimization_barrier((low_rows, high_rows, grouped))
    top_two, cot_top = from_before(low_rows, "seq")
    bot_two, cot_bot = from_after(high_rows, "seq")

    my_block = seq_place // share
    my_latent = my_block // 4
    my_a = (my_block // 2) % 2
    my_b = my_block % 2
    places = jnp.arange(group_tokens, dtype=jnp.int32)
    key_row = places // half * 2 + my_a
    key_col = places % half * 2 + my_b
    height = lax.dynamic_index_in_dim(heights, my_latent, 0, keepdims=False)
    width = lax.dynamic_index_in_dim(widths, my_latent, 0, keepdims=False)
    key_ok = (key_row < height) & (key_col < width)

    margin = half
    window = per_group + 2 * margin
    if share == 1:
        bias = jnp.broadcast_to(jnp.where(key_ok, 0.0, -1e30)[:, None], (group_tokens, 128))
        windows, lse = attend(grouped, qkv_weight, weight_t, bias, seq_count, window)
        windows, top_two, bot_two, cot_top, cot_bot = lax.optimization_barrier(
            (windows, top_two, bot_two, cot_top, cot_bot)
        )
        attended = swap(windows)
    else:
        heads = HEADS // share
        wide = heads * HEAD_DIM
        chunk = seq_place % share
        thirds = qkv_weight.reshape(D, 3, share, wide)
        my_weight = lax.dynamic_index_in_dim(thirds, chunk, 2, keepdims=False).reshape(D, 3 * wide)
        att, saved = attend_plain(grouped, my_weight, key_ok, heads)
        att = jnp.pad(att, ((margin, margin), (0, 0)))
        windows = jnp.stack(
            [att[s * per_group : s * per_group + window] for s in range(seq_count)]
        )
        attended = swap(windows).reshape(blocks, share, window, wide)
        attended = attended.transpose(0, 2, 1, 3).reshape(blocks, window, D)

    ge, get, cot_split = prepare_cot(meta, cotangent, cot_top, cot_bot, pieces)
    conditions = lax.all_gather(
        jnp.concatenate([condition, embedding.astype(F32), class_ids.astype(F32)[:, None]], axis=1),
        "batch",
        axis=0,
    )
    if share == 1:
        triple = mm(grouped, qkv_weight).astype(BF16)
        key_t = mm(weight_t[D : 2 * D], grouped, NT).astype(BF16)
        grouped_t = grouped.T
        attended, ge, triple, key_t, grouped_t, conditions = lax.optimization_barrier(
            (attended, ge, triple, key_t, grouped_t, conditions)
        )
    e2, e2t, after_attn, branch = second(
        meta, attended, tokens, (top, top_two), (bot, bot_two), pieces, proj_weight
    )
    expanded, grad_e2, send_c, keep_c, conv_ffn_part = ffn(
        core, e2, e2t, ge, get, up_weight, down_weight, conv_ffn, cols
    )
    halving = batch_count == 4 and seq_count == 8
    if halving:
        got_c = hop(send_c, "c")
    output, grad_after, grad_branch, grad_attended, mid_sums = middle(
        meta, expanded, grad_e2, after_attn, branch, cot_split, pieces, proj_weight, rows_here, cols
    )

    att_own = after(attended, grad_attended)[:, margin : margin + per_group]
    att_own = att_own.reshape(blocks * per_group, D)
    flat_branch = grad_branch.reshape(blocks * per_group, D)
    hidden = conv_ffn.shape[1]
    tall = per_group + margin
    if share == 1:
        gatt = swap(grad_attended.reshape(seq_count, per_group, D)).reshape(group_tokens, D)
        if halving:
            keep_c = after(keep_c, grad_attended)
            sums = add(keep_c, got_c).astype(BF16).reshape(2, 2, 2, 2, 2, D // devices, hidden)
            send_a, keep_a, dims_a = split(sums[0], "yhlx", "y")
            send_b, keep_b, dims_b = split(sums[1], "yhlx", "x")
            late_branch = after(flat_branch, got_c)
            proj_grad = mm(att_own, late_branch, (((0,), (0,)), ((), ()))).astype(BF16)
            send_p, keep_p, _ = split(blocks_of(proj_grad), ORDER, "c")
            got_p = hop(send_p, "c")
            gatt, send_a, send_b, send_p = lax.optimization_barrier((gatt, send_a, send_b, send_p))
            got_a, got_b = hop(send_a, "y"), hop(send_b, "x")
        offset = jnp.stack([margin * (1 - my_a), batch_place % 2]).astype(jnp.int32)
        send_r, keep_r, gm_windows = attend_back(
            offset, triple, key_t, bias, lse, gatt, qkv_weight, grouped_t, seq_count, tall
        )
        gm = swap(gm_windows)
        if halving:
            gm_windows, got_a, got_b = lax.optimization_barrier((gm_windows, got_a, got_b))
        gm = swap(gm_windows)
    else:
        sent = grad_attended.reshape(blocks, per_group, share, wide).transpose(0, 2, 1, 3)
        gatt = swap(sent.reshape(seq_count, per_group, wide)).reshape(group_tokens, wide)
        grad_triple, gm_part = attend_plain_back(saved, gatt, my_weight)
        base = jnp.pad(gm_part.astype(BF16), ((margin, margin), (0, 0)))
        base = lax.dynamic_slice_in_dim(base, margin * (1 - my_a), group_tokens + margin)
        gm_windows = jnp.stack(
            [base[s * per_group : s * per_group + tall] for s in range(seq_count)]
        )
        gm = swap(gm_windows).reshape(blocks, share, tall, D)
        gm = jnp.sum(gm.astype(F32), axis=1).astype(BF16)
        own_grad = mm(grouped, grad_triple, (((0,), (0,)), ((), ()))).astype(BF16)
        spread = jnp.zeros((D, 3, share, wide), BF16)
        qkv_grad = lax.dynamic_update_index_in_dim(
            spread, own_grad.reshape(D, 3, wide), chunk, 2
        ).reshape(D, 3 * D)
        proj_grad = mm(att_own, flat_branch, (((0,), (0,)), ((), ()))).astype(BF16)
        rest = jnp.concatenate([qkv_grad, proj_grad], axis=1)

    if halving:
        got_r = hop(send_r, "c")
        keep_a, keep_b = after(keep_a, keep_r), after(keep_b, keep_r)
        send_a, keep_a, dims_a = split(add(keep_a, got_a).astype(BF16), dims_a, "x")
        send_b, keep_b, dims_b = split(add(keep_b, got_b).astype(BF16), dims_b, "y")
        sums = add(keep_r, got_r).astype(BF16).reshape(3, 2, 2, 2, 2, D // devices, D)
        sums_p = add(keep_p, got_p).astype(BF16)
        send_one, keep_one, dims_one = split(sums[:2], "yhlx", "y")
        send_two, keep_two, dims_two = split(jnp.stack([sums[2], sums_p]), "yhlx", "x")
        gm = after(gm, send_a, send_b)
        got_a, got_b = hop(send_a, "x"), hop(send_b, "y")
        got_one, got_two = hop(send_one, "y"), hop(send_two, "x")
    total = batch_count * latents

    here = batch_place * seq_count + seq_place
    own_cols = D // devices
    conditions = conditions.reshape(total, -1)
    condition_all = conditions[:, :D]
    embedding_all = conditions[:, D : D + embedding.shape[1]]
    ids_all = conditions[:, -1].astype(jnp.int32)
    logistic_all = jax.nn.sigmoid(condition_all)
    activated_all = (condition_all * logistic_all).astype(BF16).astype(F32)
    slope_all = logistic_all * (1.0 + condition_all * (1.0 - logistic_all))

    def back_through(grads):
        high = lax.reduce_precision(grads, 8, 7)
        middle_term = lax.reduce_precision(grads - high, 8, 7)
        low = grads - high - middle_term
        product = mm(jnp.concatenate([high, middle_term, low]).astype(BF16), ada_weight, NT)
        return product[:total] + product[total : 2 * total] + product[2 * total :]

    token_grad, conv_attn_part, end_sums = leave(
        meta, gm, tokens, top, bot, grad_after, pieces, kern_attn
    )

    all_sums, (conv_attn_grad, conv_ffn_grad) = sum_and_gather(
        jnp.concatenate([end_sums, mid_sums], axis=1),
        (jnp.sum(conv_attn_part, axis=0), conv_ffn_part),
    )
    if halving:
        keep_a, keep_b, keep_one, keep_two, end_sums = lax.optimization_barrier(
            (keep_a, keep_b, keep_one, keep_two, end_sums)
        )
        pair = jnp.stack([add(keep_a, got_a), add(keep_b, got_b)])
        pair = reduce_rest(pair, dims_a, "lh")
        down_rows, up_rows = pair[0], pair[1]
        send_one, keep_one, dims_one = split(add(keep_one, got_one).astype(BF16), dims_one, "x")
        send_two, keep_two, dims_two = split(add(keep_two, got_two).astype(BF16), dims_two, "y")
        got_one, got_two = hop(send_one, "x"), hop(send_two, "y")
        rest_rows = jnp.concatenate([add(keep_one, got_one), add(keep_two, got_two)])
        rest_rows = reduce_rest(rest_rows, dims_one, "lh")
    else:
        whole = jnp.stack([keep_c, send_c])
        whole = jnp.where(core[0] == 0, whole, whole[::-1]).transpose(1, 2, 0, 3, 4)
        whole = whole.reshape(2, D, hidden)
        down_rows, up_rows = scatter_rows(whole[0]), scatter_rows(whole[1])
        if share == 1:
            rest = jnp.stack([keep_r, send_r])
            rest = jnp.where(core[0] == 0, rest, rest[::-1]).transpose(2, 0, 3, 1, 4).reshape(D, -1)
            proj_grad = mm(att_own, flat_branch, (((0,), (0,)), ((), ()))).astype(BF16)
            rest = jnp.concatenate([rest, proj_grad], axis=1)
        rest_rows = scatter_rows(rest).reshape(own_cols, 4, D).transpose(1, 0, 2)
    qkv_rows = jnp.concatenate([rest_rows[0], rest_rows[1], rest_rows[2]], axis=1)
    proj_rows = rest_rows[3]

    grad_pieces = all_sums.reshape(total, 6 * D)
    grad_silu = back_through(grad_pieces)
    cond_all = grad_silu * slope_all
    cond_grad = lax.dynamic_slice_in_dim(cond_all, batch_place * latents, latents)
    cond_cols = lax.dynamic_slice_in_dim(cond_all, here * own_cols, own_cols, axis=1)
    act_cols = lax.dynamic_slice_in_dim(activated_all, here * own_cols, own_cols, axis=1)
    outer = lambda left, right: lax.dot_general(
        left, right, (((0,), (0,)), ((), ())), precision=HIGHEST, preferred_element_type=F32
    )
    hot_all = (ids_all[:, None] == jnp.arange(class_table.shape[0], dtype=jnp.int32)[None, :]).astype(F32)
    bias_cols = 6 * D // devices
    bias_grad = jnp.sum(
        lax.dynamic_slice_in_dim(grad_pieces, here * bias_cols, bias_cols, axis=1), axis=0
    )
    return (
        output,
        token_grad,
        cond_grad,
        outer(embedding_all, cond_cols),
        outer(hot_all, cond_cols),
        outer(act_cols, grad_pieces),
        bias_grad,
        conv_attn_grad,
        qkv_rows,
        proj_rows,
        up_rows,
        conv_ffn_grad,
        down_rows.T,
    )


def solution(mesh):
    strips = P("batch", "seq", None, None)
    in_specs = (strips, strips) + (P("batch"),) * 4 + (P(),) * 10
    both = ("batch", "seq")
    out_specs = (
        strips,
        strips,
        P("batch", None),
        P(None, both),
        P(None, both),
        P(both, None),
        P(both),
        P(None, both),
        P(both, None),
        P(both, None),
        P(both, None),
        P(None, both),
        P(None, both),
    )
    return jax.shard_map(shards, mesh=mesh, in_specs=in_specs, out_specs=out_specs, check_vma=False)
```

```python
import functools
import math

import jax
import jax.numpy as jnp
from jax import lax
from jax.experimental import pallas as pl
from jax.experimental.pallas import tpu as pltpu
from jax.sharding import PartitionSpec as P

D = 768
HEADS = 12
HEAD_DIM = 64
PAIR = 2 * HEAD_DIM
PAIRS = HEADS // 2
FF_BLOCK = 256
LANE_PARTS = D // 128
FACTOR = HEAD_DIM ** (-0.5)

F32 = jnp.float32
BF16 = jnp.bfloat16
HIGHEST = lax.Precision.HIGHEST
NN = (((1,), (0,)), ((), ()))
NT = (((1,), (1,)), ((), ()))
VMEM_LIMIT = 60 * 1024 * 1024


def mm(left, right, dims=NN):
    return lax.dot_general(left, right, dims, preferred_element_type=F32)


def shift_down(values):
    rows = lax.broadcasted_iota(jnp.int32, values.shape, 0)
    return jnp.where(rows == 0, 0.0, pltpu.roll(values, 1, 0))


def shift_up(values):
    count = values.shape[0]
    rows = lax.broadcasted_iota(jnp.int32, values.shape, 0)
    return jnp.where(rows == count - 1, 0.0, pltpu.roll(values, count - 1, 0))


def put_shifts(ref, row, parity, values):
    ref[row, 1 + parity] = values
    if parity == 0:
        ref[row, 3] = shift_up(values)
    else:
        ref[row, 0] = shift_down(values)


def normalize(values):
    centre = values - jnp.mean(values, axis=-1, keepdims=True)
    spread = jnp.mean(centre * centre, axis=-1, keepdims=True)
    scaled = lax.rsqrt(spread + 1e-06)
    return centre * scaled, scaled


def norm_back(grad_norm, normed, scaled):
    return scaled * (
        grad_norm
        - jnp.mean(grad_norm, axis=-1, keepdims=True)
        - normed * jnp.mean(grad_norm * normed, axis=-1, keepdims=True)
    )


def put_row(buf, row, values):
    for k in range(LANE_PARTS):
        buf[row, k] = values[:, 128 * k : 128 * (k + 1)]


def get_row(buf, row):
    return jnp.concatenate([buf[row, k] for k in range(LANE_PARTS)], axis=1)


def put_columns(buf, row, parity, values):
    for k in range(LANE_PARTS):
        buf[row, k, pl.ds(parity, values.shape[0], stride=2), :] = values[:, 128 * k : 128 * (k + 1)]


def get_columns(buf, row, parity):
    half = buf.shape[2] // 2
    return jnp.concatenate(
        [buf[row, k, pl.ds(parity, half, stride=2), :] for k in range(LANE_PARTS)], axis=1
    )


def usable_of(meta, latents, latent, row, parity, half):
    cols = 2 * lax.broadcasted_iota(jnp.int32, (half, 1), 0) + parity
    row_ok = jnp.logical_and(row >= 0, row < meta[latent])
    limit = jnp.where(row_ok, meta[latents + latent], 0)
    return (cols < limit).astype(F32)


def sum8(values):
    total = values[0:8]
    for start in range(8, values.shape[0], 8):
        total = total + values[start : start + 8]
    return total


def enter_kernel(meta, tok, top, bot, pieces, kern, out, buf, ent):
    latents = pl.num_programs(0)
    latent = pl.program_id(0)
    rows_here, cols = tok.shape[1], tok.shape[2]
    half = cols // 2
    row0 = meta[2 * latents]
    shift = pieces[0, 0:1, :]
    scale = 1.0 + pieces[0, 1:2, :]
    for rr in range(rows_here + 2):
        source = top[0, 0] if rr == 0 else bot[0, 0] if rr == rows_here + 1 else tok[0, rr - 1]
        put_row(buf, rr, source.astype(F32))
        for parity in range(2):
            normed, _ = normalize(get_columns(buf, rr, parity))
            ok = usable_of(meta, latents, latent, row0 + rr - 1, parity, half)
            put_shifts(ent, rr, parity, ((normed * scale + shift) * ok).astype(BF16).astype(F32))
    for row in range(rows_here):
        for parity in range(2):
            total = jnp.zeros((half, D), F32)
            for i in range(3):
                for j in range(3):
                    tap = 3 * i + j
                    total = total + ent[row + i, parity + j] * kern[tap : tap + 1, :]
            mixed = (ent[row + 1, 1 + parity] + total).astype(BF16)
            group = 2 * (row % 2) + parity
            out[0, group, (row // 2) * half : (row // 2 + 1) * half, :] = mixed


def enter(meta, tokens, top, bot, pieces, kern):
    latents, rows_here, cols, _ = tokens.shape
    half = cols // 2
    per_group = rows_here // 2 * half
    whole = lambda *shape: pl.BlockSpec(shape, lambda l, m: (l,) + (0,) * (len(shape) - 1))
    return pl.pallas_call(
        enter_kernel,
        out_shape=jax.ShapeDtypeStruct((latents, 4, per_group, D), BF16),
        grid_spec=pltpu.PrefetchScalarGridSpec(
            num_scalar_prefetch=1,
            grid=(latents,),
            in_specs=[
                whole(1, rows_here, cols, D),
                whole(1, 1, cols, D),
                whole(1, 1, cols, D),
                whole(1, 6, D),
                pl.BlockSpec((9, D), lambda l, m: (0, 0)),
            ],
            out_specs=whole(1, 4, per_group, D),
            scratch_shapes=[
                pltpu.VMEM((rows_here + 2, LANE_PARTS, cols, 128), F32),
                pltpu.VMEM((rows_here + 2, 4, half, D), F32),
            ],
        ),
        compiler_params=pltpu.CompilerParams(vmem_limit_bytes=VMEM_LIMIT),
        cost_estimate=pl.CostEstimate(flops=6_000_000_000, bytes_accessed=4_000_000, transcendentals=0),
        name="enter",
    )(meta, tokens, top, bot, pieces, kern)


def cot_kernel(cot, pieces, ge_out, get_out, cot_out, buf):
    rows_here, cols = cot.shape[1], cot.shape[2]
    half = cols // 2
    gate = pieces[0, 5:6, :]
    for row in range(rows_here):
        put_row(buf, row, cot[0, row].astype(F32))
        for parity in range(2):
            values = get_columns(buf, row, parity)
            at = (2 * row + parity) * half
            ge_out[0, at : at + half, :] = (gate * values).astype(BF16)
            cot_out[0, at : at + half, :] = values.astype(BF16)
    get_out[0] = ge_out[0].astype(F32).T.astype(BF16)


def prepare_cot(cotangent, pieces):
    latents, rows_here, cols, _ = cotangent.shape
    whole = lambda *shape: pl.BlockSpec(shape, lambda l: (l,) + (0,) * (len(shape) - 1))
    own = rows_here * cols
    return pl.pallas_call(
        cot_kernel,
        out_shape=(
            jax.ShapeDtypeStruct((latents, own, D), BF16),
            jax.ShapeDtypeStruct((latents, D, own), BF16),
            jax.ShapeDtypeStruct((latents, own, D), BF16),
        ),
        grid=(latents,),
        in_specs=[whole(1, rows_here, cols, D), whole(1, 6, D)],
        out_specs=(whole(1, own, D), whole(1, D, own), whole(1, own, D)),
        scratch_shapes=[pltpu.VMEM((rows_here, LANE_PARTS, cols, 128), F32)],
        compiler_params=pltpu.CompilerParams(vmem_limit_bytes=VMEM_LIMIT),
        cost_estimate=pl.CostEstimate(flops=4_000_000_000, bytes_accessed=4_000_000, transcendentals=0),
        name="prepare_cot",
    )(cotangent, pieces)


def second_kernel(meta, att, tok, top, bot, pieces, proj, e2_out, e2t_out, after_out, branch_out, buf, bran):
    latents = pl.num_programs(0)
    latent = pl.program_id(0)
    rows_here, cols = tok.shape[1], tok.shape[2]
    half = cols // 2
    row0 = meta[2 * latents]
    gate = pieces[0, 2:3, :]
    shift = pieces[0, 3:4, :]
    scale = 1.0 + pieces[0, 4:5, :]
    for group in range(4):
        bran[group] = mm(att[group], proj[...])
    for rr in range(rows_here + 2):
        source = top[0, 0] if rr == 0 else bot[0, 0] if rr == rows_here + 1 else tok[0, rr - 1]
        put_row(buf, rr, source.astype(F32))
        for parity in range(2):
            group = 2 * ((rr + 1) % 2) + parity
            branch = bran[group, (rr // 2) * half : (rr // 2 + 1) * half, :]
            after = get_columns(buf, rr, parity) + gate * branch
            normed, _ = normalize(after)
            ok = usable_of(meta, latents, latent, row0 + rr - 1, parity, half)
            at = (2 * rr + parity) * half
            e2_out[0, at : at + half, :] = ((normed * scale + shift) * ok).astype(BF16)
            if 1 <= rr <= rows_here:
                own = at - cols
                after_out[0, own : own + half, :] = after
                branch_out[0, own : own + half, :] = branch
    e2t_out[0] = e2_out[0].astype(F32).T.astype(BF16)


def second(meta, attended, tokens, top, bot, pieces, proj):
    latents, rows_here, cols, _ = tokens.shape
    own = rows_here * cols
    wide = attended.shape[1]
    whole = lambda *shape: pl.BlockSpec(shape, lambda l, m: (l,) + (0,) * (len(shape) - 1))
    return pl.pallas_call(
        second_kernel,
        out_shape=(
            jax.ShapeDtypeStruct((latents, own + 2 * cols, D), BF16),
            jax.ShapeDtypeStruct((latents, D, own + 2 * cols), BF16),
            jax.ShapeDtypeStruct((latents, own, D), F32),
            jax.ShapeDtypeStruct((latents, own, D), F32),
        ),
        grid_spec=pltpu.PrefetchScalarGridSpec(
            num_scalar_prefetch=1,
            grid=(latents,),
            in_specs=[
                whole(4, wide, D),
                whole(1, rows_here, cols, D),
                whole(1, 1, cols, D),
                whole(1, 1, cols, D),
                whole(1, 6, D),
                pl.BlockSpec((D, D), lambda l, m: (0, 0)),
            ],
            out_specs=(
                whole(1, own + 2 * cols, D),
                whole(1, D, own + 2 * cols),
                whole(1, own, D),
                whole(1, own, D),
            ),
            scratch_shapes=[
                pltpu.VMEM((rows_here + 2, LANE_PARTS, cols, 128), F32),
                pltpu.VMEM((4, wide, D), F32),
            ],
        ),
        compiler_params=pltpu.CompilerParams(vmem_limit_bytes=VMEM_LIMIT),
        cost_estimate=pl.CostEstimate(flops=7_000_000_000, bytes_accessed=4_000_000, transcendentals=0),
        name="second",
    )(meta, attended, tokens, top, bot, pieces, proj)


def normal_parts(values):
    density = jnp.exp2(values * values * -0.7213475204444817 - 1.3257480647361592)
    t = 1.0 / (1.0 + 0.2316419 * jnp.abs(values))
    series = t * (
        0.319381530
        + t * (-0.356563782 + t * (1.781477937 + t * (-1.821255978 + t * 1.330274429)))
    )
    tail = density * series
    return jnp.where(values > 0.0, 1.0 - tail, tail), density


def ffn_kernel(core, e2, e2t, ge, get, up, down, kern_in, exp_out, ge2_out, send_out, keep_out, kern_out, *scratch):
    latents = e2.shape[0]
    lifted, gact, gconv, act, graised = [scratch[k * latents : (k + 1) * latents] for k in range(5)]
    down_acc, up_acc = scratch[5 * latents :]
    step = pl.program_id(0)
    half = lifted[0].shape[2]
    rows_here = gconv[0].shape[0]
    block = lifted[0].shape[3]
    chunks = block // 128
    lanes = [slice(c * 128, (c + 1) * 128) for c in range(chunks)]
    taps = [[kern_in[t : t + 1, cut].astype(F32) for t in range(9)] for cut in lanes]
    sums = [[jnp.zeros((8, 128), F32) for _ in range(9)] for _ in range(chunks)]
    lift_rows = 3

    def put(ref, row, parity, cut, values):
        ref[row, 1 + parity, :, cut] = values
        if parity == 0:
            ref[row, 3, :, cut] = shift_up(values)
        else:
            ref[row, 0, :, cut] = shift_down(values)

    def lift(latent, part):
        size = lift_rows * 2 * half
        raised = mm(e2[latent, part * size : (part + 1) * size], up[...])
        for k in range(lift_rows):
            for parity in range(2):
                at = (2 * k + parity) * half
                for cut in lanes:
                    put(lifted[latent], part * lift_rows + k, parity, cut, raised[at : at + half, cut])

    def pull(latent):
        gact[latent][...] = mm(ge[latent], down[...], NT)

    def bend(latent, row, c):
        cut = lanes[c]
        for parity in range(2):
            total = None
            for i in range(3):
                for j in range(3):
                    term = lifted[latent][row + i, parity + j, :, cut] * taps[c][3 * i + j]
                    total = term if total is None else total + term
            cdf, density = normal_parts(total)
            at = (2 * row + parity) * half
            act[latent][at : at + half, cut] = (total * cdf).astype(BF16)
            grad = gact[latent][at : at + half, cut] * (cdf + total * density)
            put(gconv[latent], row, parity, cut, grad)

    def unbend(latent, rr, c):
        cut = lanes[c]
        for parity in range(2):
            total = None
            for i in range(3):
                row = rr - i
                if not 0 <= row < rows_here:
                    continue
                for j in range(3):
                    term = gconv[latent][row, parity + 2 - j, :, cut] * taps[c][3 * i + j]
                    total = term if total is None else total + term
            at = (2 * rr + parity) * half
            graised[latent][at : at + half, cut] = total.astype(BF16)
            if rr < rows_here:
                here = gconv[latent][rr, 1 + parity, :, cut]
                for i in range(3):
                    for j in range(3):
                        t = 3 * i + j
                        part = lifted[latent][rr + i, parity + j, :, cut] * here
                        sums[c][t] = sums[c][t] + sum8(part)

    def expand(latent):
        exp_out[latent] += mm(act[latent][...], down[...])

    def lower(latent):
        ge2_out[latent] += mm(graised[latent][...], up[...], NT)

    def weigh_down(latent):
        value = mm(get[latent], act[latent][...])
        down_acc[...] = value if latent == 0 else down_acc[...] + value

    def weigh_up(latent):
        value = mm(e2t[latent], graised[latent][...])
        up_acc[...] = value if latent == 0 else up_acc[...] + value

    @pl.when(step == 0)
    def _():
        exp_out[...] = jnp.zeros_like(exp_out)
        ge2_out[...] = jnp.zeros_like(ge2_out)

    def mix(work, more):
        stride = max(1, len(work) // max(1, len(more)))
        for k, unit in enumerate(work):
            if k % stride == 0 and k // stride < len(more):
                more[k // stride]()
            unit()
        for unit in more[-(-len(work) // stride) :]:
            unit()

    part = functools.partial
    lifts = (rows_here + 2) // lift_rows
    for k in range(lifts):
        lift(0, k)
    pull(0)
    for latent in range(latents):
        bends = [part(bend, latent, row, c) for c in range(chunks) for row in range(rows_here)]
        unbends = [part(unbend, latent, rr, c) for c in range(chunks) for rr in range(rows_here + 2)]
        first, then = [], [part(expand, latent), part(weigh_down, latent)]
        if latent > 0:
            first += [part(lower, latent - 1), part(weigh_up, latent - 1)]
        if latent + 1 < latents:
            first += [part(lift, latent + 1, k) for k in range(lifts)] + [part(pull, latent + 1)]
        mix(bends, first)
        mix(unbends, then)
    lower(latents - 1)
    weigh_up(latents - 1)

    size = down_acc.shape[0] // 4
    for which, acc in enumerate((down_acc, up_acc)):
        for y in range(2):
            mine = pl.multiple_of((2 * y + core[0]) * size, 8)
            other = pl.multiple_of((2 * y + 1 - core[0]) * size, 8)
            keep_out[which, y] = acc[pl.ds(mine, size), :].astype(BF16)
            send_out[which, y] = acc[pl.ds(other, size), :].astype(BF16)
    for c, cut in enumerate(lanes):
        for t in range(9):
            kern_out[t : t + 1, cut] = jnp.sum(sums[c][t], axis=0, keepdims=True)


def ffn(core, e2, e2t, ge, get, up, down, kern, cols):
    latents, wide, _ = e2.shape
    half = cols // 2
    own = ge.shape[1]
    rows_here = own // cols
    hidden = up.shape[1]
    fixed = lambda *shape: pl.BlockSpec(shape, lambda f, c: (0,) * len(shape))
    parts = jax.ShapeDtypeStruct((2, 2, D // 4, hidden), BF16)
    parts_spec = pl.BlockSpec((2, 2, D // 4, FF_BLOCK), lambda f, c: (0, 0, 0, f))
    each = lambda *args: [pltpu.VMEM(*args)] * latents
    return pl.pallas_call(
        ffn_kernel,
        out_shape=(
            jax.ShapeDtypeStruct((latents, own, D), F32),
            jax.ShapeDtypeStruct((latents, wide, D), F32),
            parts,
            parts,
            jax.ShapeDtypeStruct((9, hidden), F32),
        ),
        grid_spec=pltpu.PrefetchScalarGridSpec(
            num_scalar_prefetch=1,
            grid=(hidden // FF_BLOCK,),
            in_specs=[
                fixed(latents, wide, D),
                fixed(latents, D, wide),
                fixed(latents, own, D),
                fixed(latents, D, own),
                pl.BlockSpec((D, FF_BLOCK), lambda f, c: (0, f)),
                pl.BlockSpec((FF_BLOCK, D), lambda f, c: (f, 0)),
                pl.BlockSpec((9, FF_BLOCK), lambda f, c: (0, f)),
            ],
            out_specs=(
                fixed(latents, own, D),
                fixed(latents, wide, D),
                parts_spec,
                parts_spec,
                pl.BlockSpec((9, FF_BLOCK), lambda f, c: (0, f)),
            ),
            scratch_shapes=each((rows_here + 2, 4, half, FF_BLOCK), F32)
            + each((own, FF_BLOCK), F32)
            + each((rows_here, 4, half, FF_BLOCK), F32)
            + each((own, FF_BLOCK), BF16)
            + each((wide, FF_BLOCK), BF16)
            + [pltpu.VMEM((D, FF_BLOCK), F32), pltpu.VMEM((D, FF_BLOCK), F32)],
        ),
        compiler_params=pltpu.CompilerParams(vmem_limit_bytes=VMEM_LIMIT),
        cost_estimate=pl.CostEstimate(flops=35_000_000_000, bytes_accessed=4_000_000, transcendentals=0),
        name="ffn",
    )(core, e2, e2t, ge, get, up, down, kern)


def output_kernel(exp, after_in, cot_in, pieces, out, sum_out, buf):
    rows_here, cols = out.shape[1], out.shape[2]
    half = cols // 2
    gate = pieces[0, 5:6, :]
    total = jnp.zeros((8, D), F32)
    for row in range(rows_here):
        for parity in range(2):
            part = pl.ds((2 * row + parity) * half, half)
            expanded = exp[0, part, :]
            put_columns(buf, row, parity, after_in[0, part, :] + gate * expanded)
            total = total + sum8(cot_in[0, part, :].astype(F32) * expanded)
        out[0, row] = get_row(buf, row).astype(BF16)
    sum_out[0] = jnp.sum(total, axis=0, keepdims=True)


def finish_output(exp, after, cot, pieces, rows_here, cols):
    latents, own, _ = exp.shape
    whole = lambda *shape: pl.BlockSpec(shape, lambda l: (l,) + (0,) * (len(shape) - 1))
    return pl.pallas_call(
        output_kernel,
        out_shape=(
            jax.ShapeDtypeStruct((latents, rows_here, cols, D), BF16),
            jax.ShapeDtypeStruct((latents, 1, D), F32),
        ),
        grid=(latents,),
        in_specs=[whole(1, own, D), whole(1, own, D), whole(1, own, D), whole(1, 6, D)],
        out_specs=(whole(1, rows_here, cols, D), whole(1, 1, D)),
        scratch_shapes=[pltpu.VMEM((rows_here, LANE_PARTS, cols, 128), F32)],
        compiler_params=pltpu.CompilerParams(vmem_limit_bytes=VMEM_LIMIT),
        cost_estimate=pl.CostEstimate(flops=5_000_000_000, bytes_accessed=4_000_000, transcendentals=0),
        name="finish_output",
    )(exp, after, cot, pieces)


def middle_kernel(meta, ge2, low, high, after_in, branch_in, cot_in, pieces, proj, after_grad, gb_out, gatt_out, sums_out):
    latents = pl.num_programs(0)
    latent = pl.program_id(0)
    own = after_in.shape[1]
    cols = low.shape[1]
    rows_here = own // cols
    half = cols // 2
    row0 = meta[2 * latents]
    gate_one = pieces[0, 2:3, :]
    scale = 1.0 + pieces[0, 4:5, :]
    sums = [jnp.zeros((8, D), F32) for _ in range(3)]
    for row in range(rows_here):
        for parity in range(2):
            at = (2 * row + parity) * half
            part = pl.ds(at, half)
            side = pl.ds(parity * half, half)
            after = after_in[0, part, :]
            cot = cot_in[0, part, :].astype(F32)
            normed, scaled = normalize(after)
            ok = usable_of(meta, latents, latent, row0 + row, parity, half)
            grad = ge2[0, pl.ds(at + cols, half), :]
            if row == 0:
                grad = grad + low[0, side, :].astype(F32)
            if row == rows_here - 1:
                grad = grad + high[0, side, :].astype(F32)
            grad = grad * ok
            grad_after = cot + norm_back(grad * scale, normed, scaled)
            after_grad[0, part, :] = grad_after
            sums[0] = sums[0] + sum8(grad_after * branch_in[0, part, :])
            sums[1] = sums[1] + sum8(grad)
            sums[2] = sums[2] + sum8(grad * normed)
            group = 2 * (row % 2) + parity
            to = pl.ds((row // 2) * half, half)
            gb_out[0, group, to, :] = (gate_one * grad_after).astype(BF16)
    for k in range(3):
        sums_out[0, k : k + 1, :] = jnp.sum(sums[k], axis=0, keepdims=True)
    for group in range(4):
        gatt_out[0, group] = mm(gb_out[0, group], proj[...], NT).astype(BF16)


def middle(meta, ge2, low, high, after, branch, cot, pieces, proj):
    latents, own, _ = after.shape
    wide, cols = ge2.shape[1], low.shape[1]
    per_group = own // 4
    whole = lambda *shape: pl.BlockSpec(shape, lambda l, m: (l,) + (0,) * (len(shape) - 1))
    return pl.pallas_call(
        middle_kernel,
        out_shape=(
            jax.ShapeDtypeStruct((latents, own, D), F32),
            jax.ShapeDtypeStruct((latents, 4, per_group, D), BF16),
            jax.ShapeDtypeStruct((latents, 4, per_group, D), BF16),
            jax.ShapeDtypeStruct((latents, 3, D), F32),
        ),
        grid_spec=pltpu.PrefetchScalarGridSpec(
            num_scalar_prefetch=1,
            grid=(latents,),
            in_specs=[
                whole(1, wide, D),
                whole(1, cols, D),
                whole(1, cols, D),
                whole(1, own, D),
                whole(1, own, D),
                whole(1, own, D),
                whole(1, 6, D),
                pl.BlockSpec((D, D), lambda l, m: (0, 0)),
            ],
            out_specs=(
                whole(1, own, D),
                whole(1, 4, per_group, D),
                whole(1, 4, per_group, D),
                whole(1, 3, D),
            ),
        ),
        compiler_params=pltpu.CompilerParams(vmem_limit_bytes=VMEM_LIMIT),
        cost_estimate=pl.CostEstimate(flops=8_000_000_000, bytes_accessed=4_000_000, transcendentals=0),
        name="middle",
    )(meta, ge2, low, high, after, branch, cot, pieces, proj)


def leave_kernel(meta, gm, tok, top, bot, after_grad, pieces, kern, out, kern_out, sums_out, buf, ent, gmx, obuf, nbuf, sbuf):
    latents = pl.num_programs(0)
    latent = pl.program_id(0)
    rows_here, cols = tok.shape[1], tok.shape[2]
    half = cols // 2
    row0 = meta[2 * latents]
    shift = pieces[0, 0:1, :]
    scale = 1.0 + pieces[0, 1:2, :]
    taps = [kern[t : t + 1, :] for t in range(9)]
    for rr in range(rows_here + 2):
        source = top[0, 0] if rr == 0 else bot[0, 0] if rr == rows_here + 1 else tok[0, rr - 1]
        put_row(buf, rr, source.astype(F32))
        for parity in range(2):
            normed, scaled = normalize(get_columns(buf, rr, parity))
            if 1 <= rr <= rows_here:
                nbuf[rr - 1, parity] = normed
                sbuf[rr - 1, parity] = jnp.broadcast_to(scaled, (half, 128))
            ok = usable_of(meta, latents, latent, row0 + rr - 1, parity, half)
            put_shifts(ent, rr, parity, ((normed * scale + shift) * ok).astype(BF16).astype(F32))
            group = 2 * ((rr + 1) % 2) + parity
            at = (rr // 2) * half
            put_shifts(gmx, rr, parity, gm[group, at : at + half, :].astype(F32))
    sums = [jnp.zeros((8, D), F32) for _ in range(2)]
    tap_sums = [jnp.zeros((8, D), F32) for _ in range(9)]
    for row in range(rows_here):
        for parity in range(2):
            here = gmx[row + 1, 1 + parity]
            total = here
            for i in range(3):
                for j in range(3):
                    t = 3 * i + j
                    total = total + gmx[row + 2 - i, parity + 2 - j] * taps[t]
                    tap_sums[t] = tap_sums[t] + sum8(ent[row + i, parity + j] * here)
            ok = usable_of(meta, latents, latent, row0 + row, parity, half)
            grad = total * ok
            normed, scaled = nbuf[row, parity], sbuf[row, parity, :, 0:1]
            sums[0] = sums[0] + sum8(grad)
            sums[1] = sums[1] + sum8(grad * normed)
            at = (2 * row + parity) * half
            back = after_grad[0, at : at + half, :] + norm_back(grad * scale, normed, scaled)
            put_columns(obuf, row, parity, back)
        out[0, row] = get_row(obuf, row)
    for k in range(2):
        sums_out[0, k : k + 1, :] = jnp.sum(sums[k], axis=0, keepdims=True)
    for t in range(9):
        kern_out[0, t : t + 1, :] = jnp.sum(tap_sums[t], axis=0, keepdims=True)


def leave(meta, gm, tokens, top, bot, after_grad, pieces, kern):
    latents, rows_here, cols, _ = tokens.shape
    half = cols // 2
    own = rows_here * cols
    wide = gm.shape[1]
    whole = lambda *shape: pl.BlockSpec(shape, lambda l, m: (l,) + (0,) * (len(shape) - 1))
    return pl.pallas_call(
        leave_kernel,
        out_shape=(
            jax.ShapeDtypeStruct((latents, rows_here, cols, D), F32),
            jax.ShapeDtypeStruct((latents, 9, D), F32),
            jax.ShapeDtypeStruct((latents, 2, D), F32),
        ),
        grid_spec=pltpu.PrefetchScalarGridSpec(
            num_scalar_prefetch=1,
            grid=(latents,),
            in_specs=[
                whole(4, wide, D),
                whole(1, rows_here, cols, D),
                whole(1, 1, cols, D),
                whole(1, 1, cols, D),
                whole(1, own, D),
                whole(1, 6, D),
                pl.BlockSpec((9, D), lambda l, m: (0, 0)),
            ],
            out_specs=(whole(1, rows_here, cols, D), whole(1, 9, D), whole(1, 2, D)),
            scratch_shapes=[
                pltpu.VMEM((rows_here + 2, LANE_PARTS, cols, 128), F32),
                pltpu.VMEM((rows_here + 2, 4, half, D), F32),
                pltpu.VMEM((rows_here + 2, 4, half, D), F32),
                pltpu.VMEM((rows_here, LANE_PARTS, cols, 128), F32),
                pltpu.VMEM((rows_here, 2, half, D), F32),
                pltpu.VMEM((rows_here, 2, half, 128), F32),
            ],
        ),
        compiler_params=pltpu.CompilerParams(vmem_limit_bytes=VMEM_LIMIT),
        cost_estimate=pl.CostEstimate(flops=10_000_000_000, bytes_accessed=4_000_000, transcendentals=0),
        name="leave",
    )(meta, gm, tokens, top, bot, after_grad, pieces, kern)


def pair_parts(values):
    lanes = lax.broadcasted_iota(jnp.int32, values.shape, 1)
    first = lanes < HEAD_DIM
    zero = jnp.zeros_like(values)
    return jnp.where(first, values, zero), jnp.where(first, zero, values)


def attend_kernel(offset, mixed, wq, wk, wvt, bias, out, lse_out, padded):
    tokens = mixed.shape[0]
    strips, window, _ = out.shape
    step = tokens // strips
    margin = window - step
    m = mixed[...]
    query = (mm(m, wq[...]).astype(BF16) * FACTOR).astype(BF16)
    key = mm(m, wk[...]).astype(BF16)
    value_t = mm(wvt[...], m, NT).astype(BF16)
    keep = jnp.tile(bias[...], (1, tokens // 128))
    scores = [mm(key_e, query, NT) + keep for key_e in pair_parts(key)]
    parts = []
    for e in range(2):
        peak = jnp.max(scores[e], axis=0, keepdims=True)
        raw = jnp.exp(scores[e] - peak)
        total = jnp.sum(raw, axis=0, keepdims=True)
        prob = (raw * (1.0 / total)).astype(BF16)
        parts.append(mm(value_t[e * HEAD_DIM : (e + 1) * HEAD_DIM], prob))
        lse_out[0, e : e + 1, :] = peak + jnp.log(total)
    padded[0:margin] = jnp.zeros((margin, PAIR), F32)
    padded[margin + tokens :] = jnp.zeros((margin, PAIR), F32)
    padded[margin : margin + tokens] = jnp.concatenate(parts, axis=0).T
    for s in range(strips):
        start = pl.multiple_of(offset[0] + s * step, 8)
        out[s] = padded[pl.ds(start, window), :].astype(BF16)


def attend(offset, mixed, weight, weight_t, bias, strips, window):
    tokens = mixed.shape[0]
    margin = window - tokens // strips
    return pl.pallas_call(
        attend_kernel,
        out_shape=(
            jax.ShapeDtypeStruct((strips, window, D), BF16),
            jax.ShapeDtypeStruct((PAIRS, 2, tokens), F32),
        ),
        grid_spec=pltpu.PrefetchScalarGridSpec(
            num_scalar_prefetch=1,
            grid=(PAIRS,),
            in_specs=[
                pl.BlockSpec((tokens, D), lambda p, o: (0, 0)),
                pl.BlockSpec((D, PAIR), lambda p, o: (0, p)),
                pl.BlockSpec((D, PAIR), lambda p, o: (0, PAIRS + p)),
                pl.BlockSpec((PAIR, D), lambda p, o: (2 * PAIRS + p, 0)),
                pl.BlockSpec((tokens, 128), lambda p, o: (0, 0)),
            ],
            out_specs=(
                pl.BlockSpec((strips, window, PAIR), lambda p, o: (0, 0, p)),
                pl.BlockSpec((1, 2, tokens), lambda p, o: (p, 0, 0)),
            ),
            scratch_shapes=[pltpu.VMEM((tokens + 2 * margin, PAIR), F32)],
        ),
        compiler_params=pltpu.CompilerParams(vmem_limit_bytes=VMEM_LIMIT),
        cost_estimate=pl.CostEstimate(flops=16_000_000_000, bytes_accessed=4_000_000, transcendentals=0),
        name="attend",
    )(offset, mixed, weight, weight, weight_t, bias)


def attend_back_kernel(offset, query, key, value, key_t, bias, lse, gatt, wq, wk, wv, mixed_t, send_out, keep_out, gm_out, acc, part):
    tokens = query.shape[0]
    strips, window, _ = gm_out.shape
    step = tokens // strips
    margin = window - step
    p = pl.program_id(0)
    q = query[...]
    keep = jnp.tile(bias[...], (1, tokens // 128))
    queries = pair_parts(q)
    keys = pair_parts(key[...])
    values = pair_parts(value[...])
    grads = pair_parts(gatt[...])
    scores = [mm(keys[e], q, NT) for e in range(2)]
    grad_probs = [mm(values[e], gatt[...], NT) for e in range(2)]
    parts, probs, grad_scores = [], [], []
    for e in range(2):
        prob = jnp.exp(scores[e] * FACTOR + keep - lse[0, e : e + 1, :])
        delta = jnp.sum(prob * grad_probs[e], axis=0, keepdims=True)
        probs.append(prob.astype(BF16))
        grad_scores.append((prob * (grad_probs[e] - delta)).astype(BF16))
        parts.append(mm(key_t[e * HEAD_DIM : (e + 1) * HEAD_DIM], grad_scores[e]))
    dv = mm(jnp.concatenate(probs, axis=1), jnp.concatenate(grads, axis=0))
    dk = mm(jnp.concatenate(grad_scores, axis=1), jnp.concatenate(queries, axis=0))
    dq = jnp.concatenate(parts, axis=0).T * FACTOR
    dk = dk * FACTOR
    all_three = jnp.concatenate([dq.astype(BF16), dk.astype(BF16), dv.astype(BF16)], axis=1)
    part[...] = mm(mixed_t[...], all_three)
    size = D // 4
    for y in range(2):
        mine = pl.multiple_of((2 * y + offset[1]) * size, 8)
        other = pl.multiple_of((2 * y + 1 - offset[1]) * size, 8)
        for k in range(3):
            cut = slice(k * PAIR, (k + 1) * PAIR)
            keep_out[k, y] = part[pl.ds(mine, size), cut].astype(BF16)
            send_out[k, y] = part[pl.ds(other, size), cut].astype(BF16)
    total = mm(all_three, jnp.concatenate([wq[...], wk[...], wv[...]], axis=1), NT)

    @pl.when(p == 0)
    def _():
        acc[0:margin] = jnp.zeros((margin, D), F32)
        acc[margin + tokens :] = jnp.zeros((margin, D), F32)
        acc[margin : margin + tokens] = total

    @pl.when(p > 0)
    def _():
        acc[margin : margin + tokens] += total

    @pl.when(p == pl.num_programs(0) - 1)
    def _():
        for s in range(strips):
            start = pl.multiple_of(offset[0] + s * step, 8)
            gm_out[s] = acc[pl.ds(start, window), :].astype(BF16)


def attend_back(offset, triple, key_t, bias, lse, gatt, weight, mixed_t, strips, window):
    tokens = triple.shape[0]
    margin = window - tokens // strips
    part = lambda k: pl.BlockSpec((tokens, PAIR), lambda p, o: (0, k * PAIRS + p))
    slab = lambda k: pl.BlockSpec((D, PAIR), lambda p, o: (0, k * PAIRS + p))
    parts = jax.ShapeDtypeStruct((3, 2, D // 4, D), BF16)
    parts_spec = pl.BlockSpec((3, 2, D // 4, PAIR), lambda p, o: (0, 0, 0, p))
    return pl.pallas_call(
        attend_back_kernel,
        out_shape=(
            parts,
            parts,
            jax.ShapeDtypeStruct((strips, window, D), BF16),
        ),
        grid_spec=pltpu.PrefetchScalarGridSpec(
            num_scalar_prefetch=1,
            grid=(PAIRS,),
            in_specs=[
                part(0),
                part(1),
                part(2),
                pl.BlockSpec((PAIR, tokens), lambda p, o: (p, 0)),
                pl.BlockSpec((tokens, 128), lambda p, o: (0, 0)),
                pl.BlockSpec((1, 2, tokens), lambda p, o: (p, 0, 0)),
                part(0),
                slab(0),
                slab(1),
                slab(2),
                pl.BlockSpec((D, tokens), lambda p, o: (0, 0)),
            ],
            out_specs=(
                parts_spec,
                parts_spec,
                pl.BlockSpec((strips, window, D), lambda p, o: (0, 0, 0)),
            ),
            scratch_shapes=[
                pltpu.VMEM((tokens + 2 * margin, D), F32),
                pltpu.VMEM((D, 3 * PAIR), F32),
            ],
        ),
        compiler_params=pltpu.CompilerParams(vmem_limit_bytes=VMEM_LIMIT),
        cost_estimate=pl.CostEstimate(flops=23_000_000_000, bytes_accessed=4_000_000, transcendentals=0),
        name="attend_back",
    )(offset, triple, triple, triple, key_t, bias, lse, gatt, weight, weight, weight, mixed_t)


def from_before(values, axis):
    count = lax.axis_size(axis)
    return lax.ppermute(values, axis, [(i, i + 1) for i in range(count - 1)])


def from_after(values, axis):
    count = lax.axis_size(axis)
    return lax.ppermute(values, axis, [(i + 1, i) for i in range(count - 1)])


def swap(values):
    return lax.all_to_all(values, "seq", 0, 0, tiled=False)


BITS = {"y": ("batch", 2), "c": ("batch", 1), "h": ("seq", 4), "l": ("seq", 2), "x": ("seq", 1)}
ORDER = "ychlx"


def blocks_of(values):
    return values.reshape(values.shape[:-2] + (2, 2, 2, 2, 2, values.shape[-2] // 32, values.shape[-1]))


def split(values, dims, bit):
    axis, mask = BITS[bit]
    mine = (lax.axis_index(axis) // mask) % 2
    at = values.ndim - 2 - len(dims) + dims.index(bit)
    send = lax.dynamic_index_in_dim(values, 1 - mine, at, keepdims=False)
    keep = lax.dynamic_index_in_dim(values, mine, at, keepdims=False)
    return send, keep, dims.replace(bit, "")


def hop(values, bit):
    axis, mask = BITS[bit]
    count = lax.axis_size(axis)
    return lax.ppermute(values, axis, [(i, i ^ mask) for i in range(count)])


def add(keep, got):
    return keep.astype(F32) + got.astype(F32)


def after(values, *others):
    return lax.optimization_barrier((values,) + others)[0]


def reduce_rest(values, dims, order):
    for bit in order:
        send, keep, dims = split(values.astype(BF16), dims, bit)
        values = add(keep, hop(send, bit))
    return values


def scatter_rows(values):
    return lax.psum_scatter(values, ("batch", "seq"), scatter_dimension=0, tiled=True).astype(F32)


def sum_and_gather(common, sliced):
    seq_count, batch_count = lax.axis_size("seq"), lax.axis_size("batch")
    batch_place = lax.axis_index("batch")
    flat = common.reshape(1, -1)
    pieces = [jnp.broadcast_to(flat, (seq_count, flat.shape[1]))]
    for values in sliced:
        cut = values.reshape(values.shape[0], batch_count, seq_count, -1).transpose(2, 1, 0, 3)
        pieces.append(cut.reshape(seq_count, -1))
    whole = jnp.concatenate(pieces, axis=1)
    whole = jnp.pad(whole, ((0, 0), (0, -whole.shape[1] % 1024))).reshape(seq_count, -1, 128)
    summed = jnp.sum(swap(whole), axis=0)
    gathered = lax.all_gather(summed, "batch", axis=0).reshape(batch_count, -1)
    common_all = gathered[:, : flat.shape[1]].reshape((batch_count,) + common.shape)
    at = flat.shape[1]
    own = []
    for values, piece in zip(sliced, pieces[1:]):
        part = jnp.sum(gathered[:, at : at + piece.shape[1]], axis=0)
        part = part.reshape(batch_count, values.shape[0], -1)
        own.append(lax.dynamic_index_in_dim(part, batch_place, 0, keepdims=False))
        at += piece.shape[1]
    return common_all, own


def windows_of(values, offset, margin, strips):
    step = values.shape[0] // strips
    padded = jnp.pad(values, ((margin, margin), (0, 0)))
    base = lax.dynamic_slice_in_dim(padded, offset, values.shape[0] + margin)
    return jnp.stack([base[s * step : s * step + step + margin] for s in range(strips)])


def attend_plain(mixed, weight, ok, heads):
    wide = heads * HEAD_DIM
    triple = mm(mixed, weight).astype(BF16)
    split = lambda k: triple[:, k * wide : (k + 1) * wide].reshape(-1, heads, HEAD_DIM)
    queries, keys, values = split(0), split(1), split(2)
    scores = jnp.einsum("qhe,khe->hqk", queries, keys, preferred_element_type=F32) * FACTOR
    scores = jnp.where(ok[None, None, :], scores, -1e30)
    prob = jax.nn.softmax(scores, axis=-1)
    out = jnp.einsum("hqk,khe->qhe", prob.astype(BF16), values, preferred_element_type=F32)
    return out.reshape(-1, wide).astype(BF16), (queries, keys, values, prob)


def attend_plain_back(saved, grad, weight):
    queries, keys, values, prob = saved
    heads = queries.shape[1]
    grad = grad.reshape(-1, heads, HEAD_DIM)
    grad_prob = jnp.einsum("qhe,khe->hqk", grad, values, preferred_element_type=F32)
    delta = jnp.sum(prob * grad_prob, axis=-1, keepdims=True)
    grad_scores = (prob * (grad_prob - delta)).astype(BF16)
    dq = jnp.einsum("hqk,khe->qhe", grad_scores, keys, preferred_element_type=F32) * FACTOR
    dk = jnp.einsum("hqk,qhe->khe", grad_scores, queries, preferred_element_type=F32) * FACTOR
    dv = jnp.einsum("hqk,qhe->khe", prob.astype(BF16), grad, preferred_element_type=F32)
    flat = lambda v: v.reshape(v.shape[0], -1).astype(BF16)
    grads = jnp.concatenate([flat(dq), flat(dk), flat(dv)], axis=1)
    return grads, mm(grads, weight, NT)


def shards(
    tokens,
    cotangent,
    timestep,
    class_ids,
    heights,
    widths,
    time_weight,
    class_table,
    ada_weight,
    ada_bias,
    conv_attn,
    qkv_weight,
    proj_weight,
    up_weight,
    conv_ffn,
    down_weight,
):
    latents, rows_here, cols, _ = tokens.shape
    half = cols // 2
    seq_count = lax.axis_size("seq")
    seq_place = lax.axis_index("seq")
    batch_count = lax.axis_size("batch")
    batch_place = lax.axis_index("batch")
    devices = batch_count * seq_count
    blocks = latents * 4
    share = seq_count // blocks
    per_group = rows_here // 2 * half
    group_tokens = seq_count * per_group

    first, last = tokens[:, :1], tokens[:, rows_here - 1 :]
    top = from_before(last, "seq")
    bot = from_after(first, "seq")

    half_freq = time_weight.shape[0] // 2
    frequency = jnp.exp(-math.log(10000.0) * jnp.arange(half_freq, dtype=F32) / half_freq)
    angles = timestep.astype(F32)[:, None] * frequency[None, :]
    embedding = jnp.concatenate([jnp.cos(angles), jnp.sin(angles)], axis=1).astype(BF16)
    one_hot = (
        class_ids[:, None] == jnp.arange(class_table.shape[0], dtype=jnp.int32)[None, :]
    ).astype(BF16)
    condition = mm(embedding, time_weight) + mm(one_hot, class_table)
    logistic = jax.nn.sigmoid(condition)
    activated_cond = (condition * logistic).astype(BF16)
    pieces = (mm(activated_cond, ada_weight) + ada_bias).reshape(latents, 6, D)
    meta = jnp.concatenate(
        [heights, widths, jnp.reshape(seq_place * rows_here, (1,))]
    ).astype(jnp.int32)
    kern_attn = conv_attn.astype(F32)
    core = jnp.reshape(batch_place % 2, (1,)).astype(jnp.int32)

    mixed = enter(meta, tokens, top, bot, pieces, kern_attn)
    sent = mixed.reshape(blocks, 1, per_group, D)
    sent = jnp.broadcast_to(sent, (blocks, share, per_group, D)).reshape(seq_count, per_group, D)
    grouped = swap(sent).reshape(group_tokens, D)

    weight_t = qkv_weight.T

    my_block = seq_place // share
    my_latent = my_block // 4
    my_a = (my_block // 2) % 2
    my_b = my_block % 2
    places = jnp.arange(group_tokens, dtype=jnp.int32)
    key_row = places // half * 2 + my_a
    key_col = places % half * 2 + my_b
    height = lax.dynamic_index_in_dim(heights, my_latent, 0, keepdims=False)
    width = lax.dynamic_index_in_dim(widths, my_latent, 0, keepdims=False)
    key_ok = (key_row < height) & (key_col < width)

    margin = half
    tall = per_group + margin
    offset = jnp.stack([margin * (1 - my_a), batch_place % 2]).astype(jnp.int32)
    if share == 1:
        bias = jnp.broadcast_to(jnp.where(key_ok, 0.0, -1e30)[:, None], (group_tokens, 128))
        windows, lse = attend(offset, grouped, qkv_weight, weight_t, bias, seq_count, tall)
        attended = swap(windows)
    else:
        heads = HEADS // share
        wide = heads * HEAD_DIM
        chunk = seq_place % share
        thirds = qkv_weight.reshape(D, 3, share, wide)
        my_weight = lax.dynamic_index_in_dim(thirds, chunk, 2, keepdims=False).reshape(D, 3 * wide)
        att, saved = attend_plain(grouped, my_weight, key_ok, heads)
        windows = windows_of(att, offset[0], margin, seq_count)
        attended = swap(windows).reshape(blocks, share, tall, wide)
        attended = attended.transpose(0, 2, 1, 3).reshape(blocks, tall, D)

    ge, get, cot_split = prepare_cot(cotangent, pieces)
    conditions = lax.all_gather(
        jnp.concatenate([condition, embedding.astype(F32), class_ids.astype(F32)[:, None]], axis=1),
        "batch",
        axis=0,
    )
    if share == 1:
        triple = mm(grouped, qkv_weight).astype(BF16)
        key_t = mm(weight_t[D : 2 * D], grouped, NT).astype(BF16)
        grouped_t = grouped.T
        attended, ge, triple, key_t, grouped_t, conditions = lax.optimization_barrier(
            (attended, ge, triple, key_t, grouped_t, conditions)
        )
    e2, e2t, after_attn, branch = second(
        meta, attended, tokens, top, bot, pieces, proj_weight
    )
    expanded, grad_e2, send_c, keep_c, conv_ffn_part = ffn(
        core, e2, e2t, ge, get, up_weight, down_weight, conv_ffn, cols
    )
    halving = batch_count == 4 and seq_count == 8
    if halving:
        got_c = hop(send_c, "c")
    low = from_before(grad_e2[:, cols * (rows_here + 1) :].astype(BF16), "seq")
    high = from_after(grad_e2[:, :cols].astype(BF16), "seq")
    output, gate_sums = finish_output(expanded, after_attn, cot_split, pieces, rows_here, cols)
    grad_after, grad_branch, grad_attended, mid_sums = middle(
        meta, grad_e2, low, high, after_attn, branch, cot_split, pieces, proj_weight
    )

    att_all = after(attended, grad_attended)
    starts = [margin * ((k // 2) % 2) for k in range(blocks)]
    att_own = jnp.concatenate([att_all[k, at : at + per_group] for k, at in enumerate(starts)])
    flat_branch = grad_branch.reshape(blocks * per_group, D)
    hidden = conv_ffn.shape[1]
    if share == 1:
        gatt = swap(grad_attended.reshape(seq_count, per_group, D)).reshape(group_tokens, D)
        if halving:
            keep_c = after(keep_c, grad_attended)
            sums = add(keep_c, got_c).astype(BF16).reshape(2, 2, 2, 2, 2, D // devices, hidden)
            send_a, keep_a, dims_a = split(sums[0], "yhlx", "y")
            send_b, keep_b, dims_b = split(sums[1], "yhlx", "x")
            late_branch = after(flat_branch, got_c)
            proj_grad = mm(att_own, late_branch, (((0,), (0,)), ((), ()))).astype(BF16)
            send_p, keep_p, _ = split(blocks_of(proj_grad), ORDER, "c")
            got_p = hop(send_p, "c")
            gatt, send_a, send_b, send_p = lax.optimization_barrier((gatt, send_a, send_b, send_p))
            got_a, got_b = hop(send_a, "y"), hop(send_b, "x")
        send_r, keep_r, gm_windows = attend_back(
            offset, triple, key_t, bias, lse, gatt, qkv_weight, grouped_t, seq_count, tall
        )
        gm = swap(gm_windows)
        if halving:
            gm_windows, got_a, got_b = lax.optimization_barrier((gm_windows, got_a, got_b))
        gm = swap(gm_windows)
    else:
        sent = grad_attended.reshape(blocks, per_group, share, wide).transpose(0, 2, 1, 3)
        gatt = swap(sent.reshape(seq_count, per_group, wide)).reshape(group_tokens, wide)
        grad_triple, gm_part = attend_plain_back(saved, gatt, my_weight)
        gm_windows = windows_of(gm_part.astype(BF16), offset[0], margin, seq_count)
        gm = swap(gm_windows).reshape(blocks, share, tall, D)
        gm = jnp.sum(gm.astype(F32), axis=1).astype(BF16)
        own_grad = mm(grouped, grad_triple, (((0,), (0,)), ((), ()))).astype(BF16)
        spread = jnp.zeros((D, 3, share, wide), BF16)
        qkv_grad = lax.dynamic_update_index_in_dim(
            spread, own_grad.reshape(D, 3, wide), chunk, 2
        ).reshape(D, 3 * D)
        proj_grad = mm(att_own, flat_branch, (((0,), (0,)), ((), ()))).astype(BF16)
        rest = jnp.concatenate([qkv_grad, proj_grad], axis=1)

    if halving:
        got_r = hop(send_r, "c")
        keep_a, keep_b = after(keep_a, keep_r), after(keep_b, keep_r)
        send_a, keep_a, dims_a = split(add(keep_a, got_a).astype(BF16), dims_a, "x")
        send_b, keep_b, dims_b = split(add(keep_b, got_b).astype(BF16), dims_b, "y")
        sums = add(keep_r, got_r).astype(BF16).reshape(3, 2, 2, 2, 2, D // devices, D)
        sums_p = add(keep_p, got_p).astype(BF16)
        send_one, keep_one, dims_one = split(sums[:2], "yhlx", "y")
        send_two, keep_two, dims_two = split(jnp.stack([sums[2], sums_p]), "yhlx", "x")
        gm = after(gm, send_a, send_b)
        got_a, got_b = hop(send_a, "x"), hop(send_b, "y")
        got_one, got_two = hop(send_one, "y"), hop(send_two, "x")
    total = batch_count * latents

    here = batch_place * seq_count + seq_place
    own_cols = D // devices
    conditions = conditions.reshape(total, -1)
    condition_all = conditions[:, :D]
    embedding_all = conditions[:, D : D + embedding.shape[1]]
    ids_all = conditions[:, -1].astype(jnp.int32)
    logistic_all = jax.nn.sigmoid(condition_all)
    activated_all = (condition_all * logistic_all).astype(BF16).astype(F32)
    slope_all = logistic_all * (1.0 + condition_all * (1.0 - logistic_all))

    def back_through(grads):
        high = lax.reduce_precision(grads, 8, 7)
        middle_term = lax.reduce_precision(grads - high, 8, 7)
        low = grads - high - middle_term
        product = mm(jnp.concatenate([high, middle_term, low]).astype(BF16), ada_weight, NT)
        return product[:total] + product[total : 2 * total] + product[2 * total :]

    token_grad, conv_attn_part, end_sums = leave(
        meta, gm, tokens, top, bot, grad_after, pieces, kern_attn
    )

    all_sums, (conv_attn_grad, conv_ffn_grad) = sum_and_gather(
        jnp.concatenate([end_sums, mid_sums, gate_sums], axis=1),
        (jnp.sum(conv_attn_part, axis=0), conv_ffn_part),
    )
    if halving:
        keep_a, keep_b, keep_one, keep_two, end_sums = lax.optimization_barrier(
            (keep_a, keep_b, keep_one, keep_two, end_sums)
        )
        pair = jnp.stack([add(keep_a, got_a), add(keep_b, got_b)])
        pair = reduce_rest(pair, dims_a, "lh")
        down_rows, up_rows = pair[0], pair[1]
        send_one, keep_one, dims_one = split(add(keep_one, got_one).astype(BF16), dims_one, "x")
        send_two, keep_two, dims_two = split(add(keep_two, got_two).astype(BF16), dims_two, "y")
        got_one, got_two = hop(send_one, "x"), hop(send_two, "y")
        rest_rows = jnp.concatenate([add(keep_one, got_one), add(keep_two, got_two)])
        rest_rows = reduce_rest(rest_rows, dims_one, "lh")
    else:
        whole = jnp.stack([keep_c, send_c])
        whole = jnp.where(core[0] == 0, whole, whole[::-1]).transpose(1, 2, 0, 3, 4)
        whole = whole.reshape(2, D, hidden)
        down_rows, up_rows = scatter_rows(whole[0]), scatter_rows(whole[1])
        if share == 1:
            rest = jnp.stack([keep_r, send_r])
            rest = jnp.where(core[0] == 0, rest, rest[::-1]).transpose(2, 0, 3, 1, 4).reshape(D, -1)
            proj_grad = mm(att_own, flat_branch, (((0,), (0,)), ((), ()))).astype(BF16)
            rest = jnp.concatenate([rest, proj_grad], axis=1)
        rest_rows = scatter_rows(rest).reshape(own_cols, 4, D).transpose(1, 0, 2)
    qkv_rows = jnp.concatenate([rest_rows[0], rest_rows[1], rest_rows[2]], axis=1)
    proj_rows = rest_rows[3]

    grad_pieces = all_sums.reshape(total, 6 * D)
    grad_silu = back_through(grad_pieces)
    cond_all = grad_silu * slope_all
    cond_grad = lax.dynamic_slice_in_dim(cond_all, batch_place * latents, latents)
    cond_cols = lax.dynamic_slice_in_dim(cond_all, here * own_cols, own_cols, axis=1)
    act_cols = lax.dynamic_slice_in_dim(activated_all, here * own_cols, own_cols, axis=1)
    outer = lambda left, right: lax.dot_general(
        left, right, (((0,), (0,)), ((), ())), precision=HIGHEST, preferred_element_type=F32
    )
    hot_all = (ids_all[:, None] == jnp.arange(class_table.shape[0], dtype=jnp.int32)[None, :]).astype(F32)
    bias_cols = 6 * D // devices
    bias_grad = jnp.sum(
        lax.dynamic_slice_in_dim(grad_pieces, here * bias_cols, bias_cols, axis=1), axis=0
    )
    return (
        output,
        token_grad,
        cond_grad,
        outer(embedding_all, cond_cols),
        outer(hot_all, cond_cols),
        outer(act_cols, grad_pieces),
        bias_grad,
        conv_attn_grad,
        qkv_rows,
        proj_rows,
        up_rows,
        conv_ffn_grad,
        down_rows.T,
    )


def solution(mesh):
    strips = P("batch", "seq", None, None)
    in_specs = (strips, strips) + (P("batch"),) * 4 + (P(),) * 10
    both = ("batch", "seq")
    out_specs = (
        strips,
        strips,
        P("batch", None),
        P(None, both),
        P(None, both),
        P(both, None),
        P(both),
        P(None, both),
        P(both, None),
        P(both, None),
        P(both, None),
        P(None, both),
        P(None, both),
    )
    return jax.shard_map(shards, mesh=mesh, in_specs=in_specs, out_specs=out_specs, check_vma=False)
```

```python
import functools
import math

import jax
import jax.numpy as jnp
from jax import lax
from jax.experimental import pallas as pl
from jax.experimental.pallas import tpu as pltpu
from jax.sharding import PartitionSpec as P

D = 768
HEADS = 12
HEAD_DIM = 64
PAIR = 2 * HEAD_DIM
QUAD = 2 * PAIR
QUADS = HEADS // 4
FF_BLOCK = 256
LANE_PARTS = D // 128
FACTOR = HEAD_DIM ** (-0.5)

F32 = jnp.float32
BF16 = jnp.bfloat16
HIGHEST = lax.Precision.HIGHEST
NN = (((1,), (0,)), ((), ()))
NT = (((1,), (1,)), ((), ()))
VMEM_LIMIT = 60 * 1024 * 1024


def mm(left, right, dims=NN):
    return lax.dot_general(left, right, dims, preferred_element_type=F32)


def shift_down(values):
    rows = lax.broadcasted_iota(jnp.int32, values.shape, 0)
    return jnp.where(rows == 0, 0.0, pltpu.roll(values, 1, 0))


def shift_up(values):
    count = values.shape[0]
    rows = lax.broadcasted_iota(jnp.int32, values.shape, 0)
    return jnp.where(rows == count - 1, 0.0, pltpu.roll(values, count - 1, 0))


def put_shifts(ref, row, parity, values):
    ref[row, 1 + parity] = values
    if parity == 0:
        ref[row, 3] = shift_up(values)
    else:
        ref[row, 0] = shift_down(values)


def normalize(values):
    centre = values - jnp.mean(values, axis=-1, keepdims=True)
    spread = jnp.mean(centre * centre, axis=-1, keepdims=True)
    scaled = lax.rsqrt(spread + 1e-06)
    return centre * scaled, scaled


def norm_back(grad_norm, normed, scaled):
    return scaled * (
        grad_norm
        - jnp.mean(grad_norm, axis=-1, keepdims=True)
        - normed * jnp.mean(grad_norm * normed, axis=-1, keepdims=True)
    )


def put_row(buf, row, values):
    for k in range(LANE_PARTS):
        buf[row, k] = values[:, 128 * k : 128 * (k + 1)]


def get_row(buf, row):
    return jnp.concatenate([buf[row, k] for k in range(LANE_PARTS)], axis=1)


def put_columns(buf, row, parity, values):
    for k in range(LANE_PARTS):
        buf[row, k, pl.ds(parity, values.shape[0], stride=2), :] = values[:, 128 * k : 128 * (k + 1)]


def get_columns(buf, row, parity):
    half = buf.shape[2] // 2
    return jnp.concatenate(
        [buf[row, k, pl.ds(parity, half, stride=2), :] for k in range(LANE_PARTS)], axis=1
    )


def usable_of(meta, latents, latent, row, parity, half):
    cols = 2 * lax.broadcasted_iota(jnp.int32, (half, 1), 0) + parity
    row_ok = jnp.logical_and(row >= 0, row < meta[latent])
    limit = jnp.where(row_ok, meta[latents + latent], 0)
    return (cols < limit).astype(F32)


def sum8(values):
    total = values[0:8]
    for start in range(8, values.shape[0], 8):
        total = total + values[start : start + 8]
    return total


def enter_kernel(meta, tok, top, bot, lead, kern, out, buf, ent):
    latents = pl.num_programs(0)
    latent = pl.program_id(0)
    rows_here, cols = tok.shape[1], tok.shape[2]
    half = cols // 2
    row0 = meta[2 * latents]
    shift = lead[pl.ds(latent, 1), :D]
    scale = 1.0 + lead[pl.ds(latent, 1), D:]
    taps = [kern[t : t + 1, :].astype(F32) for t in range(9)]
    for rr in range(rows_here + 2):
        source = top[0, 0] if rr == 0 else bot[0, 0] if rr == rows_here + 1 else tok[0, rr - 1]
        put_row(buf, rr, source.astype(F32))
        for parity in range(2):
            normed, _ = normalize(get_columns(buf, rr, parity))
            ok = usable_of(meta, latents, latent, row0 + rr - 1, parity, half)
            put_shifts(ent, rr, parity, ((normed * scale + shift) * ok).astype(BF16).astype(F32))
    for row in range(rows_here):
        for parity in range(2):
            total = jnp.zeros((half, D), F32)
            for i in range(3):
                for j in range(3):
                    total = total + ent[row + i, parity + j] * taps[3 * i + j]
            mixed = (ent[row + 1, 1 + parity] + total).astype(BF16)
            group = 2 * (row % 2) + parity
            out[0, group, (row // 2) * half : (row // 2 + 1) * half, :] = mixed


def enter(meta, tokens, top, bot, lead, kern):
    latents, rows_here, cols, _ = tokens.shape
    half = cols // 2
    per_group = rows_here // 2 * half
    whole = lambda *shape: pl.BlockSpec(shape, lambda l, m: (l,) + (0,) * (len(shape) - 1))
    return pl.pallas_call(
        enter_kernel,
        out_shape=jax.ShapeDtypeStruct((latents, 4, per_group, D), BF16),
        grid_spec=pltpu.PrefetchScalarGridSpec(
            num_scalar_prefetch=1,
            grid=(latents,),
            in_specs=[
                whole(1, rows_here, cols, D),
                whole(1, 1, cols, D),
                whole(1, 1, cols, D),
                pl.BlockSpec((latents, 2 * D), lambda l, m: (0, 0)),
                pl.BlockSpec((9, D), lambda l, m: (0, 0)),
            ],
            out_specs=whole(1, 4, per_group, D),
            scratch_shapes=[
                pltpu.VMEM((rows_here + 2, LANE_PARTS, cols, 128), F32),
                pltpu.VMEM((rows_here + 2, 4, half, D), F32),
            ],
        ),
        compiler_params=pltpu.CompilerParams(vmem_limit_bytes=VMEM_LIMIT),
        cost_estimate=pl.CostEstimate(flops=6_000_000_000, bytes_accessed=4_000_000, transcendentals=0),
        name="enter",
    )(meta, tokens, top, bot, lead, kern)


def cot_kernel(cot, pieces, ge_out, get_out, cot_out, buf):
    rows_here, cols = cot.shape[1], cot.shape[2]
    half = cols // 2
    gate = pieces[0, 5:6, :]
    for row in range(rows_here):
        put_row(buf, row, cot[0, row].astype(F32))
        for parity in range(2):
            values = get_columns(buf, row, parity)
            at = (2 * row + parity) * half
            ge_out[0, at : at + half, :] = (gate * values).astype(BF16)
            cot_out[0, at : at + half, :] = values.astype(BF16)
    get_out[0] = ge_out[0].astype(F32).T.astype(BF16)


def prepare_cot(cotangent, pieces):
    latents, rows_here, cols, _ = cotangent.shape
    whole = lambda *shape: pl.BlockSpec(shape, lambda l: (l,) + (0,) * (len(shape) - 1))
    own = rows_here * cols
    return pl.pallas_call(
        cot_kernel,
        out_shape=(
            jax.ShapeDtypeStruct((latents, own, D), BF16),
            jax.ShapeDtypeStruct((latents, D, own), BF16),
            jax.ShapeDtypeStruct((latents, own, D), BF16),
        ),
        grid=(latents,),
        in_specs=[whole(1, rows_here, cols, D), whole(1, 6, D)],
        out_specs=(whole(1, own, D), whole(1, D, own), whole(1, own, D)),
        scratch_shapes=[pltpu.VMEM((rows_here, LANE_PARTS, cols, 128), F32)],
        compiler_params=pltpu.CompilerParams(vmem_limit_bytes=VMEM_LIMIT),
        cost_estimate=pl.CostEstimate(flops=4_000_000_000, bytes_accessed=4_000_000, transcendentals=0),
        name="prepare_cot",
    )(cotangent, pieces)


def second_kernel(meta, att, tok, top, bot, pieces, proj, e2_out, e2t_out, after_out, branch_out, buf, bran):
    latents = pl.num_programs(0)
    latent = pl.program_id(0)
    rows_here, cols = tok.shape[1], tok.shape[2]
    half = cols // 2
    row0 = meta[2 * latents]
    gate = pieces[0, 2:3, :]
    shift = pieces[0, 3:4, :]
    scale = 1.0 + pieces[0, 4:5, :]
    for group in range(4):
        bran[group] = mm(att[group], proj[...])
    for rr in range(rows_here + 2):
        source = top[0, 0] if rr == 0 else bot[0, 0] if rr == rows_here + 1 else tok[0, rr - 1]
        put_row(buf, rr, source.astype(F32))
        for parity in range(2):
            group = 2 * ((rr + 1) % 2) + parity
            branch = bran[group, (rr // 2) * half : (rr // 2 + 1) * half, :]
            after = get_columns(buf, rr, parity) + gate * branch
            normed, _ = normalize(after)
            ok = usable_of(meta, latents, latent, row0 + rr - 1, parity, half)
            at = (2 * rr + parity) * half
            e2_out[0, at : at + half, :] = ((normed * scale + shift) * ok).astype(BF16)
            if 1 <= rr <= rows_here:
                own = at - cols
                after_out[0, own : own + half, :] = after
                branch_out[0, own : own + half, :] = branch
    e2t_out[0] = e2_out[0].astype(F32).T.astype(BF16)


def second(meta, attended, tokens, top, bot, pieces, proj):
    latents, rows_here, cols, _ = tokens.shape
    own = rows_here * cols
    wide = attended.shape[1]
    whole = lambda *shape: pl.BlockSpec(shape, lambda l, m: (l,) + (0,) * (len(shape) - 1))
    return pl.pallas_call(
        second_kernel,
        out_shape=(
            jax.ShapeDtypeStruct((latents, own + 2 * cols, D), BF16),
            jax.ShapeDtypeStruct((latents, D, own + 2 * cols), BF16),
            jax.ShapeDtypeStruct((latents, own, D), F32),
            jax.ShapeDtypeStruct((latents, own, D), F32),
        ),
        grid_spec=pltpu.PrefetchScalarGridSpec(
            num_scalar_prefetch=1,
            grid=(latents,),
            in_specs=[
                whole(4, wide, D),
                whole(1, rows_here, cols, D),
                whole(1, 1, cols, D),
                whole(1, 1, cols, D),
                whole(1, 6, D),
                pl.BlockSpec((D, D), lambda l, m: (0, 0)),
            ],
            out_specs=(
                whole(1, own + 2 * cols, D),
                whole(1, D, own + 2 * cols),
                whole(1, own, D),
                whole(1, own, D),
            ),
            scratch_shapes=[
                pltpu.VMEM((rows_here + 2, LANE_PARTS, cols, 128), F32),
                pltpu.VMEM((4, wide, D), F32),
            ],
        ),
        compiler_params=pltpu.CompilerParams(vmem_limit_bytes=VMEM_LIMIT),
        cost_estimate=pl.CostEstimate(flops=7_000_000_000, bytes_accessed=4_000_000, transcendentals=0),
        name="second",
    )(meta, attended, tokens, top, bot, pieces, proj)


def normal_parts(values):
    density = jnp.exp2(values * values * -0.7213475204444817 - 1.3257480647361592)
    t = 1.0 / (1.0 + 0.2316419 * jnp.abs(values))
    series = t * (
        0.319381530
        + t * (-0.356563782 + t * (1.781477937 + t * (-1.821255978 + t * 1.330274429)))
    )
    tail = density * series
    return jnp.where(values > 0.0, 1.0 - tail, tail), density


def ffn_kernel(core, e2, e2t, ge, get, up, down, kern_in, exp_out, ge2_out, first_out, last_out, send_out, keep_out, kern_out, *scratch):
    latents = e2.shape[0]
    lifted, gact, gconv, act, graised = [scratch[k * latents : (k + 1) * latents] for k in range(5)]
    down_acc, up_acc = scratch[5 * latents :]
    step = pl.program_id(0)
    half = lifted[0].shape[2]
    rows_here = gconv[0].shape[0]
    block = lifted[0].shape[3]
    chunks = block // 128
    lanes = [slice(c * 128, (c + 1) * 128) for c in range(chunks)]
    taps = [[kern_in[t : t + 1, cut].astype(F32) for t in range(9)] for cut in lanes]
    sums = [[jnp.zeros((8, 128), F32) for _ in range(9)] for _ in range(chunks)]
    lift_rows = 3

    def put(ref, row, parity, cut, values):
        ref[row, 1 + parity, :, cut] = values
        if parity == 0:
            ref[row, 3, :, cut] = shift_up(values)
        else:
            ref[row, 0, :, cut] = shift_down(values)

    def lift(latent, part):
        size = lift_rows * 2 * half
        raised = mm(e2[latent, part * size : (part + 1) * size], up[...])
        for k in range(lift_rows):
            for parity in range(2):
                at = (2 * k + parity) * half
                for cut in lanes:
                    put(lifted[latent], part * lift_rows + k, parity, cut, raised[at : at + half, cut])

    def pull(latent):
        gact[latent][...] = mm(ge[latent], down[...], NT)

    def bend(latent, row, c):
        cut = lanes[c]
        for parity in range(2):
            total = None
            for i in range(3):
                for j in range(3):
                    term = lifted[latent][row + i, parity + j, :, cut] * taps[c][3 * i + j]
                    total = term if total is None else total + term
            cdf, density = normal_parts(total)
            at = (2 * row + parity) * half
            act[latent][at : at + half, cut] = (total * cdf).astype(BF16)
            grad = gact[latent][at : at + half, cut] * (cdf + total * density)
            put(gconv[latent], row, parity, cut, grad)

    def unbend(latent, rr, c):
        cut = lanes[c]
        for parity in range(2):
            total = None
            for i in range(3):
                row = rr - i
                if not 0 <= row < rows_here:
                    continue
                for j in range(3):
                    term = gconv[latent][row, parity + 2 - j, :, cut] * taps[c][3 * i + j]
                    total = term if total is None else total + term
            at = (2 * rr + parity) * half
            graised[latent][at : at + half, cut] = total.astype(BF16)
            if rr < rows_here:
                here = gconv[latent][rr, 1 + parity, :, cut]
                for i in range(3):
                    for j in range(3):
                        t = 3 * i + j
                        part = lifted[latent][rr + i, parity + j, :, cut] * here
                        sums[c][t] = sums[c][t] + sum8(part)

    def expand(latent):
        exp_out[latent] += mm(act[latent][...], down[...])

    def lower(latent):
        ge2_out[latent] += mm(graised[latent][...], up[...], NT)

    def weigh_down(latent):
        value = mm(get[latent], act[latent][...])
        down_acc[...] = value if latent == 0 else down_acc[...] + value

    def weigh_up(latent):
        value = mm(e2t[latent], graised[latent][...])
        up_acc[...] = value if latent == 0 else up_acc[...] + value

    @pl.when(step == 0)
    def _():
        exp_out[...] = jnp.zeros_like(exp_out)
        ge2_out[...] = jnp.zeros_like(ge2_out)

    def mix(work, more):
        stride = max(1, len(work) // max(1, len(more)))
        for k, unit in enumerate(work):
            if k % stride == 0 and k // stride < len(more):
                more[k // stride]()
            unit()
        for unit in more[-(-len(work) // stride) :]:
            unit()

    part = functools.partial
    lifts = (rows_here + 2) // lift_rows
    for k in range(lifts):
        lift(0, k)
    pull(0)
    for latent in range(latents):
        bends = [part(bend, latent, row, c) for c in range(chunks) for row in range(rows_here)]
        unbends = [part(unbend, latent, rr, c) for c in range(chunks) for rr in range(rows_here + 2)]
        first, then = [], [part(expand, latent), part(weigh_down, latent)]
        if latent > 0:
            first += [part(lower, latent - 1), part(weigh_up, latent - 1)]
        if latent + 1 < latents:
            first += [part(lift, latent + 1, k) for k in range(lifts)] + [part(pull, latent + 1)]
        mix(bends, first)
        mix(unbends, then)
    lower(latents - 1)
    weigh_up(latents - 1)

    @pl.when(step == pl.num_programs(0) - 1)
    def _():
        first_out[...] = ge2_out[:, : 2 * half].astype(BF16)
        last_out[...] = ge2_out[:, 2 * half * (rows_here + 1) :].astype(BF16)

    size = down_acc.shape[0] // 4
    for which, acc in enumerate((down_acc, up_acc)):
        for y in range(2):
            mine = pl.multiple_of((2 * y + core[0]) * size, 8)
            other = pl.multiple_of((2 * y + 1 - core[0]) * size, 8)
            keep_out[which, y] = acc[pl.ds(mine, size), :].astype(BF16)
            send_out[which, y] = acc[pl.ds(other, size), :].astype(BF16)
    for c, cut in enumerate(lanes):
        for t in range(9):
            kern_out[t : t + 1, cut] = jnp.sum(sums[c][t], axis=0, keepdims=True)


def ffn(core, e2, e2t, ge, get, up, down, kern, cols):
    latents, wide, _ = e2.shape
    half = cols // 2
    own = ge.shape[1]
    rows_here = own // cols
    hidden = up.shape[1]
    fixed = lambda *shape: pl.BlockSpec(shape, lambda f, c: (0,) * len(shape))
    parts = jax.ShapeDtypeStruct((2, 2, D // 4, hidden), BF16)
    parts_spec = pl.BlockSpec((2, 2, D // 4, FF_BLOCK), lambda f, c: (0, 0, 0, f))
    each = lambda *args: [pltpu.VMEM(*args)] * latents
    return pl.pallas_call(
        ffn_kernel,
        out_shape=(
            jax.ShapeDtypeStruct((latents, own, D), F32),
            jax.ShapeDtypeStruct((latents, wide, D), F32),
            jax.ShapeDtypeStruct((latents, cols, D), BF16),
            jax.ShapeDtypeStruct((latents, cols, D), BF16),
            parts,
            parts,
            jax.ShapeDtypeStruct((9, hidden), F32),
        ),
        grid_spec=pltpu.PrefetchScalarGridSpec(
            num_scalar_prefetch=1,
            grid=(hidden // FF_BLOCK,),
            in_specs=[
                fixed(latents, wide, D),
                fixed(latents, D, wide),
                fixed(latents, own, D),
                fixed(latents, D, own),
                pl.BlockSpec((D, FF_BLOCK), lambda f, c: (0, f)),
                pl.BlockSpec((FF_BLOCK, D), lambda f, c: (f, 0)),
                pl.BlockSpec((9, FF_BLOCK), lambda f, c: (0, f)),
            ],
            out_specs=(
                fixed(latents, own, D),
                fixed(latents, wide, D),
                fixed(latents, cols, D),
                fixed(latents, cols, D),
                parts_spec,
                parts_spec,
                pl.BlockSpec((9, FF_BLOCK), lambda f, c: (0, f)),
            ),
            scratch_shapes=each((rows_here + 2, 4, half, FF_BLOCK), F32)
            + each((own, FF_BLOCK), F32)
            + each((rows_here, 4, half, FF_BLOCK), F32)
            + each((own, FF_BLOCK), BF16)
            + each((wide, FF_BLOCK), BF16)
            + [pltpu.VMEM((D, FF_BLOCK), F32), pltpu.VMEM((D, FF_BLOCK), F32)],
        ),
        compiler_params=pltpu.CompilerParams(vmem_limit_bytes=VMEM_LIMIT),
        cost_estimate=pl.CostEstimate(flops=35_000_000_000, bytes_accessed=4_000_000, transcendentals=0),
        name="ffn",
    )(core, e2, e2t, ge, get, up, down, kern)


def output_kernel(exp, after_in, cot_in, pieces, out, sum_out, buf):
    rows_here, cols = out.shape[1], out.shape[2]
    half = cols // 2
    gate = pieces[0, 5:6, :]
    total = jnp.zeros((8, D), F32)
    for row in range(rows_here):
        for parity in range(2):
            part = pl.ds((2 * row + parity) * half, half)
            expanded = exp[0, part, :]
            put_columns(buf, row, parity, after_in[0, part, :] + gate * expanded)
            total = total + sum8(cot_in[0, part, :].astype(F32) * expanded)
        out[0, row] = get_row(buf, row).astype(BF16)
    sum_out[0] = jnp.sum(total, axis=0, keepdims=True)


def finish_output(exp, after, cot, pieces, rows_here, cols):
    latents, own, _ = exp.shape
    whole = lambda *shape: pl.BlockSpec(shape, lambda l: (l,) + (0,) * (len(shape) - 1))
    return pl.pallas_call(
        output_kernel,
        out_shape=(
            jax.ShapeDtypeStruct((latents, rows_here, cols, D), BF16),
            jax.ShapeDtypeStruct((latents, 1, D), F32),
        ),
        grid=(latents,),
        in_specs=[whole(1, own, D), whole(1, own, D), whole(1, own, D), whole(1, 6, D)],
        out_specs=(whole(1, rows_here, cols, D), whole(1, 1, D)),
        scratch_shapes=[pltpu.VMEM((rows_here, LANE_PARTS, cols, 128), F32)],
        compiler_params=pltpu.CompilerParams(vmem_limit_bytes=VMEM_LIMIT),
        cost_estimate=pl.CostEstimate(flops=5_000_000_000, bytes_accessed=4_000_000, transcendentals=0),
        name="finish_output",
    )(exp, after, cot, pieces)


def middle_kernel(meta, ge2, low, high, after_in, branch_in, cot_in, pieces, proj, after_grad, gb_out, gatt_out, sums_out):
    latents = pl.num_programs(0)
    latent = pl.program_id(0)
    own = after_in.shape[1]
    cols = low.shape[1]
    rows_here = own // cols
    half = cols // 2
    row0 = meta[2 * latents]
    gate_one = pieces[0, 2:3, :]
    scale = 1.0 + pieces[0, 4:5, :]
    sums = [jnp.zeros((8, D), F32) for _ in range(3)]
    for row in range(rows_here):
        for parity in range(2):
            at = (2 * row + parity) * half
            part = pl.ds(at, half)
            side = pl.ds(parity * half, half)
            after = after_in[0, part, :]
            cot = cot_in[0, part, :].astype(F32)
            normed, scaled = normalize(after)
            ok = usable_of(meta, latents, latent, row0 + row, parity, half)
            grad = ge2[0, pl.ds(at + cols, half), :]
            if row == 0:
                grad = grad + low[0, side, :].astype(F32)
            if row == rows_here - 1:
                grad = grad + high[0, side, :].astype(F32)
            grad = grad * ok
            grad_after = cot + norm_back(grad * scale, normed, scaled)
            after_grad[0, part, :] = grad_after
            sums[0] = sums[0] + sum8(grad_after * branch_in[0, part, :])
            sums[1] = sums[1] + sum8(grad)
            sums[2] = sums[2] + sum8(grad * normed)
            group = 2 * (row % 2) + parity
            to = pl.ds((row // 2) * half, half)
            gb_out[0, group, to, :] = (gate_one * grad_after).astype(BF16)
    for k in range(3):
        sums_out[0, k : k + 1, :] = jnp.sum(sums[k], axis=0, keepdims=True)
    for group in range(4):
        gatt_out[0, group] = mm(gb_out[0, group], proj[...], NT).astype(BF16)


def middle(meta, ge2, low, high, after, branch, cot, pieces, proj):
    latents, own, _ = after.shape
    wide, cols = ge2.shape[1], low.shape[1]
    per_group = own // 4
    whole = lambda *shape: pl.BlockSpec(shape, lambda l, m: (l,) + (0,) * (len(shape) - 1))
    return pl.pallas_call(
        middle_kernel,
        out_shape=(
            jax.ShapeDtypeStruct((latents, own, D), F32),
            jax.ShapeDtypeStruct((latents, 4, per_group, D), BF16),
            jax.ShapeDtypeStruct((latents, 4, per_group, D), BF16),
            jax.ShapeDtypeStruct((latents, 3, D), F32),
        ),
        grid_spec=pltpu.PrefetchScalarGridSpec(
            num_scalar_prefetch=1,
            grid=(latents,),
            in_specs=[
                whole(1, wide, D),
                whole(1, cols, D),
                whole(1, cols, D),
                whole(1, own, D),
                whole(1, own, D),
                whole(1, own, D),
                whole(1, 6, D),
                pl.BlockSpec((D, D), lambda l, m: (0, 0)),
            ],
            out_specs=(
                whole(1, own, D),
                whole(1, 4, per_group, D),
                whole(1, 4, per_group, D),
                whole(1, 3, D),
            ),
        ),
        compiler_params=pltpu.CompilerParams(vmem_limit_bytes=VMEM_LIMIT),
        cost_estimate=pl.CostEstimate(flops=8_000_000_000, bytes_accessed=4_000_000, transcendentals=0),
        name="middle",
    )(meta, ge2, low, high, after, branch, cot, pieces, proj)


def leave_kernel(meta, gm, tok, top, bot, after_grad, pieces, kern, out, kern_out, sums_out, buf, ent, gmx, obuf, nbuf, sbuf, tot):
    latents = pl.num_programs(0)
    latent = pl.program_id(0)
    rows_here, cols = tok.shape[1], tok.shape[2]
    half = cols // 2
    row0 = meta[2 * latents]
    shift = pieces[0, 0:1, :]
    scale = 1.0 + pieces[0, 1:2, :]
    taps = [kern[t : t + 1, :].astype(F32) for t in range(9)]
    put_row(buf, 0, top[0, 0].astype(F32))
    for row in range(rows_here):
        put_row(buf, row + 1, tok[0, row].astype(F32))
    put_row(buf, rows_here + 1, bot[0, 0].astype(F32))

    def take(rr, carry):
        at = pl.multiple_of(rr // 2 * half, half)
        for parity in range(2):
            normed, scaled = normalize(get_columns(buf, rr, parity))
            nbuf[rr, parity] = normed
            sbuf[rr, parity] = jnp.broadcast_to(scaled, (half, 128))
            ok = usable_of(meta, latents, latent, row0 + rr - 1, parity, half)
            put_shifts(ent, rr, parity, (normed * scale + shift) * ok)
            group = 2 * ((rr + 1) % 2) + parity
            put_shifts(gmx, rr, parity, gm[group, pl.ds(at, half), :].astype(F32))
        return carry

    lax.fori_loop(0, rows_here + 2, take, 0)
    tot[...] = jnp.zeros_like(tot)

    def give(row, carry):
        for parity in range(2):
            here = gmx[row + 1, 1 + parity]
            total = here
            for i in range(3):
                for j in range(3):
                    t = 3 * i + j
                    total = total + gmx[row + 2 - i, parity + 2 - j] * taps[t]
                    tot[t] += sum8(ent[row + i, parity + j] * here)
            ok = usable_of(meta, latents, latent, row0 + row, parity, half)
            grad = total * ok
            normed, scaled = nbuf[row + 1, parity], sbuf[row + 1, parity, :, 0:1]
            tot[9] += sum8(grad)
            tot[10] += sum8(grad * normed)
            at = pl.multiple_of((2 * row + parity) * half, half)
            back = after_grad[0, pl.ds(at, half), :] + norm_back(grad * scale, normed, scaled)
            put_columns(obuf, row, parity, back)
        out[0, row] = get_row(obuf, row)
        return carry

    lax.fori_loop(0, rows_here, give, 0)
    for t in range(9):
        kern_out[0, t : t + 1, :] = jnp.sum(tot[t], axis=0, keepdims=True)
    for k in range(2):
        sums_out[0, k : k + 1, :] = jnp.sum(tot[9 + k], axis=0, keepdims=True)


def leave(meta, gm, tokens, top, bot, after_grad, pieces, kern):
    latents, rows_here, cols, _ = tokens.shape
    half = cols // 2
    own = rows_here * cols
    wide = gm.shape[1]
    whole = lambda *shape: pl.BlockSpec(shape, lambda l, m: (l,) + (0,) * (len(shape) - 1))
    return pl.pallas_call(
        leave_kernel,
        out_shape=(
            jax.ShapeDtypeStruct((latents, rows_here, cols, D), F32),
            jax.ShapeDtypeStruct((latents, 9, D), F32),
            jax.ShapeDtypeStruct((latents, 2, D), F32),
        ),
        grid_spec=pltpu.PrefetchScalarGridSpec(
            num_scalar_prefetch=1,
            grid=(latents,),
            in_specs=[
                whole(4, wide, D),
                whole(1, rows_here, cols, D),
                whole(1, 1, cols, D),
                whole(1, 1, cols, D),
                whole(1, own, D),
                whole(1, 6, D),
                pl.BlockSpec((9, D), lambda l, m: (0, 0)),
            ],
            out_specs=(whole(1, rows_here, cols, D), whole(1, 9, D), whole(1, 2, D)),
            scratch_shapes=[
                pltpu.VMEM((rows_here + 2, LANE_PARTS, cols, 128), F32),
                pltpu.VMEM((rows_here + 2, 4, half, D), F32),
                pltpu.VMEM((rows_here + 2, 4, half, D), F32),
                pltpu.VMEM((rows_here, LANE_PARTS, cols, 128), F32),
                pltpu.VMEM((rows_here + 2, 2, half, D), F32),
                pltpu.VMEM((rows_here + 2, 2, half, 128), F32),
                pltpu.VMEM((11, 8, D), F32),
            ],
        ),
        compiler_params=pltpu.CompilerParams(vmem_limit_bytes=VMEM_LIMIT),
        cost_estimate=pl.CostEstimate(flops=10_000_000_000, bytes_accessed=4_000_000, transcendentals=0),
        name="leave",
    )(meta, gm, tokens, top, bot, after_grad, pieces, kern)


def pair_parts(values):
    lanes = lax.broadcasted_iota(jnp.int32, values.shape, 1)
    first = lanes < HEAD_DIM
    zero = jnp.zeros_like(values)
    return jnp.where(first, values, zero), jnp.where(first, zero, values)


def attend_kernel(offset, mixed, wq, wk, wvt, bias, out, lse_out, padded):
    tokens = mixed.shape[0]
    strips, window, _ = out.shape
    step = tokens // strips
    margin = window - step
    m = mixed[...]
    query = (mm(m, wq[...]).astype(BF16) * FACTOR).astype(BF16)
    key = mm(m, wk[...]).astype(BF16)
    value_t = mm(wvt[...], m, NT).astype(BF16)
    keep = jnp.tile(bias[...], (1, tokens // 128))

    def score(h):
        cut = slice(h // 2 * PAIR, (h // 2 + 1) * PAIR)
        return mm(pair_parts(key[:, cut])[h % 2], query[:, cut], NT)

    scores = {0: score(0), 1: score(1)}
    parts = []
    for h in range(4):
        masked = scores.pop(h) + keep
        peak = jnp.max(masked, axis=0, keepdims=True)
        raw = jnp.exp(masked - peak)
        if h + 2 < 4:
            scores[h + 2] = score(h + 2)
        total = jnp.sum(raw, axis=0, keepdims=True)
        prob = (raw * (1.0 / total)).astype(BF16)
        parts.append(mm(value_t[h * HEAD_DIM : (h + 1) * HEAD_DIM], prob))
        lse_out[0, h : h + 1, :] = peak + jnp.log(total)
    padded[0:margin] = jnp.zeros((margin, QUAD), F32)
    padded[margin + tokens :] = jnp.zeros((margin, QUAD), F32)
    padded[margin : margin + tokens] = jnp.concatenate(parts, axis=0).T
    for s in range(strips):
        start = pl.multiple_of(offset[0] + s * step, 8)
        out[s] = padded[pl.ds(start, window), :].astype(BF16)


def attend(offset, mixed, weight, weight_t, bias, strips, window):
    tokens = mixed.shape[0]
    margin = window - tokens // strips
    return pl.pallas_call(
        attend_kernel,
        out_shape=(
            jax.ShapeDtypeStruct((strips, window, D), BF16),
            jax.ShapeDtypeStruct((QUADS, 4, tokens), F32),
        ),
        grid_spec=pltpu.PrefetchScalarGridSpec(
            num_scalar_prefetch=1,
            grid=(QUADS,),
            in_specs=[
                pl.BlockSpec((tokens, D), lambda p, o: (0, 0)),
                pl.BlockSpec((D, QUAD), lambda p, o: (0, p)),
                pl.BlockSpec((D, QUAD), lambda p, o: (0, QUADS + p)),
                pl.BlockSpec((QUAD, D), lambda p, o: (2 * QUADS + p, 0)),
                pl.BlockSpec((tokens, 128), lambda p, o: (0, 0)),
            ],
            out_specs=(
                pl.BlockSpec((strips, window, QUAD), lambda p, o: (0, 0, p)),
                pl.BlockSpec((1, 4, tokens), lambda p, o: (p, 0, 0)),
            ),
            scratch_shapes=[pltpu.VMEM((tokens + 2 * margin, QUAD), F32)],
        ),
        compiler_params=pltpu.CompilerParams(vmem_limit_bytes=VMEM_LIMIT),
        cost_estimate=pl.CostEstimate(flops=16_000_000_000, bytes_accessed=4_000_000, transcendentals=0),
        name="attend",
    )(offset, mixed, weight, weight, weight_t, bias)


def attend_back_kernel(offset, query, key, value, key_t, bias, lse, gatt, wq, wk, wv, mixed_t, send_out, keep_out, gm_out, acc, part):
    tokens = query.shape[0]
    strips, window, _ = gm_out.shape
    step = tokens // strips
    margin = window - step
    p = pl.program_id(0)
    keep = jnp.tile(bias[...], (1, tokens // 128))

    def pair(k):
        cut = slice(k * PAIR, (k + 1) * PAIR)
        q, grad = query[:, cut], gatt[:, cut]
        keys, values = pair_parts(key[:, cut]), pair_parts(value[:, cut])
        return [(mm(keys[e], q, NT), mm(values[e], grad, NT)) for e in range(2)]

    def soften(k, e, score, grad_prob):
        h = 2 * k + e
        prob = jnp.exp(score * FACTOR + keep - lse[0, h : h + 1, :])
        delta = jnp.sum(prob * grad_prob, axis=0, keepdims=True)
        return prob.astype(BF16), (prob * (grad_prob - delta)).astype(BF16)

    def finish(k, probs, grad_scores):
        cut = slice(k * PAIR, (k + 1) * PAIR)
        queries, grads = pair_parts(query[:, cut]), pair_parts(gatt[:, cut])
        dv = mm(jnp.concatenate(probs, axis=1), jnp.concatenate(grads, axis=0))
        dk = mm(jnp.concatenate(grad_scores, axis=1), jnp.concatenate(queries, axis=0)) * FACTOR
        rows = [key_t[(2 * k + e) * HEAD_DIM : (2 * k + e + 1) * HEAD_DIM] for e in range(2)]
        parts = [mm(rows[e], grad_scores[e]) for e in range(2)]
        dq = jnp.concatenate(parts, axis=0).T * FACTOR
        return dq.astype(BF16), dk.astype(BF16), dv.astype(BF16)

    first = pair(0)
    soft = [soften(0, e, *first[e]) for e in range(2)]
    then = pair(1)
    one = finish(0, [v[0] for v in soft], [v[1] for v in soft])
    soft = [soften(1, e, *then[e]) for e in range(2)]
    two = finish(1, [v[0] for v in soft], [v[1] for v in soft])
    all_three = jnp.concatenate([v for k in range(3) for v in (one[k], two[k])], axis=1)
    part[...] = mm(mixed_t[...], all_three)
    size = D // 4
    for y in range(2):
        mine = pl.multiple_of((2 * y + offset[1]) * size, 8)
        other = pl.multiple_of((2 * y + 1 - offset[1]) * size, 8)
        for k in range(3):
            cut = slice(k * QUAD, (k + 1) * QUAD)
            keep_out[k, y] = part[pl.ds(mine, size), cut].astype(BF16)
            send_out[k, y] = part[pl.ds(other, size), cut].astype(BF16)
    total = mm(all_three, jnp.concatenate([wq[...], wk[...], wv[...]], axis=1), NT)

    @pl.when(p == 0)
    def _():
        acc[0:margin] = jnp.zeros((margin, D), F32)
        acc[margin + tokens :] = jnp.zeros((margin, D), F32)
        acc[margin : margin + tokens] = total

    @pl.when(p > 0)
    def _():
        acc[margin : margin + tokens] += total

    @pl.when(p == pl.num_programs(0) - 1)
    def _():
        for s in range(strips):
            start = pl.multiple_of(offset[0] + s * step, 8)
            gm_out[s] = acc[pl.ds(start, window), :].astype(BF16)


def attend_back(offset, triple, key_t, bias, lse, gatt, weight, mixed_t, strips, window):
    tokens = triple.shape[0]
    margin = window - tokens // strips
    part = lambda k: pl.BlockSpec((tokens, QUAD), lambda p, o: (0, k * QUADS + p))
    slab = lambda k: pl.BlockSpec((D, QUAD), lambda p, o: (0, k * QUADS + p))
    parts = jax.ShapeDtypeStruct((3, 2, D // 4, D), BF16)
    parts_spec = pl.BlockSpec((3, 2, D // 4, QUAD), lambda p, o: (0, 0, 0, p))
    return pl.pallas_call(
        attend_back_kernel,
        out_shape=(
            parts,
            parts,
            jax.ShapeDtypeStruct((strips, window, D), BF16),
        ),
        grid_spec=pltpu.PrefetchScalarGridSpec(
            num_scalar_prefetch=1,
            grid=(QUADS,),
            in_specs=[
                part(0),
                part(1),
                part(2),
                pl.BlockSpec((QUAD, tokens), lambda p, o: (p, 0)),
                pl.BlockSpec((tokens, 128), lambda p, o: (0, 0)),
                pl.BlockSpec((1, 4, tokens), lambda p, o: (p, 0, 0)),
                part(0),
                slab(0),
                slab(1),
                slab(2),
                pl.BlockSpec((D, tokens), lambda p, o: (0, 0)),
            ],
            out_specs=(
                parts_spec,
                parts_spec,
                pl.BlockSpec((strips, window, D), lambda p, o: (0, 0, 0)),
            ),
            scratch_shapes=[
                pltpu.VMEM((tokens + 2 * margin, D), F32),
                pltpu.VMEM((D, 3 * QUAD), F32),
            ],
        ),
        compiler_params=pltpu.CompilerParams(vmem_limit_bytes=VMEM_LIMIT),
        cost_estimate=pl.CostEstimate(flops=23_000_000_000, bytes_accessed=4_000_000, transcendentals=0),
        name="attend_back",
    )(offset, triple, triple, triple, key_t, bias, lse, gatt, weight, weight, weight, mixed_t)


def from_before(values, axis):
    count = lax.axis_size(axis)
    return lax.ppermute(values, axis, [(i, i + 1) for i in range(count - 1)])


def from_after(values, axis):
    count = lax.axis_size(axis)
    return lax.ppermute(values, axis, [(i + 1, i) for i in range(count - 1)])


def swap(values):
    return lax.all_to_all(values, "seq", 0, 0, tiled=False)


BITS = {"y": ("batch", 2), "c": ("batch", 1), "h": ("seq", 4), "l": ("seq", 2), "x": ("seq", 1)}
ORDER = "ychlx"


def blocks_of(values):
    return values.reshape(values.shape[:-2] + (2, 2, 2, 2, 2, values.shape[-2] // 32, values.shape[-1]))


def split(values, dims, bit):
    axis, mask = BITS[bit]
    mine = (lax.axis_index(axis) // mask) % 2
    at = values.ndim - 2 - len(dims) + dims.index(bit)
    send = lax.dynamic_index_in_dim(values, 1 - mine, at, keepdims=False)
    keep = lax.dynamic_index_in_dim(values, mine, at, keepdims=False)
    return send, keep, dims.replace(bit, "")


def hop(values, bit):
    axis, mask = BITS[bit]
    count = lax.axis_size(axis)
    return lax.ppermute(values, axis, [(i, i ^ mask) for i in range(count)])


def add(keep, got):
    return keep.astype(F32) + got.astype(F32)


def after(values, *others):
    return lax.optimization_barrier((values,) + others)[0]


def reduce_rest(values, dims, order):
    for bit in order:
        send, keep, dims = split(values.astype(BF16), dims, bit)
        values = add(keep, hop(send, bit))
    return values


def scatter_rows(values):
    return lax.psum_scatter(values, ("batch", "seq"), scatter_dimension=0, tiled=True).astype(F32)


def payload_of(common, sliced):
    seq_count, batch_count = lax.axis_size("seq"), lax.axis_size("batch")
    flat = common.reshape(1, -1)
    pieces = [jnp.broadcast_to(flat, (seq_count, flat.shape[1]))]
    for values in sliced:
        cut = values.reshape(values.shape[0], batch_count, seq_count, -1).transpose(2, 1, 0, 3)
        pieces.append(cut.reshape(seq_count, -1))
    whole = jnp.concatenate(pieces, axis=1)
    return jnp.pad(whole, ((0, 0), (0, -whole.shape[1] % 1024))).reshape(seq_count, -1, 128)


def unpack(gathered, common, sliced):
    seq_count, batch_count = lax.axis_size("seq"), lax.axis_size("batch")
    gathered = gathered.reshape(batch_count, -1)
    at = common.size
    common_all = gathered[:, :at].reshape((batch_count,) + common.shape)
    own = []
    for values in sliced:
        size = values.size // seq_count
        part = jnp.sum(gathered[:, at : at + size], axis=0)
        part = part.reshape(batch_count, values.shape[0], -1)
        own.append(lax.dynamic_index_in_dim(part, lax.axis_index("batch"), 0, keepdims=False))
        at += size
    return common_all, own


def windows_of(values, offset, margin, strips):
    step = values.shape[0] // strips
    padded = jnp.pad(values, ((margin, margin), (0, 0)))
    base = lax.dynamic_slice_in_dim(padded, offset, values.shape[0] + margin)
    return jnp.stack([base[s * step : s * step + step + margin] for s in range(strips)])


def attend_plain(mixed, weight, ok, heads):
    wide = heads * HEAD_DIM
    triple = mm(mixed, weight).astype(BF16)
    split = lambda k: triple[:, k * wide : (k + 1) * wide].reshape(-1, heads, HEAD_DIM)
    queries, keys, values = split(0), split(1), split(2)
    scores = jnp.einsum("qhe,khe->hqk", queries, keys, preferred_element_type=F32) * FACTOR
    scores = jnp.where(ok[None, None, :], scores, -1e30)
    prob = jax.nn.softmax(scores, axis=-1)
    out = jnp.einsum("hqk,khe->qhe", prob.astype(BF16), values, preferred_element_type=F32)
    return out.reshape(-1, wide).astype(BF16), (queries, keys, values, prob)


def attend_plain_back(saved, grad, weight):
    queries, keys, values, prob = saved
    heads = queries.shape[1]
    grad = grad.reshape(-1, heads, HEAD_DIM)
    grad_prob = jnp.einsum("qhe,khe->hqk", grad, values, preferred_element_type=F32)
    delta = jnp.sum(prob * grad_prob, axis=-1, keepdims=True)
    grad_scores = (prob * (grad_prob - delta)).astype(BF16)
    dq = jnp.einsum("hqk,khe->qhe", grad_scores, keys, preferred_element_type=F32) * FACTOR
    dk = jnp.einsum("hqk,qhe->khe", grad_scores, queries, preferred_element_type=F32) * FACTOR
    dv = jnp.einsum("hqk,qhe->khe", prob.astype(BF16), grad, preferred_element_type=F32)
    flat = lambda v: v.reshape(v.shape[0], -1).astype(BF16)
    grads = jnp.concatenate([flat(dq), flat(dk), flat(dv)], axis=1)
    return grads, mm(grads, weight, NT)


def shards(
    tokens,
    cotangent,
    timestep,
    class_ids,
    heights,
    widths,
    time_weight,
    class_table,
    ada_weight,
    ada_bias,
    conv_attn,
    qkv_weight,
    proj_weight,
    up_weight,
    conv_ffn,
    down_weight,
):
    latents, rows_here, cols, _ = tokens.shape
    half = cols // 2
    seq_count = lax.axis_size("seq")
    seq_place = lax.axis_index("seq")
    batch_count = lax.axis_size("batch")
    batch_place = lax.axis_index("batch")
    devices = batch_count * seq_count
    blocks = latents * 4
    share = seq_count // blocks
    per_group = rows_here // 2 * half
    group_tokens = seq_count * per_group

    first, last = tokens[:, :1], tokens[:, rows_here - 1 :]
    top = from_before(last, "seq")
    bot = from_after(first, "seq")

    half_freq = time_weight.shape[0] // 2
    frequency = jnp.exp(-math.log(10000.0) * jnp.arange(half_freq, dtype=F32) / half_freq)
    angles = timestep.astype(F32)[:, None] * frequency[None, :]
    embedding = jnp.concatenate([jnp.cos(angles), jnp.sin(angles)], axis=1).astype(BF16)
    one_hot = (
        class_ids[:, None] == jnp.arange(class_table.shape[0], dtype=jnp.int32)[None, :]
    ).astype(BF16)
    condition = mm(embedding, time_weight) + mm(one_hot, class_table)
    logistic = jax.nn.sigmoid(condition)
    activated_cond = (condition * logistic).astype(BF16)
    lead = mm(activated_cond, ada_weight[:, : 2 * D]) + ada_bias[: 2 * D]
    meta = jnp.concatenate(
        [heights, widths, jnp.reshape(seq_place * rows_here, (1,))]
    ).astype(jnp.int32)
    core = jnp.reshape(batch_place % 2, (1,)).astype(jnp.int32)

    mixed = enter(meta, tokens, top, bot, lead, conv_attn)
    late_cond = after(activated_cond, mixed)
    pieces = mm(late_cond, ada_weight[:, 2 * D :]) + ada_bias[2 * D :]
    pieces = jnp.concatenate([lead, pieces], axis=1).reshape(latents, 6, D)
    sent = mixed.reshape(blocks, 1, per_group, D)
    sent = jnp.broadcast_to(sent, (blocks, share, per_group, D)).reshape(seq_count, per_group, D)
    grouped = swap(sent).reshape(group_tokens, D)

    weight_t = qkv_weight.T

    my_block = seq_place // share
    my_latent = my_block // 4
    my_a = (my_block // 2) % 2
    my_b = my_block % 2
    places = jnp.arange(group_tokens, dtype=jnp.int32)
    key_row = places // half * 2 + my_a
    key_col = places % half * 2 + my_b
    height = lax.dynamic_index_in_dim(heights, my_latent, 0, keepdims=False)
    width = lax.dynamic_index_in_dim(widths, my_latent, 0, keepdims=False)
    key_ok = (key_row < height) & (key_col < width)

    margin = half
    tall = per_group + margin
    offset = jnp.stack([margin * (1 - my_a), batch_place % 2]).astype(jnp.int32)
    if share == 1:
        bias = jnp.broadcast_to(jnp.where(key_ok, 0.0, -1e30)[:, None], (group_tokens, 128))
        windows, lse = attend(offset, grouped, qkv_weight, weight_t, bias, seq_count, tall)
        attended = swap(windows)
    else:
        heads = HEADS // share
        wide = heads * HEAD_DIM
        chunk = seq_place % share
        thirds = qkv_weight.reshape(D, 3, share, wide)
        my_weight = lax.dynamic_index_in_dim(thirds, chunk, 2, keepdims=False).reshape(D, 3 * wide)
        att, saved = attend_plain(grouped, my_weight, key_ok, heads)
        windows = windows_of(att, offset[0], margin, seq_count)
        attended = swap(windows).reshape(blocks, share, tall, wide)
        attended = attended.transpose(0, 2, 1, 3).reshape(blocks, tall, D)

    ge, get, cot_split = prepare_cot(cotangent, pieces)
    conditions = lax.all_gather(
        jnp.concatenate([condition, embedding.astype(F32), class_ids.astype(F32)[:, None]], axis=1),
        "batch",
        axis=0,
    )
    if share == 1:
        triple = mm(grouped, qkv_weight).astype(BF16)
        key_t = mm(weight_t[D : 2 * D], grouped, NT).astype(BF16)
        grouped_t = grouped.T
        attended, ge, triple, key_t, grouped_t, conditions = lax.optimization_barrier(
            (attended, ge, triple, key_t, grouped_t, conditions)
        )
    e2, e2t, after_attn, branch = second(
        meta, attended, tokens, top, bot, pieces, proj_weight
    )
    expanded, grad_e2, edge_first, edge_last, send_c, keep_c, conv_ffn_part = ffn(
        core, e2, e2t, ge, get, up_weight, down_weight, conv_ffn, cols
    )
    halving = batch_count == 4 and seq_count == 8
    if halving:
        got_c = hop(send_c, "c")
    low = from_before(edge_last, "seq")
    high = from_after(edge_first, "seq")
    output, gate_sums = finish_output(expanded, after_attn, cot_split, pieces, rows_here, cols)
    grad_after, grad_branch, grad_attended, mid_sums = middle(
        meta, grad_e2, low, high, after_attn, branch, cot_split, pieces, proj_weight
    )

    att_all = after(attended, grad_attended)
    starts = [margin * ((k // 2) % 2) for k in range(blocks)]
    att_own = jnp.concatenate([att_all[k, at : at + per_group] for k, at in enumerate(starts)])
    flat_branch = grad_branch.reshape(blocks * per_group, D)
    hidden = conv_ffn.shape[1]
    if share == 1:
        gatt = swap(grad_attended.reshape(seq_count, per_group, D)).reshape(group_tokens, D)
        if halving:
            keep_c = after(keep_c, grad_attended)
            sums = add(keep_c, got_c).astype(BF16).reshape(2, 2, 2, 2, 2, D // devices, hidden)
            send_a, keep_a, dims_a = split(sums[0], "yhlx", "y")
            send_b, keep_b, dims_b = split(sums[1], "yhlx", "x")
            late_branch = after(flat_branch, got_c)
            proj_grad = mm(att_own, late_branch, (((0,), (0,)), ((), ()))).astype(BF16)
            send_p, keep_p, _ = split(blocks_of(proj_grad), ORDER, "c")
            got_p = hop(send_p, "c")
            gatt, send_a, send_b, send_p = lax.optimization_barrier((gatt, send_a, send_b, send_p))
            got_a, got_b = hop(send_a, "y"), hop(send_b, "x")
        send_r, keep_r, gm_windows = attend_back(
            offset, triple, key_t, bias, lse, gatt, qkv_weight, grouped_t, seq_count, tall
        )
        gm = swap(gm_windows)
        if halving:
            gm_windows, got_a, got_b = lax.optimization_barrier((gm_windows, got_a, got_b))
        gm = swap(gm_windows)
    else:
        sent = grad_attended.reshape(blocks, per_group, share, wide).transpose(0, 2, 1, 3)
        gatt = swap(sent.reshape(seq_count, per_group, wide)).reshape(group_tokens, wide)
        grad_triple, gm_part = attend_plain_back(saved, gatt, my_weight)
        gm_windows = windows_of(gm_part.astype(BF16), offset[0], margin, seq_count)
        gm = swap(gm_windows).reshape(blocks, share, tall, D)
        gm = jnp.sum(gm.astype(F32), axis=1).astype(BF16)
        own_grad = mm(grouped, grad_triple, (((0,), (0,)), ((), ()))).astype(BF16)
        spread = jnp.zeros((D, 3, share, wide), BF16)
        qkv_grad = lax.dynamic_update_index_in_dim(
            spread, own_grad.reshape(D, 3, wide), chunk, 2
        ).reshape(D, 3 * D)
        proj_grad = mm(att_own, flat_branch, (((0,), (0,)), ((), ()))).astype(BF16)
        rest = jnp.concatenate([qkv_grad, proj_grad], axis=1)

    if halving:
        got_r = hop(send_r, "c")
        keep_a, keep_b = after(keep_a, keep_r), after(keep_b, keep_r)
        send_a, keep_a, dims_a = split(add(keep_a, got_a).astype(BF16), dims_a, "x")
        send_b, keep_b, dims_b = split(add(keep_b, got_b).astype(BF16), dims_b, "y")
        sums = add(keep_r, got_r).astype(BF16).reshape(3, 2, 2, 2, 2, D // devices, D)
        sums_p = add(keep_p, got_p).astype(BF16)
        send_one, keep_one, dims_one = split(sums[:2], "yhlx", "y")
        send_two, keep_two, dims_two = split(jnp.stack([sums[2], sums_p]), "yhlx", "x")
        gm = after(gm, send_a, send_b)
        got_a, got_b = hop(send_a, "x"), hop(send_b, "y")
        got_one, got_two = hop(send_one, "y"), hop(send_two, "x")
        gm, got_a, got_b = lax.optimization_barrier((gm, got_a, got_b))
        pair = jnp.stack([add(keep_a, got_a), add(keep_b, got_b)]).astype(BF16)
        send_l, keep_l, dims_l = split(pair, dims_a, "l")
        gm = after(gm, send_l)
        got_l = hop(send_l, "l")
    total = batch_count * latents

    here = batch_place * seq_count + seq_place
    own_cols = D // devices
    conditions = conditions.reshape(total, -1)
    condition_all = conditions[:, :D]
    embedding_all = conditions[:, D : D + embedding.shape[1]]
    ids_all = conditions[:, -1].astype(jnp.int32)
    logistic_all = jax.nn.sigmoid(condition_all)
    activated_all = (condition_all * logistic_all).astype(BF16).astype(F32)
    slope_all = logistic_all * (1.0 + condition_all * (1.0 - logistic_all))

    def back_through(grads):
        high = lax.reduce_precision(grads, 8, 7)
        middle_term = lax.reduce_precision(grads - high, 8, 7)
        low = grads - high - middle_term
        product = mm(jnp.concatenate([high, middle_term, low]).astype(BF16), ada_weight, NT)
        return product[:total] + product[total : 2 * total] + product[2 * total :]

    token_grad, conv_attn_part, end_sums = leave(
        meta, gm, tokens, top, bot, grad_after, pieces, conv_attn
    )

    common = jnp.concatenate([end_sums, mid_sums, gate_sums], axis=1)
    sliced = (jnp.sum(conv_attn_part, axis=0), conv_ffn_part)
    message = payload_of(common, sliced)
    if halving:
        message, keep_l, got_l, keep_one, keep_two = lax.optimization_barrier(
            (message, keep_l, got_l, keep_one, keep_two)
        )
        send_h, keep_h, _ = split(add(keep_l, got_l).astype(BF16), dims_l, "h")
        got_h = hop(send_h, "h")
        send_one, keep_one, dims_one = split(add(keep_one, got_one).astype(BF16), dims_one, "x")
        send_two, keep_two, dims_two = split(add(keep_two, got_two).astype(BF16), dims_two, "y")
        got_one, got_two = hop(send_one, "x"), hop(send_two, "y")
    gathered = lax.all_gather(jnp.sum(swap(message), axis=0), "batch", axis=0)
    if halving:
        gathered, keep_one, keep_two, keep_h = lax.optimization_barrier(
            (gathered, keep_one, keep_two, keep_h)
        )
        pair = add(keep_h, got_h)
        down_rows, up_rows = pair[0], pair[1]
        rest_rows = jnp.concatenate([add(keep_one, got_one), add(keep_two, got_two)])
        send_l, keep_l, dims_l = split(rest_rows.astype(BF16), dims_one, "l")
        got_l = hop(send_l, "l")
    else:
        whole = jnp.stack([keep_c, send_c])
        whole = jnp.where(core[0] == 0, whole, whole[::-1]).transpose(1, 2, 0, 3, 4)
        whole = whole.reshape(2, D, hidden)
        down_rows, up_rows = scatter_rows(whole[0]), scatter_rows(whole[1])
        if share == 1:
            rest = jnp.stack([keep_r, send_r])
            rest = jnp.where(core[0] == 0, rest, rest[::-1]).transpose(2, 0, 3, 1, 4).reshape(D, -1)
            proj_grad = mm(att_own, flat_branch, (((0,), (0,)), ((), ()))).astype(BF16)
            rest = jnp.concatenate([rest, proj_grad], axis=1)
        rest_rows = scatter_rows(rest).reshape(own_cols, 4, D).transpose(1, 0, 2)
    all_sums, (conv_attn_grad, conv_ffn_grad) = unpack(gathered, common, sliced)

    grad_pieces = all_sums.reshape(total, 6 * D)
    grad_silu = back_through(grad_pieces)
    if halving:
        grad_silu, got_l = lax.optimization_barrier((grad_silu, got_l))
        rest_rows = reduce_rest(add(keep_l, got_l), dims_l, "h")
    qkv_rows = jnp.concatenate([rest_rows[0], rest_rows[1], rest_rows[2]], axis=1)
    proj_rows = rest_rows[3]
    cond_all = grad_silu * slope_all
    cond_grad = lax.dynamic_slice_in_dim(cond_all, batch_place * latents, latents)
    cond_cols = lax.dynamic_slice_in_dim(cond_all, here * own_cols, own_cols, axis=1)
    act_cols = lax.dynamic_slice_in_dim(activated_all, here * own_cols, own_cols, axis=1)
    outer = lambda left, right: lax.dot_general(
        left, right, (((0,), (0,)), ((), ())), precision=HIGHEST, preferred_element_type=F32
    )
    hot_all = (ids_all[:, None] == jnp.arange(class_table.shape[0], dtype=jnp.int32)[None, :]).astype(F32)
    bias_cols = 6 * D // devices
    bias_grad = jnp.sum(
        lax.dynamic_slice_in_dim(grad_pieces, here * bias_cols, bias_cols, axis=1), axis=0
    )
    return (
        output,
        token_grad,
        cond_grad,
        outer(embedding_all, cond_cols),
        outer(hot_all, cond_cols),
        outer(act_cols, grad_pieces),
        bias_grad,
        conv_attn_grad,
        qkv_rows,
        proj_rows,
        up_rows,
        conv_ffn_grad,
        down_rows.T,
    )


def solution(mesh):
    strips = P("batch", "seq", None, None)
    in_specs = (strips, strips) + (P("batch"),) * 4 + (P(),) * 10
    both = ("batch", "seq")
    out_specs = (
        strips,
        strips,
        P("batch", None),
        P(None, both),
        P(None, both),
        P(both, None),
        P(both),
        P(None, both),
        P(both, None),
        P(both, None),
        P(both, None),
        P(None, both),
        P(None, both),
    )
    return jax.shard_map(shards, mesh=mesh, in_specs=in_specs, out_specs=out_specs, check_vma=False)
```

```python
import functools
import math

import jax
import jax.numpy as jnp
from jax import lax
from jax.experimental import pallas as pl
from jax.experimental.pallas import tpu as pltpu
from jax.sharding import PartitionSpec as P

D = 768
HEADS = 12
HEAD_DIM = 64
PAIR = 2 * HEAD_DIM
QUAD = 2 * PAIR
QUADS = HEADS // 4
FF_BLOCK = 256
LANE_PARTS = D // 128
FACTOR = HEAD_DIM ** (-0.5)

F32 = jnp.float32
BF16 = jnp.bfloat16
HIGHEST = lax.Precision.HIGHEST
NN = (((1,), (0,)), ((), ()))
NT = (((1,), (1,)), ((), ()))
VMEM_LIMIT = 60 * 1024 * 1024


def mm(left, right, dims=NN):
    return lax.dot_general(left, right, dims, preferred_element_type=F32)


def shift_down(values):
    rows = lax.broadcasted_iota(jnp.int32, values.shape, 0)
    return jnp.where(rows == 0, 0.0, pltpu.roll(values, 1, 0))


def shift_up(values):
    count = values.shape[0]
    rows = lax.broadcasted_iota(jnp.int32, values.shape, 0)
    return jnp.where(rows == count - 1, 0.0, pltpu.roll(values, count - 1, 0))


def put_shifts(ref, row, parity, values):
    ref[row, 1 + parity] = values
    if parity == 0:
        ref[row, 3] = shift_up(values)
    else:
        ref[row, 0] = shift_down(values)


def normalize(values):
    centre = values - jnp.mean(values, axis=-1, keepdims=True)
    spread = jnp.mean(centre * centre, axis=-1, keepdims=True)
    scaled = lax.rsqrt(spread + 1e-06)
    return centre * scaled, scaled


def norm_back(grad_norm, normed, scaled):
    return scaled * (
        grad_norm
        - jnp.mean(grad_norm, axis=-1, keepdims=True)
        - normed * jnp.mean(grad_norm * normed, axis=-1, keepdims=True)
    )


def put_row(buf, row, values):
    for k in range(LANE_PARTS):
        buf[row, k] = values[:, 128 * k : 128 * (k + 1)]


def get_row(buf, row):
    return jnp.concatenate([buf[row, k] for k in range(LANE_PARTS)], axis=1)


def put_columns(buf, row, parity, values):
    for k in range(LANE_PARTS):
        buf[row, k, pl.ds(parity, values.shape[0], stride=2), :] = values[:, 128 * k : 128 * (k + 1)]


def get_columns(buf, row, parity):
    half = buf.shape[2] // 2
    return jnp.concatenate(
        [buf[row, k, pl.ds(parity, half, stride=2), :] for k in range(LANE_PARTS)], axis=1
    )


def usable_of(meta, latents, latent, row, parity, half):
    cols = 2 * lax.broadcasted_iota(jnp.int32, (half, 1), 0) + parity
    row_ok = jnp.logical_and(row >= 0, row < meta[latent])
    limit = jnp.where(row_ok, meta[latents + latent], 0)
    return (cols < limit).astype(F32)


def sum8(values):
    total = values[0:8]
    for start in range(8, values.shape[0], 8):
        total = total + values[start : start + 8]
    return total


def enter_kernel(meta, tok, top, bot, lead, kern, out, buf, ent):
    latents = pl.num_programs(0)
    latent = pl.program_id(0)
    rows_here, cols = tok.shape[1], tok.shape[2]
    half = cols // 2
    row0 = meta[2 * latents]
    shift = lead[pl.ds(latent, 1), :D]
    scale = 1.0 + lead[pl.ds(latent, 1), D:]
    taps = [kern[t : t + 1, :].astype(F32) for t in range(9)]
    for rr in range(rows_here + 2):
        source = top[0, 0] if rr == 0 else bot[0, 0] if rr == rows_here + 1 else tok[0, rr - 1]
        put_row(buf, rr, source.astype(F32))
        for parity in range(2):
            normed, _ = normalize(get_columns(buf, rr, parity))
            ok = usable_of(meta, latents, latent, row0 + rr - 1, parity, half)
            put_shifts(ent, rr, parity, ((normed * scale + shift) * ok).astype(BF16).astype(F32))
    for row in range(rows_here):
        for parity in range(2):
            total = jnp.zeros((half, D), F32)
            for i in range(3):
                for j in range(3):
                    total = total + ent[row + i, parity + j] * taps[3 * i + j]
            mixed = (ent[row + 1, 1 + parity] + total).astype(BF16)
            group = 2 * (row % 2) + parity
            out[0, group, (row // 2) * half : (row // 2 + 1) * half, :] = mixed


def enter(meta, tokens, top, bot, lead, kern):
    latents, rows_here, cols, _ = tokens.shape
    half = cols // 2
    per_group = rows_here // 2 * half
    whole = lambda *shape: pl.BlockSpec(shape, lambda l, m: (l,) + (0,) * (len(shape) - 1))
    return pl.pallas_call(
        enter_kernel,
        out_shape=jax.ShapeDtypeStruct((latents, 4, per_group, D), BF16),
        grid_spec=pltpu.PrefetchScalarGridSpec(
            num_scalar_prefetch=1,
            grid=(latents,),
            in_specs=[
                whole(1, rows_here, cols, D),
                whole(1, 1, cols, D),
                whole(1, 1, cols, D),
                pl.BlockSpec((latents, 2 * D), lambda l, m: (0, 0)),
                pl.BlockSpec((9, D), lambda l, m: (0, 0)),
            ],
            out_specs=whole(1, 4, per_group, D),
            scratch_shapes=[
                pltpu.VMEM((rows_here + 2, LANE_PARTS, cols, 128), F32),
                pltpu.VMEM((rows_here + 2, 4, half, D), F32),
            ],
        ),
        compiler_params=pltpu.CompilerParams(vmem_limit_bytes=VMEM_LIMIT),
        cost_estimate=pl.CostEstimate(flops=6_000_000_000, bytes_accessed=4_000_000, transcendentals=0),
        name="enter",
    )(meta, tokens, top, bot, lead, kern)


def cot_kernel(cot, pieces, ge_out, get_out, cot_out, buf):
    rows_here, cols = cot.shape[1], cot.shape[2]
    half = cols // 2
    gate = pieces[0, 5:6, :]
    for row in range(rows_here):
        put_row(buf, row, cot[0, row].astype(F32))
        for parity in range(2):
            values = get_columns(buf, row, parity)
            at = (2 * row + parity) * half
            ge_out[0, at : at + half, :] = (gate * values).astype(BF16)
            cot_out[0, at : at + half, :] = values.astype(BF16)
    get_out[0] = ge_out[0].astype(F32).T.astype(BF16)


def prepare_cot(cotangent, pieces):
    latents, rows_here, cols, _ = cotangent.shape
    whole = lambda *shape: pl.BlockSpec(shape, lambda l: (l,) + (0,) * (len(shape) - 1))
    own = rows_here * cols
    return pl.pallas_call(
        cot_kernel,
        out_shape=(
            jax.ShapeDtypeStruct((latents, own, D), BF16),
            jax.ShapeDtypeStruct((latents, D, own), BF16),
            jax.ShapeDtypeStruct((latents, own, D), BF16),
        ),
        grid=(latents,),
        in_specs=[whole(1, rows_here, cols, D), whole(1, 6, D)],
        out_specs=(whole(1, own, D), whole(1, D, own), whole(1, own, D)),
        scratch_shapes=[pltpu.VMEM((rows_here, LANE_PARTS, cols, 128), F32)],
        compiler_params=pltpu.CompilerParams(vmem_limit_bytes=VMEM_LIMIT),
        cost_estimate=pl.CostEstimate(flops=4_000_000_000, bytes_accessed=4_000_000, transcendentals=0),
        name="prepare_cot",
    )(cotangent, pieces)


def second_kernel(meta, att, tok, top, bot, pieces, proj, e2_out, e2t_out, after_out, branch_out, buf, bran):
    latents = pl.num_programs(0)
    latent = pl.program_id(0)
    rows_here, cols = tok.shape[1], tok.shape[2]
    half = cols // 2
    row0 = meta[2 * latents]
    gate = pieces[0, 2:3, :]
    shift = pieces[0, 3:4, :]
    scale = 1.0 + pieces[0, 4:5, :]
    for group in range(4):
        bran[group] = mm(att[group], proj[...])
    for rr in range(rows_here + 2):
        source = top[0, 0] if rr == 0 else bot[0, 0] if rr == rows_here + 1 else tok[0, rr - 1]
        put_row(buf, rr, source.astype(F32))
        for parity in range(2):
            group = 2 * ((rr + 1) % 2) + parity
            branch = bran[group, (rr // 2) * half : (rr // 2 + 1) * half, :]
            after = get_columns(buf, rr, parity) + gate * branch
            normed, _ = normalize(after)
            ok = usable_of(meta, latents, latent, row0 + rr - 1, parity, half)
            at = (2 * rr + parity) * half
            e2_out[0, at : at + half, :] = ((normed * scale + shift) * ok).astype(BF16)
            if 1 <= rr <= rows_here:
                own = at - cols
                after_out[0, own : own + half, :] = after
                branch_out[0, own : own + half, :] = branch
    e2t_out[0] = e2_out[0].astype(F32).T.astype(BF16)


def second(meta, attended, tokens, top, bot, pieces, proj):
    latents, rows_here, cols, _ = tokens.shape
    own = rows_here * cols
    wide = attended.shape[1]
    whole = lambda *shape: pl.BlockSpec(shape, lambda l, m: (l,) + (0,) * (len(shape) - 1))
    return pl.pallas_call(
        second_kernel,
        out_shape=(
            jax.ShapeDtypeStruct((latents, own + 2 * cols, D), BF16),
            jax.ShapeDtypeStruct((latents, D, own + 2 * cols), BF16),
            jax.ShapeDtypeStruct((latents, own, D), F32),
            jax.ShapeDtypeStruct((latents, own, D), F32),
        ),
        grid_spec=pltpu.PrefetchScalarGridSpec(
            num_scalar_prefetch=1,
            grid=(latents,),
            in_specs=[
                whole(4, wide, D),
                whole(1, rows_here, cols, D),
                whole(1, 1, cols, D),
                whole(1, 1, cols, D),
                whole(1, 6, D),
                pl.BlockSpec((D, D), lambda l, m: (0, 0)),
            ],
            out_specs=(
                whole(1, own + 2 * cols, D),
                whole(1, D, own + 2 * cols),
                whole(1, own, D),
                whole(1, own, D),
            ),
            scratch_shapes=[
                pltpu.VMEM((rows_here + 2, LANE_PARTS, cols, 128), F32),
                pltpu.VMEM((4, wide, D), F32),
            ],
        ),
        compiler_params=pltpu.CompilerParams(vmem_limit_bytes=VMEM_LIMIT),
        cost_estimate=pl.CostEstimate(flops=7_000_000_000, bytes_accessed=4_000_000, transcendentals=0),
        name="second",
    )(meta, attended, tokens, top, bot, pieces, proj)


def normal_parts(values):
    density = jnp.exp2(values * values * -0.7213475204444817 - 1.3257480647361592)
    t = 1.0 / (1.0 + 0.2316419 * jnp.abs(values))
    series = t * (
        0.319381530
        + t * (-0.356563782 + t * (1.781477937 + t * (-1.821255978 + t * 1.330274429)))
    )
    tail = density * series
    return jnp.where(values > 0.0, 1.0 - tail, tail), density


def ffn_kernel(core, e2, e2t, ge, get, up, down, kern_in, exp_out, ge2_out, first_out, last_out, send_out, keep_out, kern_out, *scratch):
    latents = e2.shape[0]
    lifted, gact, gconv, act, graised = [scratch[k * latents : (k + 1) * latents] for k in range(5)]
    down_acc, up_acc = scratch[5 * latents :]
    step = pl.program_id(0)
    half = lifted[0].shape[2]
    rows_here = gconv[0].shape[0]
    block = lifted[0].shape[3]
    chunks = block // 128
    lanes = [slice(c * 128, (c + 1) * 128) for c in range(chunks)]
    taps = [[kern_in[t : t + 1, cut].astype(F32) for t in range(9)] for cut in lanes]
    sums = [[jnp.zeros((8, 128), F32) for _ in range(9)] for _ in range(chunks)]
    lift_rows = 3

    def put(ref, row, parity, cut, values):
        ref[row, 1 + parity, :, cut] = values
        if parity == 0:
            ref[row, 3, :, cut] = shift_up(values)
        else:
            ref[row, 0, :, cut] = shift_down(values)

    def lift(latent, part):
        size = lift_rows * 2 * half
        raised = mm(e2[latent, part * size : (part + 1) * size], up[...])
        for k in range(lift_rows):
            for parity in range(2):
                at = (2 * k + parity) * half
                for cut in lanes:
                    put(lifted[latent], part * lift_rows + k, parity, cut, raised[at : at + half, cut])

    def pull(latent):
        gact[latent][...] = mm(ge[latent], down[...], NT)

    def bend(latent, row, c):
        cut = lanes[c]
        for parity in range(2):
            total = None
            for i in range(3):
                for j in range(3):
                    term = lifted[latent][row + i, parity + j, :, cut] * taps[c][3 * i + j]
                    total = term if total is None else total + term
            cdf, density = normal_parts(total)
            at = (2 * row + parity) * half
            act[latent][at : at + half, cut] = (total * cdf).astype(BF16)
            grad = gact[latent][at : at + half, cut] * (cdf + total * density)
            put(gconv[latent], row, parity, cut, grad)

    def unbend(latent, rr, c):
        cut = lanes[c]
        for parity in range(2):
            total = None
            for i in range(3):
                row = rr - i
                if not 0 <= row < rows_here:
                    continue
                for j in range(3):
                    term = gconv[latent][row, parity + 2 - j, :, cut] * taps[c][3 * i + j]
                    total = term if total is None else total + term
            at = (2 * rr + parity) * half
            graised[latent][at : at + half, cut] = total.astype(BF16)
            if rr < rows_here:
                here = gconv[latent][rr, 1 + parity, :, cut]
                for i in range(3):
                    for j in range(3):
                        t = 3 * i + j
                        part = lifted[latent][rr + i, parity + j, :, cut] * here
                        sums[c][t] = sums[c][t] + sum8(part)

    def expand(latent):
        exp_out[latent] += mm(act[latent][...], down[...])

    def lower(latent):
        ge2_out[latent] += mm(graised[latent][...], up[...], NT)

    def weigh_down(latent):
        value = mm(get[latent], act[latent][...])
        down_acc[...] = value if latent == 0 else down_acc[...] + value

    def weigh_up(latent):
        value = mm(e2t[latent], graised[latent][...])
        up_acc[...] = value if latent == 0 else up_acc[...] + value

    @pl.when(step == 0)
    def _():
        exp_out[...] = jnp.zeros_like(exp_out)
        ge2_out[...] = jnp.zeros_like(ge2_out)

    def mix(work, more):
        stride = max(1, len(work) // max(1, len(more)))
        for k, unit in enumerate(work):
            if k % stride == 0 and k // stride < len(more):
                more[k // stride]()
            unit()
        for unit in more[-(-len(work) // stride) :]:
            unit()

    part = functools.partial
    lifts = (rows_here + 2) // lift_rows
    for k in range(lifts):
        lift(0, k)
    pull(0)
    for latent in range(latents):
        bends = [part(bend, latent, row, c) for c in range(chunks) for row in range(rows_here)]
        unbends = [part(unbend, latent, rr, c) for c in range(chunks) for rr in range(rows_here + 2)]
        first, then = [], [part(expand, latent), part(weigh_down, latent)]
        if latent > 0:
            first += [part(lower, latent - 1), part(weigh_up, latent - 1)]
        if latent + 1 < latents:
            first += [part(lift, latent + 1, k) for k in range(lifts)] + [part(pull, latent + 1)]
        mix(bends, first)
        mix(unbends, then)
    lower(latents - 1)
    weigh_up(latents - 1)

    @pl.when(step == pl.num_programs(0) - 1)
    def _():
        first_out[...] = ge2_out[:, : 2 * half].astype(BF16)
        last_out[...] = ge2_out[:, 2 * half * (rows_here + 1) :].astype(BF16)

    size = down_acc.shape[0] // 4
    for which, acc in enumerate((down_acc, up_acc)):
        for y in range(2):
            mine = pl.multiple_of((2 * y + core[0]) * size, 8)
            other = pl.multiple_of((2 * y + 1 - core[0]) * size, 8)
            keep_out[which, y] = acc[pl.ds(mine, size), :].astype(BF16)
            send_out[which, y] = acc[pl.ds(other, size), :].astype(BF16)
    for c, cut in enumerate(lanes):
        for t in range(9):
            kern_out[t : t + 1, cut] = jnp.sum(sums[c][t], axis=0, keepdims=True)


def ffn(core, e2, e2t, ge, get, up, down, kern, cols):
    latents, wide, _ = e2.shape
    half = cols // 2
    own = ge.shape[1]
    rows_here = own // cols
    hidden = up.shape[1]
    fixed = lambda *shape: pl.BlockSpec(shape, lambda f, c: (0,) * len(shape))
    parts = jax.ShapeDtypeStruct((2, 2, D // 4, hidden), BF16)
    parts_spec = pl.BlockSpec((2, 2, D // 4, FF_BLOCK), lambda f, c: (0, 0, 0, f))
    each = lambda *args: [pltpu.VMEM(*args)] * latents
    return pl.pallas_call(
        ffn_kernel,
        out_shape=(
            jax.ShapeDtypeStruct((latents, own, D), F32),
            jax.ShapeDtypeStruct((latents, wide, D), F32),
            jax.ShapeDtypeStruct((latents, cols, D), BF16),
            jax.ShapeDtypeStruct((latents, cols, D), BF16),
            parts,
            parts,
            jax.ShapeDtypeStruct((9, hidden), F32),
        ),
        grid_spec=pltpu.PrefetchScalarGridSpec(
            num_scalar_prefetch=1,
            grid=(hidden // FF_BLOCK,),
            in_specs=[
                fixed(latents, wide, D),
                fixed(latents, D, wide),
                fixed(latents, own, D),
                fixed(latents, D, own),
                pl.BlockSpec((D, FF_BLOCK), lambda f, c: (0, f)),
                pl.BlockSpec((FF_BLOCK, D), lambda f, c: (f, 0)),
                pl.BlockSpec((9, FF_BLOCK), lambda f, c: (0, f)),
            ],
            out_specs=(
                fixed(latents, own, D),
                fixed(latents, wide, D),
                fixed(latents, cols, D),
                fixed(latents, cols, D),
                parts_spec,
                parts_spec,
                pl.BlockSpec((9, FF_BLOCK), lambda f, c: (0, f)),
            ),
            scratch_shapes=each((rows_here + 2, 4, half, FF_BLOCK), F32)
            + each((own, FF_BLOCK), F32)
            + each((rows_here, 4, half, FF_BLOCK), F32)
            + each((own, FF_BLOCK), BF16)
            + each((wide, FF_BLOCK), BF16)
            + [pltpu.VMEM((D, FF_BLOCK), F32), pltpu.VMEM((D, FF_BLOCK), F32)],
        ),
        compiler_params=pltpu.CompilerParams(vmem_limit_bytes=VMEM_LIMIT),
        cost_estimate=pl.CostEstimate(flops=35_000_000_000, bytes_accessed=4_000_000, transcendentals=0),
        name="ffn",
    )(core, e2, e2t, ge, get, up, down, kern)


def output_kernel(exp, after_in, cot_in, pieces, out, sum_out, buf):
    rows_here, cols = out.shape[1], out.shape[2]
    half = cols // 2
    gate = pieces[0, 5:6, :]
    total = jnp.zeros((8, D), F32)
    for row in range(rows_here):
        for parity in range(2):
            part = pl.ds((2 * row + parity) * half, half)
            expanded = exp[0, part, :]
            put_columns(buf, row, parity, after_in[0, part, :] + gate * expanded)
            total = total + sum8(cot_in[0, part, :].astype(F32) * expanded)
        out[0, row] = get_row(buf, row).astype(BF16)
    sum_out[0] = jnp.sum(total, axis=0, keepdims=True)


def finish_output(exp, after, cot, pieces, rows_here, cols):
    latents, own, _ = exp.shape
    whole = lambda *shape: pl.BlockSpec(shape, lambda l: (l,) + (0,) * (len(shape) - 1))
    return pl.pallas_call(
        output_kernel,
        out_shape=(
            jax.ShapeDtypeStruct((latents, rows_here, cols, D), BF16),
            jax.ShapeDtypeStruct((latents, 1, D), F32),
        ),
        grid=(latents,),
        in_specs=[whole(1, own, D), whole(1, own, D), whole(1, own, D), whole(1, 6, D)],
        out_specs=(whole(1, rows_here, cols, D), whole(1, 1, D)),
        scratch_shapes=[pltpu.VMEM((rows_here, LANE_PARTS, cols, 128), F32)],
        compiler_params=pltpu.CompilerParams(vmem_limit_bytes=VMEM_LIMIT),
        cost_estimate=pl.CostEstimate(flops=5_000_000_000, bytes_accessed=4_000_000, transcendentals=0),
        name="finish_output",
    )(exp, after, cot, pieces)


def middle_kernel(meta, ge2, low, high, after_in, branch_in, cot_in, pieces, proj, after_grad, gb_out, gatt_out, sums_out):
    latents = pl.num_programs(0)
    latent = pl.program_id(0)
    own = after_in.shape[1]
    cols = low.shape[1]
    rows_here = own // cols
    half = cols // 2
    row0 = meta[2 * latents]
    gate_one = pieces[0, 2:3, :]
    scale = 1.0 + pieces[0, 4:5, :]
    sums = [jnp.zeros((8, D), F32) for _ in range(3)]
    for row in range(rows_here):
        for parity in range(2):
            at = (2 * row + parity) * half
            part = pl.ds(at, half)
            side = pl.ds(parity * half, half)
            after = after_in[0, part, :]
            cot = cot_in[0, part, :].astype(F32)
            normed, scaled = normalize(after)
            ok = usable_of(meta, latents, latent, row0 + row, parity, half)
            grad = ge2[0, pl.ds(at + cols, half), :]
            if row == 0:
                grad = grad + low[0, side, :].astype(F32)
            if row == rows_here - 1:
                grad = grad + high[0, side, :].astype(F32)
            grad = grad * ok
            grad_after = cot + norm_back(grad * scale, normed, scaled)
            after_grad[0, part, :] = grad_after
            sums[0] = sums[0] + sum8(grad_after * branch_in[0, part, :])
            sums[1] = sums[1] + sum8(grad)
            sums[2] = sums[2] + sum8(grad * normed)
            group = 2 * (row % 2) + parity
            to = pl.ds((row // 2) * half, half)
            gb_out[0, group, to, :] = (gate_one * grad_after).astype(BF16)
    for k in range(3):
        sums_out[0, k : k + 1, :] = jnp.sum(sums[k], axis=0, keepdims=True)
    for group in range(4):
        gatt_out[0, group] = mm(gb_out[0, group], proj[...], NT).astype(BF16)


def middle(meta, ge2, low, high, after, branch, cot, pieces, proj):
    latents, own, _ = after.shape
    wide, cols = ge2.shape[1], low.shape[1]
    per_group = own // 4
    whole = lambda *shape: pl.BlockSpec(shape, lambda l, m: (l,) + (0,) * (len(shape) - 1))
    return pl.pallas_call(
        middle_kernel,
        out_shape=(
            jax.ShapeDtypeStruct((latents, own, D), F32),
            jax.ShapeDtypeStruct((latents, 4, per_group, D), BF16),
            jax.ShapeDtypeStruct((latents, 4, per_group, D), BF16),
            jax.ShapeDtypeStruct((latents, 3, D), F32),
        ),
        grid_spec=pltpu.PrefetchScalarGridSpec(
            num_scalar_prefetch=1,
            grid=(latents,),
            in_specs=[
                whole(1, wide, D),
                whole(1, cols, D),
                whole(1, cols, D),
                whole(1, own, D),
                whole(1, own, D),
                whole(1, own, D),
                whole(1, 6, D),
                pl.BlockSpec((D, D), lambda l, m: (0, 0)),
            ],
            out_specs=(
                whole(1, own, D),
                whole(1, 4, per_group, D),
                whole(1, 4, per_group, D),
                whole(1, 3, D),
            ),
        ),
        compiler_params=pltpu.CompilerParams(vmem_limit_bytes=VMEM_LIMIT),
        cost_estimate=pl.CostEstimate(flops=8_000_000_000, bytes_accessed=4_000_000, transcendentals=0),
        name="middle",
    )(meta, ge2, low, high, after, branch, cot, pieces, proj)


def leave_kernel(meta, gm, tok, top, bot, after_grad, pieces, kern, out, kern_out, sums_out, buf, ent, gmx, obuf, nbuf, sbuf, tot):
    latents = pl.num_programs(0)
    latent = pl.program_id(0)
    rows_here, cols = tok.shape[1], tok.shape[2]
    half = cols // 2
    row0 = meta[2 * latents]
    shift = pieces[0, 0:1, :]
    scale = 1.0 + pieces[0, 1:2, :]
    taps = [kern[t : t + 1, :].astype(F32) for t in range(9)]
    put_row(buf, 0, top[0, 0].astype(F32))
    for row in range(rows_here):
        put_row(buf, row + 1, tok[0, row].astype(F32))
    put_row(buf, rows_here + 1, bot[0, 0].astype(F32))

    def take(rr, carry):
        at = pl.multiple_of(rr // 2 * half, half)
        for parity in range(2):
            normed, scaled = normalize(get_columns(buf, rr, parity))
            nbuf[rr, parity] = normed
            sbuf[rr, parity] = jnp.broadcast_to(scaled, (half, 128))
            ok = usable_of(meta, latents, latent, row0 + rr - 1, parity, half)
            put_shifts(ent, rr, parity, (normed * scale + shift) * ok)
            group = 2 * ((rr + 1) % 2) + parity
            put_shifts(gmx, rr, parity, gm[group, pl.ds(at, half), :].astype(F32))
        return carry

    lax.fori_loop(0, rows_here + 2, take, 0)
    tot[...] = jnp.zeros_like(tot)

    def give(row, carry):
        for parity in range(2):
            here = gmx[row + 1, 1 + parity]
            total = here
            for i in range(3):
                for j in range(3):
                    t = 3 * i + j
                    total = total + gmx[row + 2 - i, parity + 2 - j] * taps[t]
                    tot[t] += sum8(ent[row + i, parity + j] * here)
            ok = usable_of(meta, latents, latent, row0 + row, parity, half)
            grad = total * ok
            normed, scaled = nbuf[row + 1, parity], sbuf[row + 1, parity, :, 0:1]
            tot[9] += sum8(grad)
            tot[10] += sum8(grad * normed)
            at = pl.multiple_of((2 * row + parity) * half, half)
            back = after_grad[0, pl.ds(at, half), :] + norm_back(grad * scale, normed, scaled)
            put_columns(obuf, row, parity, back)
        out[0, row] = get_row(obuf, row)
        return carry

    lax.fori_loop(0, rows_here, give, 0)
    for t in range(9):
        kern_out[0, t : t + 1, :] = jnp.sum(tot[t], axis=0, keepdims=True)
    for k in range(2):
        sums_out[0, k : k + 1, :] = jnp.sum(tot[9 + k], axis=0, keepdims=True)


def leave(meta, gm, tokens, top, bot, after_grad, pieces, kern):
    latents, rows_here, cols, _ = tokens.shape
    half = cols // 2
    own = rows_here * cols
    wide = gm.shape[1]
    whole = lambda *shape: pl.BlockSpec(shape, lambda l, m: (l,) + (0,) * (len(shape) - 1))
    return pl.pallas_call(
        leave_kernel,
        out_shape=(
            jax.ShapeDtypeStruct((latents, rows_here, cols, D), F32),
            jax.ShapeDtypeStruct((latents, 9, D), F32),
            jax.ShapeDtypeStruct((latents, 2, D), F32),
        ),
        grid_spec=pltpu.PrefetchScalarGridSpec(
            num_scalar_prefetch=1,
            grid=(latents,),
            in_specs=[
                whole(4, wide, D),
                whole(1, rows_here, cols, D),
                whole(1, 1, cols, D),
                whole(1, 1, cols, D),
                whole(1, own, D),
                whole(1, 6, D),
                pl.BlockSpec((9, D), lambda l, m: (0, 0)),
            ],
            out_specs=(whole(1, rows_here, cols, D), whole(1, 9, D), whole(1, 2, D)),
            scratch_shapes=[
                pltpu.VMEM((rows_here + 2, LANE_PARTS, cols, 128), F32),
                pltpu.VMEM((rows_here + 2, 4, half, D), F32),
                pltpu.VMEM((rows_here + 2, 4, half, D), F32),
                pltpu.VMEM((rows_here, LANE_PARTS, cols, 128), F32),
                pltpu.VMEM((rows_here + 2, 2, half, D), F32),
                pltpu.VMEM((rows_here + 2, 2, half, 128), F32),
                pltpu.VMEM((11, 8, D), F32),
            ],
        ),
        compiler_params=pltpu.CompilerParams(vmem_limit_bytes=VMEM_LIMIT),
        cost_estimate=pl.CostEstimate(flops=10_000_000_000, bytes_accessed=4_000_000, transcendentals=0),
        name="leave",
    )(meta, gm, tokens, top, bot, after_grad, pieces, kern)


def pair_parts(values):
    lanes = lax.broadcasted_iota(jnp.int32, values.shape, 1)
    first = lanes < HEAD_DIM
    zero = jnp.zeros_like(values)
    return jnp.where(first, values, zero), jnp.where(first, zero, values)


def attend_kernel(offset, mixed, wq, wk, wvt, bias, out, lse_out, padded):
    tokens = mixed.shape[0]
    strips, window, _ = out.shape
    step = tokens // strips
    margin = window - step
    m = mixed[...]
    query = (mm(m, wq[...]).astype(BF16) * FACTOR).astype(BF16)
    key = mm(m, wk[...]).astype(BF16)
    value_t = mm(wvt[...], m, NT).astype(BF16)
    keep = jnp.tile(bias[...], (1, tokens // 128))

    def score(h):
        cut = slice(h // 2 * PAIR, (h // 2 + 1) * PAIR)
        return mm(pair_parts(key[:, cut])[h % 2], query[:, cut], NT)

    scores = {0: score(0), 1: score(1)}
    parts = []
    for h in range(4):
        masked = scores.pop(h) + keep
        peak = jnp.max(masked, axis=0, keepdims=True)
        raw = jnp.exp(masked - peak)
        if h + 2 < 4:
            scores[h + 2] = score(h + 2)
        total = jnp.sum(raw, axis=0, keepdims=True)
        prob = (raw * (1.0 / total)).astype(BF16)
        parts.append(mm(value_t[h * HEAD_DIM : (h + 1) * HEAD_DIM], prob))
        lse_out[0, h : h + 1, :] = peak + jnp.log(total)
    padded[0:margin] = jnp.zeros((margin, QUAD), F32)
    padded[margin + tokens :] = jnp.zeros((margin, QUAD), F32)
    padded[margin : margin + tokens] = jnp.concatenate(parts, axis=0).T
    for s in range(strips):
        start = pl.multiple_of(offset[0] + s * step, 8)
        out[s] = padded[pl.ds(start, window), :].astype(BF16)


def attend(offset, mixed, weight, weight_t, bias, strips, window):
    tokens = mixed.shape[0]
    margin = window - tokens // strips
    return pl.pallas_call(
        attend_kernel,
        out_shape=(
            jax.ShapeDtypeStruct((strips, window, D), BF16),
            jax.ShapeDtypeStruct((QUADS, 4, tokens), F32),
        ),
        grid_spec=pltpu.PrefetchScalarGridSpec(
            num_scalar_prefetch=1,
            grid=(QUADS,),
            in_specs=[
                pl.BlockSpec((tokens, D), lambda p, o: (0, 0)),
                pl.BlockSpec((D, QUAD), lambda p, o: (0, p)),
                pl.BlockSpec((D, QUAD), lambda p, o: (0, QUADS + p)),
                pl.BlockSpec((QUAD, D), lambda p, o: (2 * QUADS + p, 0)),
                pl.BlockSpec((tokens, 128), lambda p, o: (0, 0)),
            ],
            out_specs=(
                pl.BlockSpec((strips, window, QUAD), lambda p, o: (0, 0, p)),
                pl.BlockSpec((1, 4, tokens), lambda p, o: (p, 0, 0)),
            ),
            scratch_shapes=[pltpu.VMEM((tokens + 2 * margin, QUAD), F32)],
        ),
        compiler_params=pltpu.CompilerParams(vmem_limit_bytes=VMEM_LIMIT),
        cost_estimate=pl.CostEstimate(flops=16_000_000_000, bytes_accessed=4_000_000, transcendentals=0),
        name="attend",
    )(offset, mixed, weight, weight, weight_t, bias)


def attend_back_kernel(offset, query, key, value, key_t, bias, lse, gatt, wq, wk, wv, mixed_t, send_out, keep_out, gm_out, acc, part):
    tokens = query.shape[0]
    strips, window, _ = gm_out.shape
    step = tokens // strips
    margin = window - step
    p = pl.program_id(0)
    keep = jnp.tile(bias[...], (1, tokens // 128))

    def pair(k):
        cut = slice(k * PAIR, (k + 1) * PAIR)
        q, grad = query[:, cut], gatt[:, cut]
        keys, values = pair_parts(key[:, cut]), pair_parts(value[:, cut])
        return [(mm(keys[e], q, NT), mm(values[e], grad, NT)) for e in range(2)]

    def soften(k, e, score, grad_prob):
        h = 2 * k + e
        prob = jnp.exp(score * FACTOR + keep - lse[0, h : h + 1, :])
        delta = jnp.sum(prob * grad_prob, axis=0, keepdims=True)
        return prob.astype(BF16), (prob * (grad_prob - delta)).astype(BF16)

    def finish(k, probs, grad_scores):
        cut = slice(k * PAIR, (k + 1) * PAIR)
        queries, grads = pair_parts(query[:, cut]), pair_parts(gatt[:, cut])
        dv = mm(jnp.concatenate(probs, axis=1), jnp.concatenate(grads, axis=0))
        dk = mm(jnp.concatenate(grad_scores, axis=1), jnp.concatenate(queries, axis=0)) * FACTOR
        rows = [key_t[(2 * k + e) * HEAD_DIM : (2 * k + e + 1) * HEAD_DIM] for e in range(2)]
        parts = [mm(rows[e], grad_scores[e]) for e in range(2)]
        dq = jnp.concatenate(parts, axis=0).T * FACTOR
        return dq.astype(BF16), dk.astype(BF16), dv.astype(BF16)

    first = pair(0)
    soft = [soften(0, e, *first[e]) for e in range(2)]
    then = pair(1)
    one = finish(0, [v[0] for v in soft], [v[1] for v in soft])
    soft = [soften(1, e, *then[e]) for e in range(2)]
    two = finish(1, [v[0] for v in soft], [v[1] for v in soft])
    all_three = jnp.concatenate([v for k in range(3) for v in (one[k], two[k])], axis=1)
    part[...] = mm(mixed_t[...], all_three)
    size = D // 4
    for y in range(2):
        mine = pl.multiple_of((2 * y + offset[1]) * size, 8)
        other = pl.multiple_of((2 * y + 1 - offset[1]) * size, 8)
        for k in range(3):
            cut = slice(k * QUAD, (k + 1) * QUAD)
            keep_out[k, y] = part[pl.ds(mine, size), cut].astype(BF16)
            send_out[k, y] = part[pl.ds(other, size), cut].astype(BF16)
    total = mm(all_three, jnp.concatenate([wq[...], wk[...], wv[...]], axis=1), NT)

    @pl.when(p == 0)
    def _():
        acc[0:margin] = jnp.zeros((margin, D), F32)
        acc[margin + tokens :] = jnp.zeros((margin, D), F32)
        acc[margin : margin + tokens] = total

    @pl.when(p > 0)
    def _():
        acc[margin : margin + tokens] += total

    @pl.when(p == pl.num_programs(0) - 1)
    def _():
        for s in range(strips):
            start = pl.multiple_of(offset[0] + s * step, 8)
            gm_out[s] = acc[pl.ds(start, window), :].astype(BF16)


def attend_back(offset, triple, key_t, bias, lse, gatt, weight, mixed_t, strips, window):
    tokens = triple.shape[0]
    margin = window - tokens // strips
    part = lambda k: pl.BlockSpec((tokens, QUAD), lambda p, o: (0, k * QUADS + p))
    slab = lambda k: pl.BlockSpec((D, QUAD), lambda p, o: (0, k * QUADS + p))
    parts = jax.ShapeDtypeStruct((3, 2, D // 4, D), BF16)
    parts_spec = pl.BlockSpec((3, 2, D // 4, QUAD), lambda p, o: (0, 0, 0, p))
    return pl.pallas_call(
        attend_back_kernel,
        out_shape=(
            parts,
            parts,
            jax.ShapeDtypeStruct((strips, window, D), BF16),
        ),
        grid_spec=pltpu.PrefetchScalarGridSpec(
            num_scalar_prefetch=1,
            grid=(QUADS,),
            in_specs=[
                part(0),
                part(1),
                part(2),
                pl.BlockSpec((QUAD, tokens), lambda p, o: (p, 0)),
                pl.BlockSpec((tokens, 128), lambda p, o: (0, 0)),
                pl.BlockSpec((1, 4, tokens), lambda p, o: (p, 0, 0)),
                part(0),
                slab(0),
                slab(1),
                slab(2),
                pl.BlockSpec((D, tokens), lambda p, o: (0, 0)),
            ],
            out_specs=(
                parts_spec,
                parts_spec,
                pl.BlockSpec((strips, window, D), lambda p, o: (0, 0, 0)),
            ),
            scratch_shapes=[
                pltpu.VMEM((tokens + 2 * margin, D), F32),
                pltpu.VMEM((D, 3 * QUAD), F32),
            ],
        ),
        compiler_params=pltpu.CompilerParams(vmem_limit_bytes=VMEM_LIMIT),
        cost_estimate=pl.CostEstimate(flops=23_000_000_000, bytes_accessed=4_000_000, transcendentals=0),
        name="attend_back",
    )(offset, triple, triple, triple, key_t, bias, lse, gatt, weight, weight, weight, mixed_t)


def from_before(values, axis):
    count = lax.axis_size(axis)
    return lax.ppermute(values, axis, [(i, i + 1) for i in range(count - 1)])


def from_after(values, axis):
    count = lax.axis_size(axis)
    return lax.ppermute(values, axis, [(i + 1, i) for i in range(count - 1)])


def swap(values):
    return lax.all_to_all(values, "seq", 0, 0, tiled=False)


BITS = {"y": ("batch", 2), "c": ("batch", 1), "h": ("seq", 4), "l": ("seq", 2), "x": ("seq", 1)}
ORDER = "ychlx"


def blocks_of(values):
    return values.reshape(values.shape[:-2] + (2, 2, 2, 2, 2, values.shape[-2] // 32, values.shape[-1]))


def split(values, dims, bit):
    axis, mask = BITS[bit]
    mine = (lax.axis_index(axis) // mask) % 2
    at = values.ndim - 2 - len(dims) + dims.index(bit)
    send = lax.dynamic_index_in_dim(values, 1 - mine, at, keepdims=False)
    keep = lax.dynamic_index_in_dim(values, mine, at, keepdims=False)
    return send, keep, dims.replace(bit, "")


def hop(values, bit):
    axis, mask = BITS[bit]
    count = lax.axis_size(axis)
    return lax.ppermute(values, axis, [(i, i ^ mask) for i in range(count)])


def add(keep, got):
    return keep.astype(F32) + got.astype(F32)


def after(values, *others):
    return lax.optimization_barrier((values,) + others)[0]


STEPS = ("yxl", "xly", "lyx")


def step_of(parts, dims, step):
    cut = [split(part, left, order[step]) for part, left, order in zip(parts, dims, STEPS)]
    return tuple(c[0] for c in cut), tuple(c[1] for c in cut), [c[2] for c in cut]


def hops_of(sends, step):
    return tuple(hop(send, order[step]) for send, order in zip(sends, STEPS))


def fold_of(keeps, gots):
    return [add(keep, got).astype(BF16) for keep, got in zip(keeps, gots)]


def reduce_rest(values, dims, order):
    for bit in order:
        send, keep, dims = split(values.astype(BF16), dims, bit)
        values = add(keep, hop(send, bit))
    return values


def scatter_rows(values):
    return lax.psum_scatter(values, ("batch", "seq"), scatter_dimension=0, tiled=True).astype(F32)


def payload_of(common, sliced):
    seq_count, batch_count = lax.axis_size("seq"), lax.axis_size("batch")
    flat = common.reshape(1, -1)
    pieces = [jnp.broadcast_to(flat, (seq_count, flat.shape[1]))]
    for values in sliced:
        cut = values.reshape(values.shape[0], batch_count, seq_count, -1).transpose(2, 1, 0, 3)
        pieces.append(cut.reshape(seq_count, -1))
    whole = jnp.concatenate(pieces, axis=1)
    return jnp.pad(whole, ((0, 0), (0, -whole.shape[1] % 1024))).reshape(seq_count, -1, 128)


def unpack(gathered, common, sliced):
    seq_count, batch_count = lax.axis_size("seq"), lax.axis_size("batch")
    gathered = gathered.reshape(batch_count, -1)
    at = common.size
    common_all = gathered[:, :at].reshape((batch_count,) + common.shape)
    own = []
    for values in sliced:
        size = values.size // seq_count
        part = jnp.sum(gathered[:, at : at + size], axis=0)
        part = part.reshape(batch_count, values.shape[0], -1)
        own.append(lax.dynamic_index_in_dim(part, lax.axis_index("batch"), 0, keepdims=False))
        at += size
    return common_all, own


def windows_of(values, offset, margin, strips):
    step = values.shape[0] // strips
    padded = jnp.pad(values, ((margin, margin), (0, 0)))
    base = lax.dynamic_slice_in_dim(padded, offset, values.shape[0] + margin)
    return jnp.stack([base[s * step : s * step + step + margin] for s in range(strips)])


def attend_plain(mixed, weight, ok, heads):
    wide = heads * HEAD_DIM
    triple = mm(mixed, weight).astype(BF16)
    split = lambda k: triple[:, k * wide : (k + 1) * wide].reshape(-1, heads, HEAD_DIM)
    queries, keys, values = split(0), split(1), split(2)
    scores = jnp.einsum("qhe,khe->hqk", queries, keys, preferred_element_type=F32) * FACTOR
    scores = jnp.where(ok[None, None, :], scores, -1e30)
    prob = jax.nn.softmax(scores, axis=-1)
    out = jnp.einsum("hqk,khe->qhe", prob.astype(BF16), values, preferred_element_type=F32)
    return out.reshape(-1, wide).astype(BF16), (queries, keys, values, prob)


def attend_plain_back(saved, grad, weight):
    queries, keys, values, prob = saved
    heads = queries.shape[1]
    grad = grad.reshape(-1, heads, HEAD_DIM)
    grad_prob = jnp.einsum("qhe,khe->hqk", grad, values, preferred_element_type=F32)
    delta = jnp.sum(prob * grad_prob, axis=-1, keepdims=True)
    grad_scores = (prob * (grad_prob - delta)).astype(BF16)
    dq = jnp.einsum("hqk,khe->qhe", grad_scores, keys, preferred_element_type=F32) * FACTOR
    dk = jnp.einsum("hqk,qhe->khe", grad_scores, queries, preferred_element_type=F32) * FACTOR
    dv = jnp.einsum("hqk,qhe->khe", prob.astype(BF16), grad, preferred_element_type=F32)
    flat = lambda v: v.reshape(v.shape[0], -1).astype(BF16)
    grads = jnp.concatenate([flat(dq), flat(dk), flat(dv)], axis=1)
    return grads, mm(grads, weight, NT)


def shards(
    tokens,
    cotangent,
    timestep,
    class_ids,
    heights,
    widths,
    time_weight,
    class_table,
    ada_weight,
    ada_bias,
    conv_attn,
    qkv_weight,
    proj_weight,
    up_weight,
    conv_ffn,
    down_weight,
):
    latents, rows_here, cols, _ = tokens.shape
    half = cols // 2
    seq_count = lax.axis_size("seq")
    seq_place = lax.axis_index("seq")
    batch_count = lax.axis_size("batch")
    batch_place = lax.axis_index("batch")
    devices = batch_count * seq_count
    blocks = latents * 4
    share = seq_count // blocks
    per_group = rows_here // 2 * half
    group_tokens = seq_count * per_group

    first, last = tokens[:, :1], tokens[:, rows_here - 1 :]
    top = from_before(last, "seq")
    bot = from_after(first, "seq")

    half_freq = time_weight.shape[0] // 2
    frequency = jnp.exp(-math.log(10000.0) * jnp.arange(half_freq, dtype=F32) / half_freq)
    angles = timestep.astype(F32)[:, None] * frequency[None, :]
    embedding = jnp.concatenate([jnp.cos(angles), jnp.sin(angles)], axis=1).astype(BF16)
    one_hot = (
        class_ids[:, None] == jnp.arange(class_table.shape[0], dtype=jnp.int32)[None, :]
    ).astype(BF16)
    condition = mm(embedding, time_weight) + mm(one_hot, class_table)
    logistic = jax.nn.sigmoid(condition)
    activated_cond = (condition * logistic).astype(BF16)
    lead = mm(activated_cond, ada_weight[:, : 2 * D]) + ada_bias[: 2 * D]
    meta = jnp.concatenate(
        [heights, widths, jnp.reshape(seq_place * rows_here, (1,))]
    ).astype(jnp.int32)
    core = jnp.reshape(batch_place % 2, (1,)).astype(jnp.int32)

    mixed = enter(meta, tokens, top, bot, lead, conv_attn)
    late_cond = after(activated_cond, mixed)
    pieces = mm(late_cond, ada_weight[:, 2 * D :]) + ada_bias[2 * D :]
    pieces = jnp.concatenate([lead, pieces], axis=1).reshape(latents, 6, D)
    sent = mixed.reshape(blocks, 1, per_group, D)
    sent = jnp.broadcast_to(sent, (blocks, share, per_group, D)).reshape(seq_count, per_group, D)
    grouped = swap(sent).reshape(group_tokens, D)

    weight_t = qkv_weight.T

    my_block = seq_place // share
    my_latent = my_block // 4
    my_a = (my_block // 2) % 2
    my_b = my_block % 2
    places = jnp.arange(group_tokens, dtype=jnp.int32)
    key_row = places // half * 2 + my_a
    key_col = places % half * 2 + my_b
    height = lax.dynamic_index_in_dim(heights, my_latent, 0, keepdims=False)
    width = lax.dynamic_index_in_dim(widths, my_latent, 0, keepdims=False)
    key_ok = (key_row < height) & (key_col < width)

    margin = half
    tall = per_group + margin
    offset = jnp.stack([margin * (1 - my_a), batch_place % 2]).astype(jnp.int32)
    if share == 1:
        bias = jnp.broadcast_to(jnp.where(key_ok, 0.0, -1e30)[:, None], (group_tokens, 128))
        windows, lse = attend(offset, grouped, qkv_weight, weight_t, bias, seq_count, tall)
        attended = swap(windows)
    else:
        heads = HEADS // share
        wide = heads * HEAD_DIM
        chunk = seq_place % share
        thirds = qkv_weight.reshape(D, 3, share, wide)
        my_weight = lax.dynamic_index_in_dim(thirds, chunk, 2, keepdims=False).reshape(D, 3 * wide)
        att, saved = attend_plain(grouped, my_weight, key_ok, heads)
        windows = windows_of(att, offset[0], margin, seq_count)
        attended = swap(windows).reshape(blocks, share, tall, wide)
        attended = attended.transpose(0, 2, 1, 3).reshape(blocks, tall, D)

    ge, get, cot_split = prepare_cot(cotangent, pieces)
    conditions = lax.all_gather(
        jnp.concatenate([condition, embedding.astype(F32), class_ids.astype(F32)[:, None]], axis=1),
        "batch",
        axis=0,
    )
    if share == 1:
        triple = mm(grouped, qkv_weight).astype(BF16)
        key_t = mm(weight_t[D : 2 * D], grouped, NT).astype(BF16)
        grouped_t = grouped.T
        attended, ge, triple, key_t, grouped_t, conditions = lax.optimization_barrier(
            (attended, ge, triple, key_t, grouped_t, conditions)
        )
    e2, e2t, after_attn, branch = second(
        meta, attended, tokens, top, bot, pieces, proj_weight
    )
    expanded, grad_e2, edge_first, edge_last, send_c, keep_c, conv_ffn_part = ffn(
        core, e2, e2t, ge, get, up_weight, down_weight, conv_ffn, cols
    )
    halving = batch_count == 4 and seq_count == 8
    if halving:
        got_c = hop(send_c, "c")
    low = from_before(edge_last, "seq")
    high = from_after(edge_first, "seq")
    output, gate_sums = finish_output(expanded, after_attn, cot_split, pieces, rows_here, cols)
    grad_after, grad_branch, grad_attended, mid_sums = middle(
        meta, grad_e2, low, high, after_attn, branch, cot_split, pieces, proj_weight
    )

    att_all = after(attended, grad_attended)
    starts = [margin * ((k // 2) % 2) for k in range(blocks)]
    att_own = jnp.concatenate([att_all[k, at : at + per_group] for k, at in enumerate(starts)])
    flat_branch = grad_branch.reshape(blocks * per_group, D)
    hidden = conv_ffn.shape[1]
    if share == 1:
        gatt = swap(grad_attended.reshape(seq_count, per_group, D)).reshape(group_tokens, D)
        if halving:
            keep_c = after(keep_c, grad_attended)
            sums = add(keep_c, got_c).astype(BF16).reshape(2, 2, 2, 2, 2, D // devices, hidden)
            third = hidden // 3
            cuts = [sums[..., k * third : (k + 1) * third] for k in range(3)]
            sends, keeps, dims = step_of(cuts, ["yhlx"] * 3, 0)
            late_branch = after(flat_branch, got_c)
            proj_grad = mm(att_own, late_branch, (((0,), (0,)), ((), ()))).astype(BF16)
            send_p, keep_p, _ = split(blocks_of(proj_grad), ORDER, "c")
            got_p = hop(send_p, "c")
            gatt, sends, send_p, gate_sums = lax.optimization_barrier((gatt, sends, send_p, gate_sums))
            gots = hops_of(sends, 0)
        send_r, keep_r, gm_windows = attend_back(
            offset, triple, key_t, bias, lse, gatt, qkv_weight, grouped_t, seq_count, tall
        )
        gm = swap(gm_windows)
        if halving:
            gm_windows, gots = lax.optimization_barrier((gm_windows, gots))
        gm = swap(gm_windows)
    else:
        sent = grad_attended.reshape(blocks, per_group, share, wide).transpose(0, 2, 1, 3)
        gatt = swap(sent.reshape(seq_count, per_group, wide)).reshape(group_tokens, wide)
        grad_triple, gm_part = attend_plain_back(saved, gatt, my_weight)
        gm_windows = windows_of(gm_part.astype(BF16), offset[0], margin, seq_count)
        gm = swap(gm_windows).reshape(blocks, share, tall, D)
        gm = jnp.sum(gm.astype(F32), axis=1).astype(BF16)
        own_grad = mm(grouped, grad_triple, (((0,), (0,)), ((), ()))).astype(BF16)
        spread = jnp.zeros((D, 3, share, wide), BF16)
        qkv_grad = lax.dynamic_update_index_in_dim(
            spread, own_grad.reshape(D, 3, wide), chunk, 2
        ).reshape(D, 3 * D)
        proj_grad = mm(att_own, flat_branch, (((0,), (0,)), ((), ()))).astype(BF16)
        rest = jnp.concatenate([qkv_grad, proj_grad], axis=1)

    if halving:
        got_r = hop(send_r, "c")
        keeps = lax.optimization_barrier((keeps, keep_r))[0]
        sends, keeps, dims = step_of(fold_of(keeps, gots), dims, 1)
        sums = add(keep_r, got_r).astype(BF16).reshape(3, 2, 2, 2, 2, D // devices, D)
        sums_p = add(keep_p, got_p).astype(BF16)
        send_one, keep_one, dims_one = split(sums[:2], "yhlx", "y")
        send_two, keep_two, dims_two = split(jnp.stack([sums[2], sums_p]), "yhlx", "x")
        gm = after(gm, *sends)
        gots = hops_of(sends, 1)
        got_one, got_two = hop(send_one, "y"), hop(send_two, "x")
    total = batch_count * latents

    here = batch_place * seq_count + seq_place
    own_cols = D // devices
    conditions = conditions.reshape(total, -1)
    condition_all = conditions[:, :D]
    embedding_all = conditions[:, D : D + embedding.shape[1]]
    ids_all = conditions[:, -1].astype(jnp.int32)
    logistic_all = jax.nn.sigmoid(condition_all)
    activated_all = (condition_all * logistic_all).astype(BF16).astype(F32)
    slope_all = logistic_all * (1.0 + condition_all * (1.0 - logistic_all))

    def back_through(grads):
        high = lax.reduce_precision(grads, 8, 7)
        middle_term = lax.reduce_precision(grads - high, 8, 7)
        low = grads - high - middle_term
        product = mm(jnp.concatenate([high, middle_term, low]).astype(BF16), ada_weight, NT)
        return product[:total] + product[total : 2 * total] + product[2 * total :]

    token_grad, conv_attn_part, end_sums = leave(
        meta, gm, tokens, top, bot, grad_after, pieces, conv_attn
    )

    common = jnp.concatenate([end_sums, mid_sums, gate_sums], axis=1)
    sliced = (jnp.sum(conv_attn_part, axis=0), conv_ffn_part)
    message = payload_of(common, sliced)
    if halving:
        message, keeps, gots, keep_one, keep_two = lax.optimization_barrier(
            (message, keeps, gots, keep_one, keep_two)
        )
        sends, keeps, dims = step_of(fold_of(keeps, gots), dims, 2)
        gots = hops_of(sends, 2)
        pair = jnp.concatenate(fold_of(keeps, gots), axis=-1)
        send_h, keep_h, _ = split(pair, dims[0], "h")
        got_h = hop(send_h, "h")
        send_one, keep_one, dims_one = split(add(keep_one, got_one).astype(BF16), dims_one, "x")
        send_two, keep_two, dims_two = split(add(keep_two, got_two).astype(BF16), dims_two, "y")
        got_one, got_two = hop(send_one, "x"), hop(send_two, "y")
    gathered = lax.all_gather(jnp.sum(swap(message), axis=0), "batch", axis=0)
    if halving:
        gathered, keep_one, keep_two, keep_h = lax.optimization_barrier(
            (gathered, keep_one, keep_two, keep_h)
        )
        pair = add(keep_h, got_h)
        down_rows, up_rows = pair[0], pair[1]
        rest_rows = jnp.concatenate([add(keep_one, got_one), add(keep_two, got_two)])
        send_l, keep_l, dims_l = split(rest_rows.astype(BF16), dims_one, "l")
        got_l = hop(send_l, "l")
    else:
        whole = jnp.stack([keep_c, send_c])
        whole = jnp.where(core[0] == 0, whole, whole[::-1]).transpose(1, 2, 0, 3, 4)
        whole = whole.reshape(2, D, hidden)
        down_rows, up_rows = scatter_rows(whole[0]), scatter_rows(whole[1])
        if share == 1:
            rest = jnp.stack([keep_r, send_r])
            rest = jnp.where(core[0] == 0, rest, rest[::-1]).transpose(2, 0, 3, 1, 4).reshape(D, -1)
            proj_grad = mm(att_own, flat_branch, (((0,), (0,)), ((), ()))).astype(BF16)
            rest = jnp.concatenate([rest, proj_grad], axis=1)
        rest_rows = scatter_rows(rest).reshape(own_cols, 4, D).transpose(1, 0, 2)
    all_sums, (conv_attn_grad, conv_ffn_grad) = unpack(gathered, common, sliced)

    grad_pieces = all_sums.reshape(total, 6 * D)
    grad_silu = back_through(grad_pieces)
    if halving:
        grad_silu, got_l = lax.optimization_barrier((grad_silu, got_l))
        rest_rows = reduce_rest(add(keep_l, got_l), dims_l, "h")
    qkv_rows = jnp.concatenate([rest_rows[0], rest_rows[1], rest_rows[2]], axis=1)
    proj_rows = rest_rows[3]
    cond_all = grad_silu * slope_all
    cond_grad = lax.dynamic_slice_in_dim(cond_all, batch_place * latents, latents)
    cond_cols = lax.dynamic_slice_in_dim(cond_all, here * own_cols, own_cols, axis=1)
    act_cols = lax.dynamic_slice_in_dim(activated_all, here * own_cols, own_cols, axis=1)
    outer = lambda left, right: lax.dot_general(
        left, right, (((0,), (0,)), ((), ())), precision=HIGHEST, preferred_element_type=F32
    )
    hot_all = (ids_all[:, None] == jnp.arange(class_table.shape[0], dtype=jnp.int32)[None, :]).astype(F32)
    bias_cols = 6 * D // devices
    bias_grad = jnp.sum(
        lax.dynamic_slice_in_dim(grad_pieces, here * bias_cols, bias_cols, axis=1), axis=0
    )
    return (
        output,
        token_grad,
        cond_grad,
        outer(embedding_all, cond_cols),
        outer(hot_all, cond_cols),
        outer(act_cols, grad_pieces),
        bias_grad,
        conv_attn_grad,
        qkv_rows,
        proj_rows,
        up_rows,
        conv_ffn_grad,
        down_rows.T,
    )


def solution(mesh):
    strips = P("batch", "seq", None, None)
    in_specs = (strips, strips) + (P("batch"),) * 4 + (P(),) * 10
    both = ("batch", "seq")
    out_specs = (
        strips,
        strips,
        P("batch", None),
        P(None, both),
        P(None, both),
        P(both, None),
        P(both),
        P(None, both),
        P(both, None),
        P(both, None),
        P(both, None),
        P(None, both),
        P(None, both),
    )
    return jax.shard_map(shards, mesh=mesh, in_specs=in_specs, out_specs=out_specs, check_vma=False)
```

```python
import functools
import math

import jax
import jax.numpy as jnp
from jax import lax
from jax.experimental import pallas as pl
from jax.experimental.pallas import tpu as pltpu
from jax.sharding import PartitionSpec as P

D = 768
HEADS = 12
HEAD_DIM = 64
PAIR = 2 * HEAD_DIM
QUAD = 2 * PAIR
QUADS = HEADS // 4
FF_BLOCK = 256
LANE_PARTS = D // 128
FACTOR = HEAD_DIM ** (-0.5)

F32 = jnp.float32
BF16 = jnp.bfloat16
HIGHEST = lax.Precision.HIGHEST
NN = (((1,), (0,)), ((), ()))
NT = (((1,), (1,)), ((), ()))
VMEM_LIMIT = 60 * 1024 * 1024


def mm(left, right, dims=NN):
    return lax.dot_general(left, right, dims, preferred_element_type=F32)


def shift_down(values):
    rows = lax.broadcasted_iota(jnp.int32, values.shape, 0)
    return jnp.where(rows == 0, 0.0, pltpu.roll(values, 1, 0))


def shift_up(values):
    count = values.shape[0]
    rows = lax.broadcasted_iota(jnp.int32, values.shape, 0)
    return jnp.where(rows == count - 1, 0.0, pltpu.roll(values, count - 1, 0))


def put_shifts(ref, row, parity, values):
    ref[row, 1 + parity] = values
    if parity == 0:
        ref[row, 3] = shift_up(values)
    else:
        ref[row, 0] = shift_down(values)


def normalize(values):
    centre = values - jnp.mean(values, axis=-1, keepdims=True)
    spread = jnp.mean(centre * centre, axis=-1, keepdims=True)
    scaled = lax.rsqrt(spread + 1e-06)
    return centre * scaled, scaled


def norm_back(grad_norm, normed, scaled):
    return scaled * (
        grad_norm
        - jnp.mean(grad_norm, axis=-1, keepdims=True)
        - normed * jnp.mean(grad_norm * normed, axis=-1, keepdims=True)
    )


def put_row(buf, row, values):
    for k in range(LANE_PARTS):
        buf[row, k] = values[:, 128 * k : 128 * (k + 1)]


def get_row(buf, row):
    return jnp.concatenate([buf[row, k] for k in range(LANE_PARTS)], axis=1)


def put_columns(buf, row, parity, values):
    for k in range(LANE_PARTS):
        buf[row, k, pl.ds(parity, values.shape[0], stride=2), :] = values[:, 128 * k : 128 * (k + 1)]


def get_columns(buf, row, parity):
    half = buf.shape[2] // 2
    return jnp.concatenate(
        [buf[row, k, pl.ds(parity, half, stride=2), :] for k in range(LANE_PARTS)], axis=1
    )


def usable_of(meta, latents, latent, row, parity, half):
    cols = 2 * lax.broadcasted_iota(jnp.int32, (half, 1), 0) + parity
    row_ok = jnp.logical_and(row >= 0, row < meta[latent])
    limit = jnp.where(row_ok, meta[latents + latent], 0)
    return (cols < limit).astype(F32)


def sum8(values):
    total = values[0:8]
    for start in range(8, values.shape[0], 8):
        total = total + values[start : start + 8]
    return total


def enter_kernel(meta, tok, top, bot, lead, kern, out, buf, ent):
    latents = pl.num_programs(0)
    latent = pl.program_id(0)
    rows_here, cols = tok.shape[1], tok.shape[2]
    half = cols // 2
    row0 = meta[2 * latents]
    shift = lead[pl.ds(latent, 1), :D]
    scale = 1.0 + lead[pl.ds(latent, 1), D:]
    taps = [kern[t : t + 1, :].astype(F32) for t in range(9)]
    for rr in range(rows_here + 2):
        source = top[0, 0] if rr == 0 else bot[0, 0] if rr == rows_here + 1 else tok[0, rr - 1]
        put_row(buf, rr, source.astype(F32))
        for parity in range(2):
            normed, _ = normalize(get_columns(buf, rr, parity))
            ok = usable_of(meta, latents, latent, row0 + rr - 1, parity, half)
            put_shifts(ent, rr, parity, ((normed * scale + shift) * ok).astype(BF16).astype(F32))
    for row in range(rows_here):
        for parity in range(2):
            total = jnp.zeros((half, D), F32)
            for i in range(3):
                for j in range(3):
                    total = total + ent[row + i, parity + j] * taps[3 * i + j]
            mixed = (ent[row + 1, 1 + parity] + total).astype(BF16)
            group = 2 * (row % 2) + parity
            out[0, group, (row // 2) * half : (row // 2 + 1) * half, :] = mixed


def enter(meta, tokens, top, bot, lead, kern):
    latents, rows_here, cols, _ = tokens.shape
    half = cols // 2
    per_group = rows_here // 2 * half
    whole = lambda *shape: pl.BlockSpec(shape, lambda l, m: (l,) + (0,) * (len(shape) - 1))
    return pl.pallas_call(
        enter_kernel,
        out_shape=jax.ShapeDtypeStruct((latents, 4, per_group, D), BF16),
        grid_spec=pltpu.PrefetchScalarGridSpec(
            num_scalar_prefetch=1,
            grid=(latents,),
            in_specs=[
                whole(1, rows_here, cols, D),
                whole(1, 1, cols, D),
                whole(1, 1, cols, D),
                pl.BlockSpec((latents, 2 * D), lambda l, m: (0, 0)),
                pl.BlockSpec((9, D), lambda l, m: (0, 0)),
            ],
            out_specs=whole(1, 4, per_group, D),
            scratch_shapes=[
                pltpu.VMEM((rows_here + 2, LANE_PARTS, cols, 128), F32),
                pltpu.VMEM((rows_here + 2, 4, half, D), F32),
            ],
        ),
        compiler_params=pltpu.CompilerParams(vmem_limit_bytes=VMEM_LIMIT),
        cost_estimate=pl.CostEstimate(flops=6_000_000_000, bytes_accessed=4_000_000, transcendentals=0),
        name="enter",
    )(meta, tokens, top, bot, lead, kern)


def cot_kernel(cot, pieces, ge_out, get_out, cot_out, buf):
    rows_here, cols = cot.shape[1], cot.shape[2]
    half = cols // 2
    gate = pieces[0, 5:6, :]
    for row in range(rows_here):
        put_row(buf, row, cot[0, row].astype(F32))
        for parity in range(2):
            values = get_columns(buf, row, parity)
            at = (2 * row + parity) * half
            ge_out[0, at : at + half, :] = (gate * values).astype(BF16)
            cot_out[0, at : at + half, :] = values.astype(BF16)
    get_out[0] = ge_out[0].astype(F32).T.astype(BF16)


def prepare_cot(cotangent, pieces):
    latents, rows_here, cols, _ = cotangent.shape
    whole = lambda *shape: pl.BlockSpec(shape, lambda l: (l,) + (0,) * (len(shape) - 1))
    own = rows_here * cols
    return pl.pallas_call(
        cot_kernel,
        out_shape=(
            jax.ShapeDtypeStruct((latents, own, D), BF16),
            jax.ShapeDtypeStruct((latents, D, own), BF16),
            jax.ShapeDtypeStruct((latents, own, D), BF16),
        ),
        grid=(latents,),
        in_specs=[whole(1, rows_here, cols, D), whole(1, 6, D)],
        out_specs=(whole(1, own, D), whole(1, D, own), whole(1, own, D)),
        scratch_shapes=[pltpu.VMEM((rows_here, LANE_PARTS, cols, 128), F32)],
        compiler_params=pltpu.CompilerParams(vmem_limit_bytes=VMEM_LIMIT),
        cost_estimate=pl.CostEstimate(flops=4_000_000_000, bytes_accessed=4_000_000, transcendentals=0),
        name="prepare_cot",
    )(cotangent, pieces)


def second_kernel(meta, att, tok, top, bot, pieces, proj, e2_out, e2t_out, after_out, branch_out, buf, bran):
    latents = pl.num_programs(0)
    latent = pl.program_id(0)
    rows_here, cols = tok.shape[1], tok.shape[2]
    half = cols // 2
    row0 = meta[2 * latents]
    gate = pieces[0, 2:3, :]
    shift = pieces[0, 3:4, :]
    scale = 1.0 + pieces[0, 4:5, :]
    for group in range(4):
        bran[group] = mm(att[group], proj[...])
    for rr in range(rows_here + 2):
        source = top[0, 0] if rr == 0 else bot[0, 0] if rr == rows_here + 1 else tok[0, rr - 1]
        put_row(buf, rr, source.astype(F32))
        for parity in range(2):
            group = 2 * ((rr + 1) % 2) + parity
            branch = bran[group, (rr // 2) * half : (rr // 2 + 1) * half, :]
            after = get_columns(buf, rr, parity) + gate * branch
            normed, _ = normalize(after)
            ok = usable_of(meta, latents, latent, row0 + rr - 1, parity, half)
            at = (2 * rr + parity) * half
            e2_out[0, at : at + half, :] = ((normed * scale + shift) * ok).astype(BF16)
            if 1 <= rr <= rows_here:
                own = at - cols
                after_out[0, own : own + half, :] = after
                branch_out[0, own : own + half, :] = branch
    e2t_out[0] = e2_out[0].astype(F32).T.astype(BF16)


def second(meta, attended, tokens, top, bot, pieces, proj):
    latents, rows_here, cols, _ = tokens.shape
    own = rows_here * cols
    wide = attended.shape[1]
    whole = lambda *shape: pl.BlockSpec(shape, lambda l, m: (l,) + (0,) * (len(shape) - 1))
    return pl.pallas_call(
        second_kernel,
        out_shape=(
            jax.ShapeDtypeStruct((latents, own + 2 * cols, D), BF16),
            jax.ShapeDtypeStruct((latents, D, own + 2 * cols), BF16),
            jax.ShapeDtypeStruct((latents, own, D), F32),
            jax.ShapeDtypeStruct((latents, own, D), F32),
        ),
        grid_spec=pltpu.PrefetchScalarGridSpec(
            num_scalar_prefetch=1,
            grid=(latents,),
            in_specs=[
                whole(4, wide, D),
                whole(1, rows_here, cols, D),
                whole(1, 1, cols, D),
                whole(1, 1, cols, D),
                whole(1, 6, D),
                pl.BlockSpec((D, D), lambda l, m: (0, 0)),
            ],
            out_specs=(
                whole(1, own + 2 * cols, D),
                whole(1, D, own + 2 * cols),
                whole(1, own, D),
                whole(1, own, D),
            ),
            scratch_shapes=[
                pltpu.VMEM((rows_here + 2, LANE_PARTS, cols, 128), F32),
                pltpu.VMEM((4, wide, D), F32),
            ],
        ),
        compiler_params=pltpu.CompilerParams(vmem_limit_bytes=VMEM_LIMIT),
        cost_estimate=pl.CostEstimate(flops=7_000_000_000, bytes_accessed=4_000_000, transcendentals=0),
        name="second",
    )(meta, attended, tokens, top, bot, pieces, proj)


def normal_parts(values):
    density = jnp.exp2(values * values * -0.7213475204444817 - 1.3257480647361592)
    t = 1.0 / (1.0 + 0.2316419 * jnp.abs(values))
    series = t * (
        0.319381530
        + t * (-0.356563782 + t * (1.781477937 + t * (-1.821255978 + t * 1.330274429)))
    )
    tail = density * series
    return jnp.where(values > 0.0, 1.0 - tail, tail), density


def ffn_kernel(core, e2, e2t, ge, get, up, down, kern_in, exp_out, ge2_out, first_out, last_out, send_out, keep_out, kern_out, *scratch):
    latents = e2.shape[0]
    lifted, gact, gconv, act, graised = [scratch[k * latents : (k + 1) * latents] for k in range(5)]
    down_acc, up_acc = scratch[5 * latents :]
    step = pl.program_id(0)
    half = lifted[0].shape[2]
    rows_here = gconv[0].shape[0]
    block = lifted[0].shape[3]
    chunks = block // 128
    lanes = [slice(c * 128, (c + 1) * 128) for c in range(chunks)]
    taps = [[kern_in[t : t + 1, cut].astype(F32) for t in range(9)] for cut in lanes]
    sums = [[jnp.zeros((8, 128), F32) for _ in range(9)] for _ in range(chunks)]
    lift_rows = 3

    def put(ref, row, parity, cut, values):
        ref[row, 1 + parity, :, cut] = values
        if parity == 0:
            ref[row, 3, :, cut] = shift_up(values)
        else:
            ref[row, 0, :, cut] = shift_down(values)

    def lift(latent, part):
        size = lift_rows * 2 * half
        raised = mm(e2[latent, part * size : (part + 1) * size], up[...])
        for k in range(lift_rows):
            for parity in range(2):
                at = (2 * k + parity) * half
                for cut in lanes:
                    put(lifted[latent], part * lift_rows + k, parity, cut, raised[at : at + half, cut])

    def pull(latent):
        gact[latent][...] = mm(ge[latent], down[...], NT)

    def bend(latent, row, c):
        cut = lanes[c]
        for parity in range(2):
            total = None
            for i in range(3):
                for j in range(3):
                    term = lifted[latent][row + i, parity + j, :, cut] * taps[c][3 * i + j]
                    total = term if total is None else total + term
            cdf, density = normal_parts(total)
            at = (2 * row + parity) * half
            act[latent][at : at + half, cut] = (total * cdf).astype(BF16)
            grad = gact[latent][at : at + half, cut] * (cdf + total * density)
            put(gconv[latent], row, parity, cut, grad)

    def unbend(latent, rr, c):
        cut = lanes[c]
        for parity in range(2):
            total = None
            for i in range(3):
                row = rr - i
                if not 0 <= row < rows_here:
                    continue
                for j in range(3):
                    term = gconv[latent][row, parity + 2 - j, :, cut] * taps[c][3 * i + j]
                    total = term if total is None else total + term
            at = (2 * rr + parity) * half
            graised[latent][at : at + half, cut] = total.astype(BF16)
            if rr < rows_here:
                here = gconv[latent][rr, 1 + parity, :, cut]
                for i in range(3):
                    for j in range(3):
                        t = 3 * i + j
                        part = lifted[latent][rr + i, parity + j, :, cut] * here
                        sums[c][t] = sums[c][t] + sum8(part)

    def expand(latent):
        exp_out[latent] += mm(act[latent][...], down[...])

    def lower(latent):
        ge2_out[latent] += mm(graised[latent][...], up[...], NT)

    def weigh_down(latent):
        value = mm(get[latent], act[latent][...])
        down_acc[...] = value if latent == 0 else down_acc[...] + value

    def weigh_up(latent):
        value = mm(e2t[latent], graised[latent][...])
        up_acc[...] = value if latent == 0 else up_acc[...] + value

    @pl.when(step == 0)
    def _():
        exp_out[...] = jnp.zeros_like(exp_out)
        ge2_out[...] = jnp.zeros_like(ge2_out)

    def mix(work, more):
        stride = max(1, len(work) // max(1, len(more)))
        for k, unit in enumerate(work):
            if k % stride == 0 and k // stride < len(more):
                more[k // stride]()
            unit()
        for unit in more[-(-len(work) // stride) :]:
            unit()

    part = functools.partial
    lifts = (rows_here + 2) // lift_rows
    for k in range(lifts):
        lift(0, k)
    pull(0)
    for latent in range(latents):
        bends = [part(bend, latent, row, c) for c in range(chunks) for row in range(rows_here)]
        unbends = [part(unbend, latent, rr, c) for c in range(chunks) for rr in range(rows_here + 2)]
        first, then = [], [part(expand, latent), part(weigh_down, latent)]
        if latent > 0:
            first += [part(lower, latent - 1), part(weigh_up, latent - 1)]
        if latent + 1 < latents:
            first += [part(lift, latent + 1, k) for k in range(lifts)] + [part(pull, latent + 1)]
        mix(bends, first)
        mix(unbends, then)
    lower(latents - 1)
    weigh_up(latents - 1)

    @pl.when(step == pl.num_programs(0) - 1)
    def _():
        first_out[...] = ge2_out[:, : 2 * half].astype(BF16)
        last_out[...] = ge2_out[:, 2 * half * (rows_here + 1) :].astype(BF16)

    size = down_acc.shape[0] // 4
    for which, acc in enumerate((down_acc, up_acc)):
        for y in range(2):
            mine = pl.multiple_of((2 * y + core[0]) * size, 8)
            other = pl.multiple_of((2 * y + 1 - core[0]) * size, 8)
            keep_out[which, y] = acc[pl.ds(mine, size), :].astype(BF16)
            send_out[which, y] = acc[pl.ds(other, size), :].astype(BF16)
    for c, cut in enumerate(lanes):
        for t in range(9):
            kern_out[t : t + 1, cut] = jnp.sum(sums[c][t], axis=0, keepdims=True)


def ffn(core, e2, e2t, ge, get, up, down, kern, cols):
    latents, wide, _ = e2.shape
    half = cols // 2
    own = ge.shape[1]
    rows_here = own // cols
    hidden = up.shape[1]
    fixed = lambda *shape: pl.BlockSpec(shape, lambda f, c: (0,) * len(shape))
    parts = jax.ShapeDtypeStruct((2, 2, D // 4, hidden), BF16)
    parts_spec = pl.BlockSpec((2, 2, D // 4, FF_BLOCK), lambda f, c: (0, 0, 0, f))
    each = lambda *args: [pltpu.VMEM(*args)] * latents
    return pl.pallas_call(
        ffn_kernel,
        out_shape=(
            jax.ShapeDtypeStruct((latents, own, D), F32),
            jax.ShapeDtypeStruct((latents, wide, D), F32),
            jax.ShapeDtypeStruct((latents, cols, D), BF16),
            jax.ShapeDtypeStruct((latents, cols, D), BF16),
            parts,
            parts,
            jax.ShapeDtypeStruct((9, hidden), F32),
        ),
        grid_spec=pltpu.PrefetchScalarGridSpec(
            num_scalar_prefetch=1,
            grid=(hidden // FF_BLOCK,),
            in_specs=[
                fixed(latents, wide, D),
                fixed(latents, D, wide),
                fixed(latents, own, D),
                fixed(latents, D, own),
                pl.BlockSpec((D, FF_BLOCK), lambda f, c: (0, f)),
                pl.BlockSpec((FF_BLOCK, D), lambda f, c: (f, 0)),
                pl.BlockSpec((9, FF_BLOCK), lambda f, c: (0, f)),
            ],
            out_specs=(
                fixed(latents, own, D),
                fixed(latents, wide, D),
                fixed(latents, cols, D),
                fixed(latents, cols, D),
                parts_spec,
                parts_spec,
                pl.BlockSpec((9, FF_BLOCK), lambda f, c: (0, f)),
            ),
            scratch_shapes=each((rows_here + 2, 4, half, FF_BLOCK), F32)
            + each((own, FF_BLOCK), F32)
            + each((rows_here, 4, half, FF_BLOCK), F32)
            + each((own, FF_BLOCK), BF16)
            + each((wide, FF_BLOCK), BF16)
            + [pltpu.VMEM((D, FF_BLOCK), F32), pltpu.VMEM((D, FF_BLOCK), F32)],
        ),
        compiler_params=pltpu.CompilerParams(vmem_limit_bytes=VMEM_LIMIT),
        cost_estimate=pl.CostEstimate(flops=35_000_000_000, bytes_accessed=4_000_000, transcendentals=0),
        name="ffn",
    )(core, e2, e2t, ge, get, up, down, kern)


def output_kernel(exp, after_in, cot_in, pieces, out, sum_out, buf):
    rows_here, cols = out.shape[1], out.shape[2]
    half = cols // 2
    gate = pieces[0, 5:6, :]
    total = jnp.zeros((8, D), F32)
    for row in range(rows_here):
        for parity in range(2):
            part = pl.ds((2 * row + parity) * half, half)
            expanded = exp[0, part, :]
            put_columns(buf, row, parity, after_in[0, part, :] + gate * expanded)
            total = total + sum8(cot_in[0, part, :].astype(F32) * expanded)
        out[0, row] = get_row(buf, row).astype(BF16)
    sum_out[0] = jnp.sum(total, axis=0, keepdims=True)


def finish_output(exp, after, cot, pieces, rows_here, cols):
    latents, own, _ = exp.shape
    whole = lambda *shape: pl.BlockSpec(shape, lambda l: (l,) + (0,) * (len(shape) - 1))
    return pl.pallas_call(
        output_kernel,
        out_shape=(
            jax.ShapeDtypeStruct((latents, rows_here, cols, D), BF16),
            jax.ShapeDtypeStruct((latents, 1, D), F32),
        ),
        grid=(latents,),
        in_specs=[whole(1, own, D), whole(1, own, D), whole(1, own, D), whole(1, 6, D)],
        out_specs=(whole(1, rows_here, cols, D), whole(1, 1, D)),
        scratch_shapes=[pltpu.VMEM((rows_here, LANE_PARTS, cols, 128), F32)],
        compiler_params=pltpu.CompilerParams(vmem_limit_bytes=VMEM_LIMIT),
        cost_estimate=pl.CostEstimate(flops=5_000_000_000, bytes_accessed=4_000_000, transcendentals=0),
        name="finish_output",
    )(exp, after, cot, pieces)


def middle_kernel(meta, ge2, low, high, after_in, branch_in, cot_in, pieces, proj, after_grad, gb_out, gatt_out, sums_out):
    latents = pl.num_programs(0)
    latent = pl.program_id(0)
    own = after_in.shape[1]
    cols = low.shape[1]
    rows_here = own // cols
    half = cols // 2
    row0 = meta[2 * latents]
    gate_one = pieces[0, 2:3, :]
    scale = 1.0 + pieces[0, 4:5, :]
    sums = [jnp.zeros((8, D), F32) for _ in range(3)]
    for row in range(rows_here):
        for parity in range(2):
            at = (2 * row + parity) * half
            part = pl.ds(at, half)
            side = pl.ds(parity * half, half)
            after = after_in[0, part, :]
            cot = cot_in[0, part, :].astype(F32)
            normed, scaled = normalize(after)
            ok = usable_of(meta, latents, latent, row0 + row, parity, half)
            grad = ge2[0, pl.ds(at + cols, half), :]
            if row == 0:
                grad = grad + low[0, side, :].astype(F32)
            if row == rows_here - 1:
                grad = grad + high[0, side, :].astype(F32)
            grad = grad * ok
            grad_after = cot + norm_back(grad * scale, normed, scaled)
            after_grad[0, part, :] = grad_after
            sums[0] = sums[0] + sum8(grad_after * branch_in[0, part, :])
            sums[1] = sums[1] + sum8(grad)
            sums[2] = sums[2] + sum8(grad * normed)
            group = 2 * (row % 2) + parity
            to = pl.ds((row // 2) * half, half)
            gb_out[0, group, to, :] = (gate_one * grad_after).astype(BF16)
    for k in range(3):
        sums_out[0, k : k + 1, :] = jnp.sum(sums[k], axis=0, keepdims=True)
    for group in range(4):
        gatt_out[0, group] = mm(gb_out[0, group], proj[...], NT).astype(BF16)


def middle(meta, ge2, low, high, after, branch, cot, pieces, proj):
    latents, own, _ = after.shape
    wide, cols = ge2.shape[1], low.shape[1]
    per_group = own // 4
    whole = lambda *shape: pl.BlockSpec(shape, lambda l, m: (l,) + (0,) * (len(shape) - 1))
    return pl.pallas_call(
        middle_kernel,
        out_shape=(
            jax.ShapeDtypeStruct((latents, own, D), F32),
            jax.ShapeDtypeStruct((latents, 4, per_group, D), BF16),
            jax.ShapeDtypeStruct((latents, 4, per_group, D), BF16),
            jax.ShapeDtypeStruct((latents, 3, D), F32),
        ),
        grid_spec=pltpu.PrefetchScalarGridSpec(
            num_scalar_prefetch=1,
            grid=(latents,),
            in_specs=[
                whole(1, wide, D),
                whole(1, cols, D),
                whole(1, cols, D),
                whole(1, own, D),
                whole(1, own, D),
                whole(1, own, D),
                whole(1, 6, D),
                pl.BlockSpec((D, D), lambda l, m: (0, 0)),
            ],
            out_specs=(
                whole(1, own, D),
                whole(1, 4, per_group, D),
                whole(1, 4, per_group, D),
                whole(1, 3, D),
            ),
        ),
        compiler_params=pltpu.CompilerParams(vmem_limit_bytes=VMEM_LIMIT),
        cost_estimate=pl.CostEstimate(flops=8_000_000_000, bytes_accessed=4_000_000, transcendentals=0),
        name="middle",
    )(meta, ge2, low, high, after, branch, cot, pieces, proj)


def leave_kernel(meta, gm, tok, top, bot, after_grad, pieces, kern, out, kern_out, sums_out, buf, ent, gmx, obuf, nbuf, sbuf, tot):
    latents = pl.num_programs(0)
    latent = pl.program_id(0)
    rows_here, cols = tok.shape[1], tok.shape[2]
    half = cols // 2
    row0 = meta[2 * latents]
    shift = pieces[0, 0:1, :]
    scale = 1.0 + pieces[0, 1:2, :]
    taps = [kern[t : t + 1, :].astype(F32) for t in range(9)]
    put_row(buf, 0, top[0, 0].astype(F32))
    for row in range(rows_here):
        put_row(buf, row + 1, tok[0, row].astype(F32))
    put_row(buf, rows_here + 1, bot[0, 0].astype(F32))

    def take(rr, carry):
        at = pl.multiple_of(rr // 2 * half, half)
        for parity in range(2):
            normed, scaled = normalize(get_columns(buf, rr, parity))
            nbuf[rr, parity] = normed
            sbuf[rr, parity] = jnp.broadcast_to(scaled, (half, 128))
            ok = usable_of(meta, latents, latent, row0 + rr - 1, parity, half)
            put_shifts(ent, rr, parity, (normed * scale + shift) * ok)
            group = 2 * ((rr + 1) % 2) + parity
            put_shifts(gmx, rr, parity, gm[group, pl.ds(at, half), :].astype(F32))
        return carry

    lax.fori_loop(0, rows_here + 2, take, 0)
    tot[...] = jnp.zeros_like(tot)

    def give(row, carry):
        for parity in range(2):
            here = gmx[row + 1, 1 + parity]
            total = here
            for i in range(3):
                for j in range(3):
                    t = 3 * i + j
                    total = total + gmx[row + 2 - i, parity + 2 - j] * taps[t]
                    tot[t] += sum8(ent[row + i, parity + j] * here)
            ok = usable_of(meta, latents, latent, row0 + row, parity, half)
            grad = total * ok
            normed, scaled = nbuf[row + 1, parity], sbuf[row + 1, parity, :, 0:1]
            tot[9] += sum8(grad)
            tot[10] += sum8(grad * normed)
            at = pl.multiple_of((2 * row + parity) * half, half)
            back = after_grad[0, pl.ds(at, half), :] + norm_back(grad * scale, normed, scaled)
            put_columns(obuf, row, parity, back)
        out[0, row] = get_row(obuf, row)
        return carry

    lax.fori_loop(0, rows_here, give, 0)
    for t in range(9):
        kern_out[0, t : t + 1, :] = jnp.sum(tot[t], axis=0, keepdims=True)
    for k in range(2):
        sums_out[0, k : k + 1, :] = jnp.sum(tot[9 + k], axis=0, keepdims=True)


def leave(meta, gm, tokens, top, bot, after_grad, pieces, kern):
    latents, rows_here, cols, _ = tokens.shape
    half = cols // 2
    own = rows_here * cols
    wide = gm.shape[1]
    whole = lambda *shape: pl.BlockSpec(shape, lambda l, m: (l,) + (0,) * (len(shape) - 1))
    return pl.pallas_call(
        leave_kernel,
        out_shape=(
            jax.ShapeDtypeStruct((latents, rows_here, cols, D), F32),
            jax.ShapeDtypeStruct((latents, 9, D), F32),
            jax.ShapeDtypeStruct((latents, 2, D), F32),
        ),
        grid_spec=pltpu.PrefetchScalarGridSpec(
            num_scalar_prefetch=1,
            grid=(latents,),
            in_specs=[
                whole(4, wide, D),
                whole(1, rows_here, cols, D),
                whole(1, 1, cols, D),
                whole(1, 1, cols, D),
                whole(1, own, D),
                whole(1, 6, D),
                pl.BlockSpec((9, D), lambda l, m: (0, 0)),
            ],
            out_specs=(whole(1, rows_here, cols, D), whole(1, 9, D), whole(1, 2, D)),
            scratch_shapes=[
                pltpu.VMEM((rows_here + 2, LANE_PARTS, cols, 128), F32),
                pltpu.VMEM((rows_here + 2, 4, half, D), F32),
                pltpu.VMEM((rows_here + 2, 4, half, D), F32),
                pltpu.VMEM((rows_here, LANE_PARTS, cols, 128), F32),
                pltpu.VMEM((rows_here + 2, 2, half, D), F32),
                pltpu.VMEM((rows_here + 2, 2, half, 128), F32),
                pltpu.VMEM((11, 8, D), F32),
            ],
        ),
        compiler_params=pltpu.CompilerParams(vmem_limit_bytes=VMEM_LIMIT),
        cost_estimate=pl.CostEstimate(flops=10_000_000_000, bytes_accessed=4_000_000, transcendentals=0),
        name="leave",
    )(meta, gm, tokens, top, bot, after_grad, pieces, kern)


def pair_parts(values):
    lanes = lax.broadcasted_iota(jnp.int32, values.shape, 1)
    first = lanes < HEAD_DIM
    zero = jnp.zeros_like(values)
    return jnp.where(first, values, zero), jnp.where(first, zero, values)


def attend_kernel(offset, mixed, wq, wk, wvt, bias, out, lse_out, padded):
    tokens = mixed.shape[0]
    strips, window, _ = out.shape
    step = tokens // strips
    margin = window - step
    m = mixed[...]
    query = (mm(m, wq[...]).astype(BF16) * FACTOR).astype(BF16)
    key = mm(m, wk[...]).astype(BF16)
    value_t = mm(wvt[...], m, NT).astype(BF16)
    keep = jnp.tile(bias[...], (1, tokens // 128))

    def score(h):
        cut = slice(h // 2 * PAIR, (h // 2 + 1) * PAIR)
        return mm(pair_parts(key[:, cut])[h % 2], query[:, cut], NT)

    scores = {0: score(0), 1: score(1)}
    parts = []
    for h in range(4):
        masked = scores.pop(h) + keep
        peak = jnp.max(masked, axis=0, keepdims=True)
        raw = jnp.exp(masked - peak)
        if h + 2 < 4:
            scores[h + 2] = score(h + 2)
        total = jnp.sum(raw, axis=0, keepdims=True)
        prob = (raw * (1.0 / total)).astype(BF16)
        parts.append(mm(value_t[h * HEAD_DIM : (h + 1) * HEAD_DIM], prob))
        lse_out[0, h : h + 1, :] = peak + jnp.log(total)
    padded[0:margin] = jnp.zeros((margin, QUAD), F32)
    padded[margin + tokens :] = jnp.zeros((margin, QUAD), F32)
    padded[margin : margin + tokens] = jnp.concatenate(parts, axis=0).T
    for s in range(strips):
        start = pl.multiple_of(offset[0] + s * step, 8)
        out[s] = padded[pl.ds(start, window), :].astype(BF16)


def attend(offset, mixed, weight, weight_t, bias, strips, window):
    tokens = mixed.shape[0]
    margin = window - tokens // strips
    return pl.pallas_call(
        attend_kernel,
        out_shape=(
            jax.ShapeDtypeStruct((strips, window, D), BF16),
            jax.ShapeDtypeStruct((QUADS, 4, tokens), F32),
        ),
        grid_spec=pltpu.PrefetchScalarGridSpec(
            num_scalar_prefetch=1,
            grid=(QUADS,),
            in_specs=[
                pl.BlockSpec((tokens, D), lambda p, o: (0, 0)),
                pl.BlockSpec((D, QUAD), lambda p, o: (0, p)),
                pl.BlockSpec((D, QUAD), lambda p, o: (0, QUADS + p)),
                pl.BlockSpec((QUAD, D), lambda p, o: (2 * QUADS + p, 0)),
                pl.BlockSpec((tokens, 128), lambda p, o: (0, 0)),
            ],
            out_specs=(
                pl.BlockSpec((strips, window, QUAD), lambda p, o: (0, 0, p)),
                pl.BlockSpec((1, 4, tokens), lambda p, o: (p, 0, 0)),
            ),
            scratch_shapes=[pltpu.VMEM((tokens + 2 * margin, QUAD), F32)],
        ),
        compiler_params=pltpu.CompilerParams(vmem_limit_bytes=VMEM_LIMIT),
        cost_estimate=pl.CostEstimate(flops=16_000_000_000, bytes_accessed=4_000_000, transcendentals=0),
        name="attend",
    )(offset, mixed, weight, weight, weight_t, bias)


def attend_back_kernel(offset, query, key, value, key_t, bias, lse, gatt, wq, wk, wv, mixed_t, send_out, keep_out, gm_out, acc, part):
    tokens = query.shape[0]
    strips, window, _ = gm_out.shape
    step = tokens // strips
    margin = window - step
    p = pl.program_id(0)
    keep = jnp.tile(bias[...], (1, tokens // 128))

    def pair(k):
        cut = slice(k * PAIR, (k + 1) * PAIR)
        q, grad = query[:, cut], gatt[:, cut]
        keys, values = pair_parts(key[:, cut]), pair_parts(value[:, cut])
        return [(mm(keys[e], q, NT), mm(values[e], grad, NT)) for e in range(2)]

    def soften(k, e, score, grad_prob):
        h = 2 * k + e
        prob = jnp.exp(score * FACTOR + keep - lse[0, h : h + 1, :])
        delta = jnp.sum(prob * grad_prob, axis=0, keepdims=True)
        return prob.astype(BF16), (prob * (grad_prob - delta)).astype(BF16)

    def finish(k, probs, grad_scores):
        cut = slice(k * PAIR, (k + 1) * PAIR)
        queries, grads = pair_parts(query[:, cut]), pair_parts(gatt[:, cut])
        dv = mm(jnp.concatenate(probs, axis=1), jnp.concatenate(grads, axis=0))
        dk = mm(jnp.concatenate(grad_scores, axis=1), jnp.concatenate(queries, axis=0)) * FACTOR
        rows = [key_t[(2 * k + e) * HEAD_DIM : (2 * k + e + 1) * HEAD_DIM] for e in range(2)]
        parts = [mm(rows[e], grad_scores[e]) for e in range(2)]
        dq = jnp.concatenate(parts, axis=0).T * FACTOR
        return dq.astype(BF16), dk.astype(BF16), dv.astype(BF16)

    first = pair(0)
    soft = [soften(0, e, *first[e]) for e in range(2)]
    then = pair(1)
    one = finish(0, [v[0] for v in soft], [v[1] for v in soft])
    soft = [soften(1, e, *then[e]) for e in range(2)]
    two = finish(1, [v[0] for v in soft], [v[1] for v in soft])
    all_three = jnp.concatenate([v for k in range(3) for v in (one[k], two[k])], axis=1)
    part[...] = mm(mixed_t[...], all_three)
    size = D // 4
    for y in range(2):
        mine = pl.multiple_of((2 * y + offset[1]) * size, 8)
        other = pl.multiple_of((2 * y + 1 - offset[1]) * size, 8)
        for k in range(3):
            cut = slice(k * QUAD, (k + 1) * QUAD)
            keep_out[k, y] = part[pl.ds(mine, size), cut].astype(BF16)
            send_out[k, y] = part[pl.ds(other, size), cut].astype(BF16)
    total = mm(all_three, jnp.concatenate([wq[...], wk[...], wv[...]], axis=1), NT)

    @pl.when(p == 0)
    def _():
        acc[0:margin] = jnp.zeros((margin, D), F32)
        acc[margin + tokens :] = jnp.zeros((margin, D), F32)
        acc[margin : margin + tokens] = total

    @pl.when(p > 0)
    def _():
        acc[margin : margin + tokens] += total

    @pl.when(p == pl.num_programs(0) - 1)
    def _():
        for s in range(strips):
            start = pl.multiple_of(offset[0] + s * step, 8)
            gm_out[s] = acc[pl.ds(start, window), :].astype(BF16)


def attend_back(offset, triple, key_t, bias, lse, gatt, weight, mixed_t, strips, window):
    tokens = triple.shape[0]
    margin = window - tokens // strips
    part = lambda k: pl.BlockSpec((tokens, QUAD), lambda p, o: (0, k * QUADS + p))
    slab = lambda k: pl.BlockSpec((D, QUAD), lambda p, o: (0, k * QUADS + p))
    parts = jax.ShapeDtypeStruct((3, 2, D // 4, D), BF16)
    parts_spec = pl.BlockSpec((3, 2, D // 4, QUAD), lambda p, o: (0, 0, 0, p))
    return pl.pallas_call(
        attend_back_kernel,
        out_shape=(
            parts,
            parts,
            jax.ShapeDtypeStruct((strips, window, D), BF16),
        ),
        grid_spec=pltpu.PrefetchScalarGridSpec(
            num_scalar_prefetch=1,
            grid=(QUADS,),
            in_specs=[
                part(0),
                part(1),
                part(2),
                pl.BlockSpec((QUAD, tokens), lambda p, o: (p, 0)),
                pl.BlockSpec((tokens, 128), lambda p, o: (0, 0)),
                pl.BlockSpec((1, 4, tokens), lambda p, o: (p, 0, 0)),
                part(0),
                slab(0),
                slab(1),
                slab(2),
                pl.BlockSpec((D, tokens), lambda p, o: (0, 0)),
            ],
            out_specs=(
                parts_spec,
                parts_spec,
                pl.BlockSpec((strips, window, D), lambda p, o: (0, 0, 0)),
            ),
            scratch_shapes=[
                pltpu.VMEM((tokens + 2 * margin, D), F32),
                pltpu.VMEM((D, 3 * QUAD), F32),
            ],
        ),
        compiler_params=pltpu.CompilerParams(vmem_limit_bytes=VMEM_LIMIT),
        cost_estimate=pl.CostEstimate(flops=23_000_000_000, bytes_accessed=4_000_000, transcendentals=0),
        name="attend_back",
    )(offset, triple, triple, triple, key_t, bias, lse, gatt, weight, weight, weight, mixed_t)


def from_before(values, axis):
    count = lax.axis_size(axis)
    return lax.ppermute(values, axis, [(i, i + 1) for i in range(count - 1)])


def from_after(values, axis):
    count = lax.axis_size(axis)
    return lax.ppermute(values, axis, [(i + 1, i) for i in range(count - 1)])


def swap(values):
    return lax.all_to_all(values, "seq", 0, 0, tiled=False)


BITS = {"y": ("batch", 2), "c": ("batch", 1), "h": ("seq", 4), "l": ("seq", 2), "x": ("seq", 1)}
ORDER = "ychlx"


def blocks_of(values):
    return values.reshape(values.shape[:-2] + (2, 2, 2, 2, 2, values.shape[-2] // 32, values.shape[-1]))


def split(values, dims, bit):
    axis, mask = BITS[bit]
    mine = (lax.axis_index(axis) // mask) % 2
    at = values.ndim - 2 - len(dims) + dims.index(bit)
    send = lax.dynamic_index_in_dim(values, 1 - mine, at, keepdims=False)
    keep = lax.dynamic_index_in_dim(values, mine, at, keepdims=False)
    return send, keep, dims.replace(bit, "")


def hop(values, bit):
    axis, mask = BITS[bit]
    count = lax.axis_size(axis)
    return lax.ppermute(values, axis, [(i, i ^ mask) for i in range(count)])


def add(keep, got):
    return keep.astype(F32) + got.astype(F32)


def after(values, *others):
    return lax.optimization_barrier((values,) + others)[0]


STEPS = ("yxl", "xly", "lyx")


def step_of(parts, dims, step):
    cut = [split(part, left, order[step]) for part, left, order in zip(parts, dims, STEPS)]
    return tuple(c[0] for c in cut), tuple(c[1] for c in cut), [c[2] for c in cut]


def hops_of(sends, step):
    return tuple(hop(send, order[step]) for send, order in zip(sends, STEPS))


def fold_of(keeps, gots):
    return [add(keep, got).astype(BF16) for keep, got in zip(keeps, gots)]


def reduce_rest(values, dims, order):
    for bit in order:
        send, keep, dims = split(values.astype(BF16), dims, bit)
        values = add(keep, hop(send, bit))
    return values


def scatter_rows(values):
    return lax.psum_scatter(values, ("batch", "seq"), scatter_dimension=0, tiled=True).astype(F32)


def payload_of(common, sliced):
    seq_count, batch_count = lax.axis_size("seq"), lax.axis_size("batch")
    flat = common.reshape(1, -1)
    pieces = [jnp.broadcast_to(flat, (seq_count, flat.shape[1]))]
    for values in sliced:
        cut = values.reshape(values.shape[0], batch_count, seq_count, -1).transpose(2, 1, 0, 3)
        pieces.append(cut.reshape(seq_count, -1))
    whole = jnp.concatenate(pieces, axis=1)
    return jnp.pad(whole, ((0, 0), (0, -whole.shape[1] % 1024))).reshape(seq_count, -1, 128)


def unpack(gathered, common, sliced):
    seq_count, batch_count = lax.axis_size("seq"), lax.axis_size("batch")
    gathered = gathered.reshape(batch_count, -1)
    at = common.size
    common_all = gathered[:, :at].reshape((batch_count,) + common.shape)
    own = []
    for values in sliced:
        size = values.size // seq_count
        part = jnp.sum(gathered[:, at : at + size], axis=0)
        part = part.reshape(batch_count, values.shape[0], -1)
        own.append(lax.dynamic_index_in_dim(part, lax.axis_index("batch"), 0, keepdims=False))
        at += size
    return common_all, own


def windows_of(values, offset, margin, strips):
    step = values.shape[0] // strips
    padded = jnp.pad(values, ((margin, margin), (0, 0)))
    base = lax.dynamic_slice_in_dim(padded, offset, values.shape[0] + margin)
    return jnp.stack([base[s * step : s * step + step + margin] for s in range(strips)])


def attend_plain(mixed, weight, ok, heads):
    wide = heads * HEAD_DIM
    triple = mm(mixed, weight).astype(BF16)
    split = lambda k: triple[:, k * wide : (k + 1) * wide].reshape(-1, heads, HEAD_DIM)
    queries, keys, values = split(0), split(1), split(2)
    scores = jnp.einsum("qhe,khe->hqk", queries, keys, preferred_element_type=F32) * FACTOR
    scores = jnp.where(ok[None, None, :], scores, -1e30)
    prob = jax.nn.softmax(scores, axis=-1)
    out = jnp.einsum("hqk,khe->qhe", prob.astype(BF16), values, preferred_element_type=F32)
    return out.reshape(-1, wide).astype(BF16), (queries, keys, values, prob)


def attend_plain_back(saved, grad, weight):
    queries, keys, values, prob = saved
    heads = queries.shape[1]
    grad = grad.reshape(-1, heads, HEAD_DIM)
    grad_prob = jnp.einsum("qhe,khe->hqk", grad, values, preferred_element_type=F32)
    delta = jnp.sum(prob * grad_prob, axis=-1, keepdims=True)
    grad_scores = (prob * (grad_prob - delta)).astype(BF16)
    dq = jnp.einsum("hqk,khe->qhe", grad_scores, keys, preferred_element_type=F32) * FACTOR
    dk = jnp.einsum("hqk,qhe->khe", grad_scores, queries, preferred_element_type=F32) * FACTOR
    dv = jnp.einsum("hqk,qhe->khe", prob.astype(BF16), grad, preferred_element_type=F32)
    flat = lambda v: v.reshape(v.shape[0], -1).astype(BF16)
    grads = jnp.concatenate([flat(dq), flat(dk), flat(dv)], axis=1)
    return grads, mm(grads, weight, NT)


def shards(
    tokens,
    cotangent,
    timestep,
    class_ids,
    heights,
    widths,
    time_weight,
    class_table,
    ada_weight,
    ada_bias,
    conv_attn,
    qkv_weight,
    proj_weight,
    up_weight,
    conv_ffn,
    down_weight,
):
    latents, rows_here, cols, _ = tokens.shape
    half = cols // 2
    seq_count = lax.axis_size("seq")
    seq_place = lax.axis_index("seq")
    batch_count = lax.axis_size("batch")
    batch_place = lax.axis_index("batch")
    devices = batch_count * seq_count
    blocks = latents * 4
    share = seq_count // blocks
    per_group = rows_here // 2 * half
    group_tokens = seq_count * per_group

    first, last = tokens[:, :1], tokens[:, rows_here - 1 :]
    top = from_before(last, "seq")
    bot = from_after(first, "seq")

    half_freq = time_weight.shape[0] // 2
    frequency = jnp.exp(-math.log(10000.0) * jnp.arange(half_freq, dtype=F32) / half_freq)
    angles = timestep.astype(F32)[:, None] * frequency[None, :]
    embedding = jnp.concatenate([jnp.cos(angles), jnp.sin(angles)], axis=1).astype(BF16)
    one_hot = (
        class_ids[:, None] == jnp.arange(class_table.shape[0], dtype=jnp.int32)[None, :]
    ).astype(BF16)
    condition = mm(embedding, time_weight) + mm(one_hot, class_table)
    logistic = jax.nn.sigmoid(condition)
    activated_cond = (condition * logistic).astype(BF16)
    lead = mm(activated_cond, ada_weight[:, : 2 * D]) + ada_bias[: 2 * D]
    meta = jnp.concatenate(
        [heights, widths, jnp.reshape(seq_place * rows_here, (1,))]
    ).astype(jnp.int32)
    core = jnp.reshape(batch_place % 2, (1,)).astype(jnp.int32)

    mixed = enter(meta, tokens, top, bot, lead, conv_attn)
    late_cond = after(activated_cond, mixed)
    pieces = mm(late_cond, ada_weight[:, 2 * D :]) + ada_bias[2 * D :]
    pieces = jnp.concatenate([lead, pieces], axis=1).reshape(latents, 6, D)
    sent = mixed.reshape(blocks, 1, per_group, D)
    sent = jnp.broadcast_to(sent, (blocks, share, per_group, D)).reshape(seq_count, per_group, D)
    grouped = swap(sent).reshape(group_tokens, D)

    weight_t = qkv_weight.T

    my_block = seq_place // share
    my_latent = my_block // 4
    my_a = (my_block // 2) % 2
    my_b = my_block % 2
    places = jnp.arange(group_tokens, dtype=jnp.int32)
    key_row = places // half * 2 + my_a
    key_col = places % half * 2 + my_b
    height = lax.dynamic_index_in_dim(heights, my_latent, 0, keepdims=False)
    width = lax.dynamic_index_in_dim(widths, my_latent, 0, keepdims=False)
    key_ok = (key_row < height) & (key_col < width)

    margin = half
    tall = per_group + margin
    offset = jnp.stack([margin * (1 - my_a), batch_place % 2]).astype(jnp.int32)
    if share == 1:
        bias = jnp.broadcast_to(jnp.where(key_ok, 0.0, -1e30)[:, None], (group_tokens, 128))
        windows, lse = attend(offset, grouped, qkv_weight, weight_t, bias, seq_count, tall)
        attended = swap(windows)
    else:
        heads = HEADS // share
        wide = heads * HEAD_DIM
        chunk = seq_place % share
        thirds = qkv_weight.reshape(D, 3, share, wide)
        my_weight = lax.dynamic_index_in_dim(thirds, chunk, 2, keepdims=False).reshape(D, 3 * wide)
        att, saved = attend_plain(grouped, my_weight, key_ok, heads)
        windows = windows_of(att, offset[0], margin, seq_count)
        attended = swap(windows).reshape(blocks, share, tall, wide)
        attended = attended.transpose(0, 2, 1, 3).reshape(blocks, tall, D)

    ge, get, cot_split = prepare_cot(cotangent, pieces)
    conditions = lax.all_gather(
        jnp.concatenate([condition, embedding.astype(F32), class_ids.astype(F32)[:, None]], axis=1),
        "batch",
        axis=0,
    )
    if share == 1:
        triple = mm(grouped, qkv_weight).astype(BF16)
        key_t = mm(weight_t[D : 2 * D], grouped, NT).astype(BF16)
        grouped_t = grouped.T
        attended, ge, triple, key_t, grouped_t, conditions = lax.optimization_barrier(
            (attended, ge, triple, key_t, grouped_t, conditions)
        )
    e2, e2t, after_attn, branch = second(
        meta, attended, tokens, top, bot, pieces, proj_weight
    )
    expanded, grad_e2, edge_first, edge_last, send_c, keep_c, conv_ffn_part = ffn(
        core, e2, e2t, ge, get, up_weight, down_weight, conv_ffn, cols
    )
    halving = batch_count == 4 and seq_count == 8
    if halving:
        got_c = hop(send_c, "c")
    low = from_before(edge_last, "seq")
    high = from_after(edge_first, "seq")
    output, gate_sums = finish_output(expanded, after_attn, cot_split, pieces, rows_here, cols)
    grad_after, grad_branch, grad_attended, mid_sums = middle(
        meta, grad_e2, low, high, after_attn, branch, cot_split, pieces, proj_weight
    )

    att_all = after(attended, grad_attended)
    starts = [margin * ((k // 2) % 2) for k in range(blocks)]
    att_own = jnp.concatenate([att_all[k, at : at + per_group] for k, at in enumerate(starts)])
    flat_branch = grad_branch.reshape(blocks * per_group, D)
    hidden = conv_ffn.shape[1]
    if share == 1:
        gatt = swap(grad_attended.reshape(seq_count, per_group, D)).reshape(group_tokens, D)
        if halving:
            keep_c = after(keep_c, grad_attended)
            sums = add(keep_c, got_c).astype(BF16).reshape(2, 2, 2, 2, 2, D // devices, hidden)
            third = hidden // 3
            cuts = [sums[..., k * third : (k + 1) * third] for k in range(3)]
            sends, keeps, dims = step_of(cuts, ["yhlx"] * 3, 0)
            late_branch = after(flat_branch, got_c)
            proj_grad = mm(att_own, late_branch, (((0,), (0,)), ((), ()))).astype(BF16)
            send_p, keep_p, _ = split(blocks_of(proj_grad), ORDER, "c")
            got_p = hop(send_p, "c")
            gatt, sends, send_p, gate_sums = lax.optimization_barrier((gatt, sends, send_p, gate_sums))
            gots = hops_of(sends, 0)
        send_r, keep_r, gm_windows = attend_back(
            offset, triple, key_t, bias, lse, gatt, qkv_weight, grouped_t, seq_count, tall
        )
        gm = swap(gm_windows)
        if halving:
            gm_windows, gots = lax.optimization_barrier((gm_windows, gots))
        gm = swap(gm_windows)
    else:
        sent = grad_attended.reshape(blocks, per_group, share, wide).transpose(0, 2, 1, 3)
        gatt = swap(sent.reshape(seq_count, per_group, wide)).reshape(group_tokens, wide)
        grad_triple, gm_part = attend_plain_back(saved, gatt, my_weight)
        gm_windows = windows_of(gm_part.astype(BF16), offset[0], margin, seq_count)
        gm = swap(gm_windows).reshape(blocks, share, tall, D)
        gm = jnp.sum(gm.astype(F32), axis=1).astype(BF16)
        own_grad = mm(grouped, grad_triple, (((0,), (0,)), ((), ()))).astype(BF16)
        spread = jnp.zeros((D, 3, share, wide), BF16)
        qkv_grad = lax.dynamic_update_index_in_dim(
            spread, own_grad.reshape(D, 3, wide), chunk, 2
        ).reshape(D, 3 * D)
        proj_grad = mm(att_own, flat_branch, (((0,), (0,)), ((), ()))).astype(BF16)
        rest = jnp.concatenate([qkv_grad, proj_grad], axis=1)

    if halving:
        got_r = hop(send_r, "c")
        keeps = lax.optimization_barrier((keeps, keep_r))[0]
        sends, keeps, dims = step_of(fold_of(keeps, gots), dims, 1)
        sums = add(keep_r, got_r).astype(BF16).reshape(3, 2, 2, 2, 2, D // devices, D)
        sums_p = add(keep_p, got_p).astype(BF16)
        send_one, keep_one, dims_one = split(sums[:2], "yhlx", "y")
        send_two, keep_two, dims_two = split(jnp.stack([sums[2], sums_p]), "yhlx", "x")
        gm = after(gm, *sends)
        gots = hops_of(sends, 1)
        got_one, got_two = hop(send_one, "y"), hop(send_two, "x")
    total = batch_count * latents

    here = batch_place * seq_count + seq_place
    own_cols = D // devices
    conditions = conditions.reshape(total, -1)
    condition_all = conditions[:, :D]
    embedding_all = conditions[:, D : D + embedding.shape[1]]
    ids_all = conditions[:, -1].astype(jnp.int32)
    logistic_all = jax.nn.sigmoid(condition_all)
    activated_all = (condition_all * logistic_all).astype(BF16).astype(F32)
    slope_all = logistic_all * (1.0 + condition_all * (1.0 - logistic_all))

    def back_through(grads):
        high = lax.reduce_precision(grads, 8, 7)
        middle_term = lax.reduce_precision(grads - high, 8, 7)
        low = grads - high - middle_term
        product = mm(jnp.concatenate([high, middle_term, low]).astype(BF16), ada_weight, NT)
        return product[:total] + product[total : 2 * total] + product[2 * total :]

    token_grad, conv_attn_part, end_sums = leave(
        meta, gm, tokens, top, bot, grad_after, pieces, conv_attn
    )

    common = jnp.concatenate([end_sums, mid_sums, gate_sums], axis=1)
    sliced = (jnp.sum(conv_attn_part, axis=0), conv_ffn_part)
    message = payload_of(common, sliced)
    if halving:
        message, keeps, gots, keep_one, keep_two = lax.optimization_barrier(
            (message, keeps, gots, keep_one, keep_two)
        )
        sends, keeps, dims = step_of(fold_of(keeps, gots), dims, 2)
        gots = hops_of(sends, 2)
        pair = jnp.concatenate(fold_of(keeps, gots), axis=-1)
        send_h, keep_h, _ = split(pair, dims[0], "h")
        got_h = hop(send_h, "h")
        send_one, keep_one, dims_one = split(add(keep_one, got_one).astype(BF16), dims_one, "x")
        send_two, keep_two, dims_two = split(add(keep_two, got_two).astype(BF16), dims_two, "y")
        got_one, got_two = hop(send_one, "x"), hop(send_two, "y")
    gathered = lax.all_gather(jnp.sum(swap(message), axis=0), "batch", axis=0)
    if halving:
        gathered, keep_one, keep_two, keep_h = lax.optimization_barrier(
            (gathered, keep_one, keep_two, keep_h)
        )
        pair = add(keep_h, got_h)
        down_rows, up_rows = pair[0], pair[1]
        rest_rows = jnp.concatenate([add(keep_one, got_one), add(keep_two, got_two)])
        send_l, keep_l, dims_l = split(rest_rows.astype(BF16), dims_one, "l")
        got_l = hop(send_l, "l")
    else:
        whole = jnp.stack([keep_c, send_c])
        whole = jnp.where(core[0] == 0, whole, whole[::-1]).transpose(1, 2, 0, 3, 4)
        whole = whole.reshape(2, D, hidden)
        down_rows, up_rows = scatter_rows(whole[0]), scatter_rows(whole[1])
        if share == 1:
            rest = jnp.stack([keep_r, send_r])
            rest = jnp.where(core[0] == 0, rest, rest[::-1]).transpose(2, 0, 3, 1, 4).reshape(D, -1)
            proj_grad = mm(att_own, flat_branch, (((0,), (0,)), ((), ()))).astype(BF16)
            rest = jnp.concatenate([rest, proj_grad], axis=1)
        rest_rows = scatter_rows(rest).reshape(own_cols, 4, D).transpose(1, 0, 2)
    all_sums, (conv_attn_grad, conv_ffn_grad) = unpack(gathered, common, sliced)

    grad_pieces = all_sums.reshape(total, 6 * D)
    if halving:
        grad_pieces, got_l = lax.optimization_barrier((grad_pieces, got_l))
    grad_silu = back_through(grad_pieces)
    if halving:
        rest_rows = reduce_rest(add(keep_l, got_l), dims_l, "h")
    qkv_rows = jnp.concatenate([rest_rows[0], rest_rows[1], rest_rows[2]], axis=1)
    proj_rows = rest_rows[3]
    cond_all = grad_silu * slope_all
    cond_grad = lax.dynamic_slice_in_dim(cond_all, batch_place * latents, latents)
    cond_cols = lax.dynamic_slice_in_dim(cond_all, here * own_cols, own_cols, axis=1)
    act_cols = lax.dynamic_slice_in_dim(activated_all, here * own_cols, own_cols, axis=1)
    outer = lambda left, right: lax.dot_general(
        left, right, (((0,), (0,)), ((), ())), precision=HIGHEST, preferred_element_type=F32
    )
    hot_all = (ids_all[:, None] == jnp.arange(class_table.shape[0], dtype=jnp.int32)[None, :]).astype(F32)
    bias_cols = 6 * D // devices
    bias_grad = jnp.sum(
        lax.dynamic_slice_in_dim(grad_pieces, here * bias_cols, bias_cols, axis=1), axis=0
    )
    return (
        output,
        token_grad,
        cond_grad,
        outer(embedding_all, cond_cols),
        outer(hot_all, cond_cols),
        outer(act_cols, grad_pieces),
        bias_grad,
        conv_attn_grad,
        qkv_rows,
        proj_rows,
        up_rows,
        conv_ffn_grad,
        down_rows.T,
    )


def solution(mesh):
    strips = P("batch", "seq", None, None)
    in_specs = (strips, strips) + (P("batch"),) * 4 + (P(),) * 10
    both = ("batch", "seq")
    out_specs = (
        strips,
        strips,
        P("batch", None),
        P(None, both),
        P(None, both),
        P(both, None),
        P(both),
        P(None, both),
        P(both, None),
        P(both, None),
        P(both, None),
        P(None, both),
        P(None, both),
    )
    return jax.shard_map(shards, mesh=mesh, in_specs=in_specs, out_specs=out_specs, check_vma=False)
```
